32 devices in a mesh: wide: 8 (over y, x, core), narrow: 4 (over z).
Axes of the slice: x: 2, y: 2, z: 4, core: 2. Of those that a mesh axis runs over, the one named last changes fastest.
Arguments:
- latents: bfloat16 [2, 32, 16, 16, 768], P(None, ('wide', 'narrow')), may hold values from -6 to 6
- buckets: int32 [2, 32], P(None, ('wide', 'narrow')), may hold values from 0 to 2
- step_ids: int32 [2, 32], P(None, ('wide', 'narrow')), may hold values from 0 to 999
- qkv_spatial: bfloat16 [1769472], P(('wide', 'narrow')), may hold values from -0.21875 to 0.21875
- proj_spatial: bfloat16 [589824], P(('wide', 'narrow')), may hold values from -0.625 to 0.625
- qkv_temporal: bfloat16 [1769472], P(('wide', 'narrow')), may hold values from -0.21875 to 0.21875
- proj_temporal: bfloat16 [589824], P(('wide', 'narrow')), may hold values from -0.4375 to 0.4375
- up_weight: bfloat16 [2359296], P(('wide', 'narrow')), may hold values from -0.21875 to 0.21875
- down_weight: bfloat16 [2359296], P(('wide', 'narrow')), may hold values from -0.109375 to 0.109375
- ada_weight: bfloat16 [5308416], P(('wide', 'narrow')), may hold values from -0.21875 to 0.21875
- biases: bfloat16 [10752], P(('wide', 'narrow')), may hold values from -3 to 3
- cotangent: bfloat16 [2, 32, 16, 16, 768], P(None, ('wide', 'narrow')), may hold values from -6 to 6
Outputs:
- output: bfloat16 [2, 32, 16, 16, 768], P(None, ('wide', 'narrow'))
- latents_grad: float32 [2, 32, 16, 16, 768], P(None, ('wide', 'narrow'))
- qkv_spatial_grad: float32 [1769472], P(('wide', 'narrow'))
- proj_spatial_grad: float32 [589824], P(('wide', 'narrow'))
- qkv_temporal_grad: float32 [1769472], P(('wide', 'narrow'))
- proj_temporal_grad: float32 [589824], P(('wide', 'narrow'))
- up_weight_grad: float32 [2359296], P(('wide', 'narrow'))
- down_weight_grad: float32 [2359296], P(('wide', 'narrow'))
- ada_weight_grad: float32 [5308416], P(('wide', 'narrow'))
- biases_grad: float32 [10752], P(('wide', 'narrow'))
The draws below stay inside these ranges and needn't reach their ends.
Inputs may be any that keep to these rules, and one draw needn't show every extreme that they name: `buckets`: an item's bucket sets how many leading spatial positions of each of its frames hold data: 16, 8 or 2 for 0, 1 or 2.
All inputs are finite; a program needn't handle non-finite values.
Results may differ from the reference program's by a relative error of at most 0.02.
Values may be sent and summed in bfloat16 or wider, within the bound.
A program may use at most 320 MiB of HBM per device.

```python
import math
import jax
import jax.numpy as jnp
from jax import lax

D = 768
HEADS = 12
HD = 64
FF = 3072
FRAMES = 16
SPAT = 16
MICRO = 2
ITEMS = 32


def plant(array, own_key, low, largest):
    index_at = [jax.random.randint(jax.random.fold_in(own_key, axis), (), 0, length) for axis, length in enumerate(array.shape)]
    widest = array.shape.index(max(array.shape))
    next_to = index_at[:widest] + [(index_at[widest] + 1) % array.shape[widest]] + index_at[widest + 1:]
    return array.at[tuple(index_at)].set(low).at[tuple(next_to)].set(largest)


def steps_of(key, extent, split, low, largest):
    loudness = 1.0
    for dim, blocks in split:
        heights = jax.random.uniform(jax.random.fold_in(jax.random.fold_in(key, 6), dim), (blocks,), jnp.float32, low / len(split), largest / len(split))
        loudness = loudness * jnp.repeat(jnp.exp(heights), extent[dim] // blocks).reshape((-1,) + (1,) * (len(extent) - 1 - dim))
    return loudness


def normal_values(own_key, extent, width, most, shards=(), kind=jnp.bfloat16):
    level = steps_of(own_key, extent, shards, -0.22, 0.18) if shards else 1.0
    values = jax.random.normal(own_key, extent, jnp.float32) * width * level
    return jnp.minimum(jnp.maximum(values, -most), most).astype(kind)


def setup_inputs(seed: int = 0) -> dict:
    streams_of = jax.random.split(jax.random.key(seed), 13)
    return {
        "latents": normal_values(streams_of[0], (MICRO, ITEMS, FRAMES, SPAT, D), 1.0, 6.0, ((1, 32),)),
        "buckets": plant(jax.random.randint(streams_of[1], (MICRO, ITEMS), 0, 3), jax.random.fold_in(streams_of[1], 1), 0, 2).astype(jnp.int32),
        "step_ids": plant(jax.random.randint(streams_of[2], (MICRO, ITEMS), 0, 1000), jax.random.fold_in(streams_of[2], 1), 0, 999).astype(jnp.int32),
        "qkv_spatial": normal_values(streams_of[3], (3 * D * D,), D ** -0.5, 0.21875, ((0, 32),)),
        "proj_spatial": normal_values(streams_of[4], (D * D,), (D // 8) ** -0.5, 0.625, ((0, 32),)),
        "qkv_temporal": normal_values(streams_of[5], (3 * D * D,), D ** -0.5, 0.21875, ((0, 32),)),
        "proj_temporal": normal_values(streams_of[6], (D * D,), (D // 4) ** -0.5, 0.4375, ((0, 32),)),
        "up_weight": normal_values(streams_of[7], (D * FF,), D ** -0.5, 0.21875, ((0, 32),)),
        "down_weight": normal_values(streams_of[8], (FF * D,), FF ** -0.5, 0.109375, ((0, 32),)),
        "ada_weight": normal_values(streams_of[9], (9 * D * D,), D ** -0.5, 0.21875, ((0, 32),)),
        "biases": normal_values(streams_of[10], (10 * D + FF,), 0.5, 3.0, ((0, 32),)),
        "cotangent": normal_values(streams_of[11], (MICRO, ITEMS, FRAMES, SPAT, D), 1.0, 6.0, ((1, 32),)),
    }


@jax.custom_vjp
def low(v):
    return lax.optimization_barrier(v.astype(jnp.bfloat16)).astype(jnp.float32)

@jax.custom_vjp
def low_back(v):
    return v

def low_keep(v):
    return (low(v), None)

def low_pass(kept, grad):
    return (grad,)

def back_keep(v):
    return (v, None)

def back_low(kept, grad):
    return (low(grad),)
low.defvjp(low_keep, low_pass)
low_back.defvjp(back_keep, back_low)
highest = lax.Precision.HIGHEST
epsilon = 1e-06
masked_score = -1e+30

def matmul(left_side, right_side):
    return jnp.dot(left_side, right_side, precision=highest, preferred_element_type=jnp.float32)

def layer_norm(token_rows):
    centre = token_rows - lax.optimization_barrier(jnp.mean(token_rows, axis=-1, keepdims=True))
    return centre * lax.rsqrt(lax.optimization_barrier(jnp.mean(centre * centre, axis=-1, keepdims=True)) + epsilon)

def attention(normed, qkv_matrix, proj_matrix, key_valid):
    leading, length = (normed.shape[0], normed.shape[1])
    projected = low_back(low(matmul(normed, qkv_matrix)))
    pieces = projected.reshape(leading, length, 3, HEADS, HD)
    queries, key_rows, values = (pieces[:, :, 0], pieces[:, :, 1], pieces[:, :, 2])
    scores = jnp.einsum('blhd,bmhd->bhlm', queries, key_rows, precision=highest) * HD ** (-0.5)
    if key_valid is not None:
        scores = jnp.where(key_valid[None, None, None, :] > 0.5, scores, masked_score)
    soft_rows = low(jax.nn.softmax(low_back(scores), axis=-1))
    context = jnp.einsum('bhlm,bmhd->blhd', soft_rows, values, precision=highest)
    context = low_back(low(context.reshape(leading, length, D)))
    return matmul(context, proj_matrix)

def condition_row(step_value):
    half_width = D // 2
    frequency = jnp.exp(-math.log(10000.0) * jnp.arange(half_width, dtype=jnp.float32) / half_width)
    angles = step_value.astype(jnp.float32) * frequency
    return jax.nn.silu(jnp.concatenate([jnp.cos(angles), jnp.sin(angles)]))

def layer_block(latent, step_value, valid_mask, flat_weights):
    space_qkv = flat_weights[0].reshape(D, 3 * D)
    space_proj = flat_weights[1].reshape(D, D)
    time_qkv = flat_weights[2].reshape(D, 3 * D)
    time_proj = flat_weights[3].reshape(D, D)
    up_matrix = flat_weights[4].reshape(D, FF)
    down_matrix = flat_weights[5].reshape(FF, D)
    ada_matrix = flat_weights[6].reshape(D, 9 * D)
    bias_vector = flat_weights[7]
    condition = low(condition_row(step_value))
    modulation = (matmul(condition[None, :], ada_matrix)[0] + bias_vector[:9 * D]).reshape(9, D)
    normed = low(layer_norm(latent) * (1.0 + modulation[1]) + modulation[0])
    space_out = low_back(attention(normed, space_qkv, space_proj, valid_mask))
    after_space = latent + modulation[2] * space_out
    normed = low(layer_norm(after_space) * (1.0 + modulation[4]) + modulation[3])
    time_out = low_back(jnp.swapaxes(attention(jnp.swapaxes(normed, 0, 1), time_qkv, time_proj, None), 0, 1))
    after_time = after_space + modulation[5] * time_out
    normed = low(layer_norm(after_time) * (1.0 + modulation[7]) + modulation[6])
    hidden = low_back(matmul(normed, up_matrix) + bias_vector[9 * D:9 * D + FF])
    activated = low(jax.nn.gelu(hidden, approximate=True))
    branch = low_back(matmul(activated, down_matrix) + bias_vector[9 * D + FF:])
    after_mlp = after_time + modulation[8] * branch
    return after_mlp * valid_mask[None, :, None]

def reference(latents, buckets, step_ids, qkv_spatial, proj_spatial, qkv_temporal, proj_temporal, up_weight, down_weight, ada_weight, biases, cotangent):
    flat_weights = tuple((weight.astype(jnp.float32) for weight in (qkv_spatial, proj_spatial, qkv_temporal, proj_temporal, up_weight, down_weight, ada_weight, biases)))
    lengths = jnp.where(buckets == 0, SPAT, jnp.where(buckets == 1, SPAT // 2, SPAT // 8)).astype(jnp.int32).reshape(MICRO * ITEMS)
    positions = jnp.arange(SPAT).astype(jnp.int32)
    shape_rows = (MICRO * ITEMS, FRAMES, SPAT, D)

    def per_item(running, item_data):
        latent, length, step_value, grad_rows = item_data
        valid_mask = (positions < length).astype(jnp.float32)

        def forward(latent_in, weights_in):
            return layer_block(latent_in, step_value, valid_mask, weights_in)
        result, pullback = jax.vjp(forward, latent.astype(jnp.float32), flat_weights)
        latent_grad, weight_grads = pullback(grad_rows.astype(jnp.float32))
        running = jax.tree.map(jnp.add, running, weight_grads)
        return (running, (result.astype(jnp.bfloat16), latent_grad))
    empty_grads = tuple((jnp.zeros(weight.shape, jnp.float32) for weight in flat_weights))
    scanned = (latents.reshape(shape_rows), lengths, step_ids.reshape(MICRO * ITEMS), cotangent.reshape(shape_rows))
    totals, (outputs, latent_grads) = lax.scan(per_item, empty_grads, scanned)
    full_shape = (MICRO, ITEMS, FRAMES, SPAT, D)
    return (outputs.reshape(full_shape), latent_grads.reshape(full_shape), totals[0], totals[1], totals[2], totals[3], totals[4], totals[5], totals[6], totals[7])
```

```python
import math

import jax
import jax.numpy as jnp
from jax import lax
from jax.sharding import PartitionSpec as P

D = 768
HEADS = 12
HD = 64
FF = 3072
AXES = ("wide", "narrow")
EPS = 1e-06
MASKED = -1e30
F32 = jnp.float32
BF16 = jnp.bfloat16


def timestep_condition(step_values):
    half_width = D // 2
    frequency = jnp.exp(-math.log(10000.0) * jnp.arange(half_width, dtype=F32) / half_width)
    angles = step_values.astype(F32)[:, None] * frequency
    return jax.nn.silu(jnp.concatenate([jnp.cos(angles), jnp.sin(angles)], axis=-1)).astype(BF16)


def norm_parts(rows):
    centre = rows - jnp.mean(rows, axis=-1, keepdims=True)
    inverse = lax.rsqrt(jnp.mean(centre * centre, axis=-1, keepdims=True) + EPS)
    return centre * inverse, inverse


def norm_back(grad, normed, inverse, scale):
    shift_grad = jnp.sum(grad, axis=1)
    scale_grad = jnp.sum(grad * normed, axis=1)
    pulled = grad * (1.0 + scale)
    back = inverse * (
        pulled
        - jnp.mean(pulled, axis=-1, keepdims=True)
        - normed * jnp.mean(pulled * normed, axis=-1, keepdims=True)
    )
    return back, shift_grad, scale_grad


def dot(a, b):
    return jnp.dot(a, b, preferred_element_type=F32)


def heads(x):
    return x.reshape(x.shape[0], x.shape[1], HEADS, HD)


def attention(low, qkv_w, proj_w, mask):
    packed = dot(low, qkv_w).astype(BF16)
    q, k, v = (heads(part) for part in jnp.split(packed, 3, axis=-1))
    scores = jnp.einsum("bqhd,bkhd->bhqk", q, k, preferred_element_type=F32) * HD ** (-0.5)
    scores = jnp.where(mask, scores, MASKED)
    soft = jax.nn.softmax(scores, axis=-1)
    context = jnp.einsum("bhqk,bkhd->bqhd", soft.astype(BF16), v, preferred_element_type=F32)
    context = context.astype(BF16).reshape(low.shape)
    return dot(context, proj_w), (q, k, v, soft, context)


def attention_back(grad_low, low, qkv_w, proj_w, kept):
    q, k, v, soft, context = kept
    proj_grad = jnp.einsum("bld,ble->de", context, grad_low, preferred_element_type=F32)
    ctx = heads(jnp.einsum("ble,de->bld", grad_low, proj_w, preferred_element_type=F32).astype(BF16))
    v_grad = jnp.einsum("bhqk,bqhd->bkhd", soft.astype(BF16), ctx, preferred_element_type=F32)
    soft_grad = jnp.einsum("bqhd,bkhd->bhqk", ctx, v, preferred_element_type=F32)
    row_dot = jnp.sum(soft_grad * soft, axis=-1, keepdims=True)
    score_grad = (soft * (soft_grad - row_dot)).astype(BF16)
    q_grad = jnp.einsum("bhqk,bkhd->bqhd", score_grad, k, preferred_element_type=F32) * HD ** (-0.5)
    k_grad = jnp.einsum("bhqk,bqhd->bkhd", score_grad, q, preferred_element_type=F32) * HD ** (-0.5)
    packed = jnp.concatenate(
        [part.astype(BF16).reshape(low.shape) for part in (q_grad, k_grad, v_grad)], axis=-1
    )
    qkv_grad = jnp.einsum("bld,ble->de", low, packed, preferred_element_type=F32)
    low_grad = jnp.einsum("ble,de->bld", packed, qkv_w, preferred_element_type=F32)
    return low_grad, qkv_grad, proj_grad


def per_device(latents, buckets, step_ids, qs, ps, qt, pt, up, down, ada, biases, cotangent):
    devices = lax.axis_size(AXES)
    micro = latents.shape[0]
    frames, spatial = latents.shape[2], latents.shape[3]
    tokens = frames * spatial
    rows = D // devices

    steps = lax.all_gather(step_ids[:, 0], AXES, axis=0, tiled=True)
    condition = timestep_condition(steps)
    ada_columns = lax.all_to_all(
        ada.reshape(rows, 9 * D), AXES, split_axis=1, concat_axis=0, tiled=True
    )
    modulation = lax.all_to_all(
        dot(condition, ada_columns), AXES, split_axis=0, concat_axis=1, tiled=True
    )
    bias = lax.all_gather(biases, AXES, axis=0, tiled=True).astype(F32)
    modulation = (modulation + bias[: 9 * D]).reshape(micro, 9, 1, D)
    b_up, b_down = bias[9 * D : 9 * D + FF], bias[9 * D + FF :]

    wide_shard = jnp.concatenate([w.reshape(rows, -1) for w in (qs, ps, qt, pt, up)], axis=1)
    wide = lax.all_gather(wide_shard, AXES, axis=0, tiled=True)
    w_down = lax.all_gather(down.reshape(-1, D), AXES, axis=0, tiled=True)
    cuts = [3 * D, 4 * D, 7 * D, 8 * D]
    w_qs, w_ps, w_qt, w_pt, w_up = jnp.split(wide, cuts, axis=1)

    positions = jnp.arange(tokens)
    frame, place = positions // spatial, positions % spatial
    bucket = buckets[:, 0]
    length = jnp.where(bucket == 0, spatial, jnp.where(bucket == 1, spatial // 2, spatial // 8))
    valid = place[None, :] < length[:, None]
    space_mask = (frame[:, None] == frame[None, :])[None, None] & valid[:, None, None, :]
    time_mask = (place[:, None] == place[None, :])[None, None]
    valid_rows = valid.astype(F32)[:, :, None]

    sh1, sc1, ga1, sh2, sc2, ga2, sh3, sc3, ga3 = (modulation[:, i] for i in range(9))
    x = latents.reshape(micro, tokens, D).astype(F32)
    n1, r1 = norm_parts(x)
    h1 = (n1 * (1.0 + sc1) + sh1).astype(BF16)
    a1, kept1 = attention(h1, w_qs, w_ps, space_mask)
    x1 = x + ga1 * a1
    n2, r2 = norm_parts(x1)
    h2 = (n2 * (1.0 + sc2) + sh2).astype(BF16)
    a2, kept2 = attention(h2, w_qt, w_pt, time_mask)
    x2 = x1 + ga2 * a2
    n3, r3 = norm_parts(x2)
    h3 = (n3 * (1.0 + sc3) + sh3).astype(BF16)
    hidden = dot(h3, w_up) + b_up
    gelu, pull = jax.vjp(lambda u: jax.nn.gelu(u, approximate=True), hidden)
    g = gelu.astype(BF16)
    m = dot(g, w_down) + b_down
    x3 = x2 + ga3 * m
    output = (x3 * valid_rows).astype(BF16)

    d3 = cotangent.reshape(micro, tokens, D).astype(F32) * valid_rows
    dm = (ga3 * d3).astype(BF16)
    dga3 = jnp.sum(d3 * m, axis=1)
    db_down = jnp.sum(dm.astype(F32), axis=(0, 1))
    dw_down = jnp.einsum("bsk,bsd->kd", g, dm, preferred_element_type=F32)
    dg = jnp.einsum("bsd,kd->bsk", dm, w_down, preferred_element_type=F32)
    du = pull(dg)[0].astype(BF16)
    db_up = jnp.sum(du.astype(F32), axis=(0, 1))
    dw_up = jnp.einsum("bsd,bsk->dk", h3, du, preferred_element_type=F32)
    dh3 = jnp.einsum("bsk,dk->bsd", du, w_up, preferred_element_type=F32)
    dv, dsh3, dsc3 = norm_back(dh3, n3, r3, sc3)
    d2 = d3 + dv
    da2 = (ga2 * d2).astype(BF16)
    dga2 = jnp.sum(d2 * a2, axis=1)
    dh2, dw_qt, dw_pt = attention_back(da2, h2, w_qt, w_pt, kept2)
    dv, dsh2, dsc2 = norm_back(dh2, n2, r2, sc2)
    d1 = d2 + dv
    da1 = (ga1 * d1).astype(BF16)
    dga1 = jnp.sum(d1 * a1, axis=1)
    dh1, dw_qs, dw_ps = attention_back(da1, h1, w_qs, w_ps, kept1)
    dv, dsh1, dsc1 = norm_back(dh1, n1, r1, sc1)
    latents_grad = d1 + dv

    dmod = jnp.concatenate([dsh1, dsc1, dga1, dsh2, dsc2, dga2, dsh3, dsc3, dga3], axis=-1)
    small = jnp.concatenate([dmod.reshape(1, -1), db_up[None], db_down[None]], axis=-1)
    small = lax.all_gather(small.astype(BF16), AXES, axis=0, tiled=True)
    dmod_all = small[:, : micro * 9 * D].reshape(devices * micro, 9 * D)
    me = lax.axis_index(AXES)
    my_condition = lax.dynamic_slice_in_dim(condition, me * rows, rows, axis=1)
    dw_ada = lax.dot_general(
        my_condition, dmod_all, (((0,), (0,)), ((), ())), preferred_element_type=F32
    )
    db = jnp.concatenate(
        [
            jnp.sum(dmod_all.astype(F32), axis=0),
            jnp.sum(small[:, micro * 9 * D :].astype(F32), axis=0),
        ]
    )
    db = lax.dynamic_slice_in_dim(db, me * biases.shape[0], biases.shape[0])

    dwide = jnp.concatenate([w.astype(BF16) for w in (dw_qs, dw_ps, dw_qt, dw_pt, dw_up)], axis=1)
    dwide = lax.psum_scatter(dwide, AXES, scatter_dimension=0, tiled=True).astype(F32)
    ddown = lax.psum_scatter(dw_down.astype(BF16), AXES, scatter_dimension=0, tiled=True).astype(F32)
    flat = tuple(part.reshape(-1) for part in jnp.split(dwide, cuts, axis=1))
    shape = latents.shape
    return (
        output.reshape(shape),
        latents_grad.reshape(shape),
        *flat,
        ddown.reshape(-1),
        dw_ada.reshape(-1),
        db,
    )


def solution(mesh):
    items = P(None, AXES, None, None, None)
    flat = P(AXES)
    return jax.shard_map(
        per_device,
        mesh=mesh,
        in_specs=(items, P(None, AXES), P(None, AXES)) + (flat,) * 8 + (items,),
        out_specs=(items, items) + (flat,) * 8,
        check_vma=False,
    )
```

```python
import math

import jax
import jax.numpy as jnp
from jax import lax
from jax.experimental import pallas as pl
from jax.experimental.pallas import tpu as pltpu
from jax.sharding import PartitionSpec as P

D = 768
HEADS = 12
HD = 64
FF = 3072
AXES = ("wide", "narrow")
EPS = 1e-06
MASKED = -1e30
F32 = jnp.float32
BF16 = jnp.bfloat16


def timestep_condition(step_values):
    half_width = D // 2
    frequency = jnp.exp(-math.log(10000.0) * jnp.arange(half_width, dtype=F32) / half_width)
    angles = step_values.astype(F32)[:, None] * frequency
    return jax.nn.silu(jnp.concatenate([jnp.cos(angles), jnp.sin(angles)], axis=-1)).astype(BF16)


def norm_parts(rows):
    centre = rows - jnp.mean(rows, axis=-1, keepdims=True)
    inverse = lax.rsqrt(jnp.mean(centre * centre, axis=-1, keepdims=True) + EPS)
    return centre * inverse, inverse


def norm_back(grad, normed, inverse, scale):
    shift_grad = jnp.sum(grad, axis=1)
    scale_grad = jnp.sum(grad * normed, axis=1)
    pulled = grad * (1.0 + scale)
    back = inverse * (
        pulled
        - jnp.mean(pulled, axis=-1, keepdims=True)
        - normed * jnp.mean(pulled * normed, axis=-1, keepdims=True)
    )
    return back, shift_grad, scale_grad


def dot(a, b):
    return jnp.dot(a, b, preferred_element_type=F32)


def heads(x):
    return x.reshape(x.shape[0], x.shape[1], HEADS, HD)


def attention(low, qkv_w, proj_w, mask):
    packed = dot(low, qkv_w).astype(BF16)
    q, k, v = (heads(part) for part in jnp.split(packed, 3, axis=-1))
    scores = jnp.einsum("bqhd,bkhd->bhqk", q, k, preferred_element_type=F32) * HD ** (-0.5)
    scores = jnp.where(mask, scores, MASKED)
    soft = jax.nn.softmax(scores, axis=-1)
    context = jnp.einsum("bhqk,bkhd->bqhd", soft.astype(BF16), v, preferred_element_type=F32)
    context = context.astype(BF16).reshape(low.shape)
    return dot(context, proj_w), (q, k, v, soft, context)


def attention_back(grad_low, low, qkv_w, proj_w, kept):
    q, k, v, soft, context = kept
    proj_grad = jnp.einsum("bld,ble->de", context, grad_low, preferred_element_type=F32)
    ctx = heads(jnp.einsum("ble,de->bld", grad_low, proj_w, preferred_element_type=F32).astype(BF16))
    v_grad = jnp.einsum("bhqk,bqhd->bkhd", soft.astype(BF16), ctx, preferred_element_type=F32)
    soft_grad = jnp.einsum("bqhd,bkhd->bhqk", ctx, v, preferred_element_type=F32)
    row_dot = jnp.sum(soft_grad * soft, axis=-1, keepdims=True)
    score_grad = (soft * (soft_grad - row_dot)).astype(BF16)
    q_grad = jnp.einsum("bhqk,bkhd->bqhd", score_grad, k, preferred_element_type=F32) * HD ** (-0.5)
    k_grad = jnp.einsum("bhqk,bqhd->bkhd", score_grad, q, preferred_element_type=F32) * HD ** (-0.5)
    packed = jnp.concatenate(
        [part.astype(BF16).reshape(low.shape) for part in (q_grad, k_grad, v_grad)], axis=-1
    )
    qkv_grad = jnp.einsum("bld,ble->de", low, packed, preferred_element_type=F32)
    low_grad = jnp.einsum("ble,de->bld", packed, qkv_w, preferred_element_type=F32)
    return low_grad, qkv_grad, proj_grad

MESH = pl.DeviceIdType.MESH


def place():
    w, z = lax.axis_index("wide"), lax.axis_index("narrow")
    return w // 4, (w // 2) % 2, w % 2, z


def device_at(y, x, c, z):
    return {"wide": (y * 2 + x) * 2 + c, "narrow": z}


def greet(here):
    y, x, c, z = here
    barrier = pltpu.get_barrier_semaphore()
    partners = [device_at(y, x, 1 - c, z), device_at(y, 1 - x, c, z), device_at(1 - y, x, c, z)]
    partners += [device_at(y, x, c, (z + step) % 4) for step in (1, 2, 3)]
    for partner in partners:
        pl.semaphore_signal(barrier, inc=1, device_id=partner, device_id_type=MESH)
    pl.semaphore_wait(barrier, 6)


def remote(src, dst, send, recv, target):
    return pltpu.make_async_remote_copy(
        src_ref=src, dst_ref=dst, send_sem=send, recv_sem=recv,
        device_id=target, device_id_type=MESH,
    )


class Sender:
    def __init__(self):
        self.copies = []

    def go(self, src, dst, send, recv, target):
        copy = remote(src, dst, send, recv, target)
        copy.start()
        self.copies.append(copy)

    def drain(self):
        for copy in self.copies:
            copy.wait_send()


class Gather:
    SEMAPHORES = (3, 3, 10, 10, 3, 3, 3, 3)

    def __init__(self, here, sender, own, out, semaphores, local):
        self.here, self.sender, self.own, self.out, self.local = here, sender, own, out, local
        self.zs, self.zr, self.cs, self.cr, self.xs, self.xr, self.ys, self.yr = semaphores
        y, x, c, z = here
        self.sib = device_at(y, x, 1 - c, z)
        self.xn = device_at(y, 1 - x, c, z)
        self.yn = device_at(1 - y, x, c, z)

    @staticmethod
    def scratch(count):
        kinds = [pltpu.SemaphoreType.DMA((count, k)) for k in Gather.SEMAPHORES]
        return kinds + [pltpu.SemaphoreType.DMA((count,))]

    def start(self):
        y, x, c, z = self.here
        count = len(self.own)
        for i in range(count):
            for step in (2, 1, 3):
                self.sender.go(
                    self.own[i], self.out[i].at[y, x, c, z], self.zs.at[i, step - 1],
                    self.zr.at[i, step - 1], device_at(y, x, c, (z + step) % 4),
                )
        for i in range(count):
            mine = self.out[i].at[y, x, c, z]
            pltpu.make_async_copy(self.own[i], mine, self.local.at[i]).start()
            self.sender.go(self.own[i], mine, self.cs.at[i, 0], self.cr.at[i, 0], self.sib)

    def along(self, ref, send, recv, target):
        self.sender.go(ref, ref, send, recv, target)

    def arrived(self, ref, send, recv):
        remote(ref, ref, send, recv, self.sib).wait_recv()

    def across(self, i, k, ref):
        self.sender.go(ref, ref, self.cs.at[i, k], self.cr.at[i, k], self.sib)

    def stage1(self, i):
        y, x, c, z = self.here
        out = self.out[i]
        pltpu.make_async_copy(self.own[i], out.at[y, x, c, z], self.local.at[i]).wait()
        for step in (1, 2, 3):
            self.arrived(out.at[y, x, c, (z + 4 - step) % 4], self.zs.at[i, step - 1], self.zr.at[i, step - 1])
        low, high = out.at[y, x, c, pl.ds(0, 2)], out.at[y, x, c, pl.ds(2, 2)]
        self.along(low, self.xs.at[i, 0], self.xr.at[i, 0], self.xn)
        self.along(high, self.ys.at[i, 0], self.yr.at[i, 0], self.yn)
        self.along(high, self.xs.at[i, 1], self.xr.at[i, 1], self.xn)
        self.along(low, self.ys.at[i, 1], self.yr.at[i, 1], self.yn)
        for step in (1, 2, 3):
            self.across(i, step, out.at[y, x, c, (z + 4 - step) % 4])

    def stage2(self, i):
        y, x, c, z = self.here
        low_x = self.out[i].at[y, 1 - x, c, pl.ds(0, 2)]
        high_y = self.out[i].at[1 - y, x, c, pl.ds(2, 2)]
        self.arrived(low_x, self.xs.at[i, 0], self.xr.at[i, 0])
        self.along(low_x, self.ys.at[i, 2], self.yr.at[i, 2], self.yn)
        self.arrived(high_y, self.ys.at[i, 0], self.yr.at[i, 0])
        self.along(high_y, self.xs.at[i, 2], self.xr.at[i, 2], self.xn)
        self.across(i, 4, low_x)
        self.across(i, 5, high_y)

    def stage3(self, i):
        y, x, c, z = self.here
        out = self.out[i]
        arrivals = (
            (out.at[y, 1 - x, c, pl.ds(2, 2)], self.xs.at[i, 1], self.xr.at[i, 1]),
            (out.at[1 - y, x, c, pl.ds(0, 2)], self.ys.at[i, 1], self.yr.at[i, 1]),
            (out.at[1 - y, 1 - x, c, pl.ds(2, 2)], self.xs.at[i, 2], self.xr.at[i, 2]),
            (out.at[1 - y, 1 - x, c, pl.ds(0, 2)], self.ys.at[i, 2], self.yr.at[i, 2]),
        )
        for k, (ref, send, recv) in enumerate(arrivals):
            self.arrived(ref, send, recv)
            self.across(i, 6 + k, ref)

    def finish(self, i):
        y, x, c, z = self.here
        o = 1 - c
        out = self.out[i]
        arrivals = [out.at[y, x, o, (z + 4 - step) % 4] for step in (0, 1, 2, 3)]
        arrivals += [
            out.at[y, 1 - x, o, pl.ds(0, 2)],
            out.at[1 - y, x, o, pl.ds(2, 2)],
            out.at[y, 1 - x, o, pl.ds(2, 2)],
            out.at[1 - y, x, o, pl.ds(0, 2)],
            out.at[1 - y, 1 - x, o, pl.ds(2, 2)],
            out.at[1 - y, 1 - x, o, pl.ds(0, 2)],
        ]
        for k, ref in enumerate(arrivals):
            self.arrived(ref, self.cs.at[i, k], self.cr.at[i, k])


def gather_kernel(count, *refs):
    here = place()
    sender = Sender()
    rest = refs[2 * count :]
    gather = Gather(here, sender, refs[:count], refs[count : 2 * count], rest[:8], rest[8])
    greet(here)
    gather.start()
    for t in range(count + 2):
        if t < count:
            gather.stage1(t)
        if 0 <= t - 1 < count:
            gather.stage2(t - 1)
        if 0 <= t - 2 < count:
            gather.stage3(t - 2)
    for i in range(count):
        gather.finish(i)
    sender.drain()


def gather_all(shards):
    count = len(shards)
    return pl.pallas_call(
        lambda *refs: gather_kernel(count, *refs),
        out_shape=tuple(jax.ShapeDtypeStruct((2, 2, 2, 4) + s.shape, s.dtype) for s in shards),
        in_specs=[pl.BlockSpec(memory_space=pltpu.VMEM)] * count,
        out_specs=tuple([pl.BlockSpec(memory_space=pl.ANY)] * count),
        scratch_shapes=Gather.scratch(count),
        compiler_params=pltpu.CompilerParams(collective_id=1, has_side_effects=True),
        name="gather_weights",
    )(*shards)


class Scatter:
    SEMAPHORES = ((), (), (), (2,), (2,), (2,), (2,), (3,), (3,))
    LEADING = ((2, 2, 4), (2, 2, 4), (2, 2), (2, 2), (2,), (2,), (3,))

    def __init__(self, here, sender, part, out, buffers, semaphores):
        self.here, self.sender, self.part, self.out = here, sender, part, out
        n = len(part)
        self.acc, self.r0, self.r1a, self.r1b, self.r2a, self.r2b, self.r3 = (
            buffers[k * n : (k + 1) * n] for k in range(7)
        )
        self.local, self.cs, self.cr, self.s1, self.v1, self.s2, self.v2, self.s3, self.v3 = semaphores
        y, x, c, z = here
        self.sib = device_at(y, x, 1 - c, z)
        self.xn = device_at(y, 1 - x, c, z)
        self.yn = device_at(1 - y, x, c, z)

    @staticmethod
    def scratch(blocks):
        n = len(blocks)
        kinds = [pltpu.VMEM(lead + b, BF16) for lead in Scatter.LEADING for b in blocks]
        return kinds + [pltpu.SemaphoreType.DMA((n,) + k) for k in Scatter.SEMAPHORES]

    def load(self, i):
        c = self.here[2]
        return pltpu.make_async_copy(self.part[i].at[:, :, c], self.acc[i], self.local.at[i])

    def hop(self, i, stage, k):
        y, x, c, z = self.here
        acc = self.acc[i]
        if stage == 0:
            return (self.part[i].at[:, :, 1 - c], self.r0[i], self.cs.at[i], self.cr.at[i], self.sib)
        if stage == 1:
            if k == 0:
                return (acc.at[1 - y, :, pl.ds(0, 2)], self.r1a[i], self.s1.at[i, 0], self.v1.at[i, 0], self.yn)
            return (acc.at[:, 1 - x, pl.ds(2, 2)], self.r1b[i], self.s1.at[i, 1], self.v1.at[i, 1], self.xn)
        if stage == 2:
            if k == 0:
                return (acc.at[y, 1 - x, pl.ds(0, 2)], self.r2a[i], self.s2.at[i, 0], self.v2.at[i, 0], self.xn)
            return (acc.at[1 - y, x, pl.ds(2, 2)], self.r2b[i], self.s2.at[i, 1], self.v2.at[i, 1], self.yn)
        there = (z + k + 1) % 4
        return (acc.at[y, x, there], self.r3[i].at[k], self.s3.at[i, k], self.v3.at[i, k], device_at(y, x, c, there))

    def send(self, i, stage, k):
        self.sender.go(*self.hop(i, stage, k))

    def wait(self, i, stage, k):
        remote(*self.hop(i, stage, k)).wait_recv()

    def start(self):
        for i in range(len(self.part)):
            self.send(i, 0, 0)

    def stage1(self, i):
        acc, r0 = self.acc[i], self.r0[i]
        self.load(i).wait()
        self.wait(i, 0, 0)

        def add(k, _):
            a, b, q = k // 8, (k // 4) % 2, k % 4
            acc[a, b, q] = acc[a, b, q] + r0[a, b, q]
            return 0

        lax.fori_loop(0, 16, add, 0)
        self.send(i, 1, 0)
        self.send(i, 1, 1)

    def stage2(self, i):
        y, x, c, z = self.here
        acc, r1a, r1b = self.acc[i], self.r1a[i], self.r1b[i]
        self.wait(i, 1, 0)
        self.wait(i, 1, 1)

        def add(k, _):
            a, q = k // 2, k % 2
            acc[y, a, q] = acc[y, a, q] + r1a[a, q]
            acc[a, x, q + 2] = acc[a, x, q + 2] + r1b[a, q]
            return 0

        lax.fori_loop(0, 4, add, 0)
        self.send(i, 2, 0)
        self.send(i, 2, 1)

    def stage3(self, i):
        y, x, c, z = self.here
        acc = self.acc[i]
        self.wait(i, 2, 0)
        self.wait(i, 2, 1)
        for q in range(2):
            acc[y, x, q] = acc[y, x, q] + self.r2a[i][q]
            acc[y, x, q + 2] = acc[y, x, q + 2] + self.r2b[i][q]
        for k in (1, 0, 2):
            self.send(i, 3, k)

    def stage4(self, i):
        y, x, c, z = self.here
        for k in range(3):
            self.wait(i, 3, k)
        acc, r3 = self.acc[i], self.r3[i]
        self.out[i][...] = (acc[y, x, z].astype(F32) + r3[0].astype(F32)) + (
            r3[1].astype(F32) + r3[2].astype(F32)
        )


def scatter_kernel(n, *refs):
    here = place()
    sender = Sender()
    part, small = refs[:n], refs[n]
    out, small_out = refs[n + 1 : 2 * n + 1], refs[2 * n + 1]
    rest = refs[2 * n + 2 :]
    scatter = Scatter(here, sender, part, out, rest[: 7 * n], rest[7 * n : 7 * n + 9])
    gather = Gather(here, sender, [small], [small_out], rest[7 * n + 9 : -1], rest[-1])
    for i in range(n):
        scatter.load(i).start()
    greet(here)
    gather.start()
    scatter.start()
    for t in range(n + 3):
        if t < n:
            scatter.stage1(t)
        if 0 <= t - 1 < n:
            scatter.stage2(t - 1)
        if 0 <= t - 2 < n:
            scatter.stage3(t - 2)
        if 0 <= t - 3 < n:
            scatter.stage4(t - 3)
        if t < 4:
            (gather.stage1, gather.stage2, gather.stage3, gather.finish)[t](0)
    sender.drain()


def scatter_all(parts, small):
    n = len(parts)
    blocks = [p.shape[4:] for p in parts]
    any_space = pl.BlockSpec(memory_space=pl.ANY)
    vmem = pl.BlockSpec(memory_space=pltpu.VMEM)
    return pl.pallas_call(
        lambda *refs: scatter_kernel(n, *refs),
        out_shape=tuple(jax.ShapeDtypeStruct(b, F32) for b in blocks)
        + (jax.ShapeDtypeStruct((2, 2, 2, 4) + small.shape, small.dtype),),
        in_specs=[any_space] * n + [vmem],
        out_specs=tuple([vmem] * n + [any_space]),
        scratch_shapes=Scatter.scratch(blocks) + Gather.scratch(1),
        compiler_params=pltpu.CompilerParams(
            collective_id=2, has_side_effects=True, vmem_limit_bytes=60 << 20
        ),
        name="scatter_gradients",
    )(*parts, small)


def gather_plain(shards):
    return tuple(lax.all_gather(s, AXES, axis=0) for s in shards)


def scatter_plain(parts, small):
    devices = lax.axis_size(AXES)
    sums = tuple(
        lax.psum_scatter(p.reshape((devices,) + p.shape[-2:]), AXES, scatter_dimension=0, tiled=True)[
            0
        ].astype(F32)
        for p in parts
    )
    return sums + (lax.all_gather(small, AXES, axis=0),)


def per_device(latents, buckets, step_ids, qs, ps, qt, pt, up, down, ada, biases, cotangent):
    devices = lax.axis_size(AXES)
    micro = latents.shape[0]
    frames, spatial = latents.shape[2], latents.shape[3]
    tokens = frames * spatial
    rows = D // devices

    known = lax.axis_size("wide") == 8 and lax.axis_size("narrow") == 4
    gather, scatter = (gather_all, scatter_all) if known else (gather_plain, scatter_plain)

    ada_columns = lax.all_to_all(
        ada.reshape(rows, 9 * D), AXES, split_axis=1, concat_axis=0, tiled=True
    )
    own_bias = jnp.pad(biases, (0, D - biases.shape[0]))[None]
    small = jnp.concatenate([timestep_condition(step_ids[:, 0]), own_bias], axis=0)
    shards = [small] + [w.reshape(rows, -1) for w in (qs, ps, qt, pt, up)] + [down.reshape(-1, D)]
    small, *gathered = gather(shards)
    w_qs, w_ps, w_qt, w_pt, w_up = (w.reshape(D, -1) for w in gathered[:5])
    w_down = gathered[5].reshape(-1, D)
    small = small.reshape(devices, micro + 1, D)
    condition = small[:, :micro].reshape(devices * micro, D)
    bias = small[:, micro, : biases.shape[0]].reshape(-1).astype(F32)
    modulation = lax.all_to_all(
        dot(condition, ada_columns), AXES, split_axis=0, concat_axis=1, tiled=True
    )
    modulation = (modulation + bias[: 9 * D]).reshape(micro, 9, 1, D)
    b_up, b_down = bias[9 * D : 9 * D + FF], bias[9 * D + FF :]

    positions = jnp.arange(tokens)
    frame, place = positions // spatial, positions % spatial
    bucket = buckets[:, 0]
    length = jnp.where(bucket == 0, spatial, jnp.where(bucket == 1, spatial // 2, spatial // 8))
    valid = place[None, :] < length[:, None]
    space_mask = (frame[:, None] == frame[None, :])[None, None] & valid[:, None, None, :]
    time_mask = (place[:, None] == place[None, :])[None, None]
    valid_rows = valid.astype(F32)[:, :, None]

    sh1, sc1, ga1, sh2, sc2, ga2, sh3, sc3, ga3 = (modulation[:, i] for i in range(9))
    x = latents.reshape(micro, tokens, D).astype(F32)
    n1, r1 = norm_parts(x)
    h1 = (n1 * (1.0 + sc1) + sh1).astype(BF16)
    a1, kept1 = attention(h1, w_qs, w_ps, space_mask)
    x1 = x + ga1 * a1
    n2, r2 = norm_parts(x1)
    h2 = (n2 * (1.0 + sc2) + sh2).astype(BF16)
    a2, kept2 = attention(h2, w_qt, w_pt, time_mask)
    x2 = x1 + ga2 * a2
    n3, r3 = norm_parts(x2)
    h3 = (n3 * (1.0 + sc3) + sh3).astype(BF16)
    hidden = dot(h3, w_up) + b_up
    gelu, pull = jax.vjp(lambda u: jax.nn.gelu(u, approximate=True), hidden)
    g = gelu.astype(BF16)
    m = dot(g, w_down) + b_down
    x3 = x2 + ga3 * m
    output = (x3 * valid_rows).astype(BF16)

    d3 = cotangent.reshape(micro, tokens, D).astype(F32) * valid_rows
    dm = (ga3 * d3).astype(BF16)
    dga3 = jnp.sum(d3 * m, axis=1)
    db_down = jnp.sum(dm.astype(F32), axis=(0, 1))
    dw_down = jnp.einsum("bsk,bsd->kd", g, dm, preferred_element_type=F32)
    dg = jnp.einsum("bsd,kd->bsk", dm, w_down, preferred_element_type=F32)
    du = pull(dg)[0].astype(BF16)
    db_up = jnp.sum(du.astype(F32), axis=(0, 1))
    dw_up = jnp.einsum("bsd,bsk->dk", h3, du, preferred_element_type=F32)
    dh3 = jnp.einsum("bsk,dk->bsd", du, w_up, preferred_element_type=F32)
    dv, dsh3, dsc3 = norm_back(dh3, n3, r3, sc3)
    d2 = d3 + dv
    da2 = (ga2 * d2).astype(BF16)
    dga2 = jnp.sum(d2 * a2, axis=1)
    dh2, dw_qt, dw_pt = attention_back(da2, h2, w_qt, w_pt, kept2)
    dv, dsh2, dsc2 = norm_back(dh2, n2, r2, sc2)
    d1 = d2 + dv
    da1 = (ga1 * d1).astype(BF16)
    dga1 = jnp.sum(d1 * a1, axis=1)
    dh1, dw_qs, dw_ps = attention_back(da1, h1, w_qs, w_ps, kept1)
    dv, dsh1, dsc1 = norm_back(dh1, n1, r1, sc1)
    latents_grad = d1 + dv

    dmod = jnp.stack([dsh1, dsc1, dga1, dsh2, dsc2, dga2, dsh3, dsc3, dga3], axis=1)
    small = jnp.concatenate(
        [dmod.reshape(micro * 9, D), db_up.reshape(-1, D), db_down.reshape(-1, D)], axis=0
    ).astype(BF16)
    parts = [
        part.astype(BF16).reshape(tuple(gathered[i].shape))
        for i, part in ((5, dw_down), (4, dw_up), (3, dw_pt), (2, dw_qt), (1, dw_ps), (0, dw_qs))
    ]
    ddown, dup, dpt, dqt, dps, dqs, small = scatter(parts, small)
    flat = tuple(part.reshape(-1) for part in (dqs, dps, dqt, dpt, dup))
    small = small.reshape(devices, -1, D)
    dmod_all = small[:, : micro * 9].reshape(devices * micro, 9 * D)
    me = lax.axis_index(AXES)
    my_condition = lax.dynamic_slice_in_dim(condition, me * rows, rows, axis=1)
    dw_ada = lax.dot_general(
        my_condition, dmod_all, (((0,), (0,)), ((), ())), preferred_element_type=F32
    )
    db = jnp.concatenate(
        [
            jnp.sum(dmod_all.astype(F32), axis=0),
            jnp.sum(small[:, micro * 9 :].astype(F32), axis=0).reshape(-1),
        ]
    )
    db = lax.dynamic_slice_in_dim(db, me * biases.shape[0], biases.shape[0])

    shape = latents.shape
    return (
        output.reshape(shape),
        latents_grad.reshape(shape),
        *flat,
        ddown.reshape(-1),
        dw_ada.reshape(-1),
        db,
    )


def solution(mesh):
    items = P(None, AXES, None, None, None)
    flat = P(AXES)
    return jax.shard_map(
        per_device,
        mesh=mesh,
        in_specs=(items, P(None, AXES), P(None, AXES)) + (flat,) * 8 + (items,),
        out_specs=(items, items) + (flat,) * 8,
        check_vma=False,
    )
```

```python
import math

import jax
import jax.numpy as jnp
from jax import lax
from jax.experimental import pallas as pl
from jax.experimental.pallas import tpu as pltpu
from jax.sharding import PartitionSpec as P

D = 768
HEADS = 12
HD = 64
FF = 3072
AXES = ("wide", "narrow")
EPS = 1e-06
MASKED = -1e30
F32 = jnp.float32
BF16 = jnp.bfloat16
GELU = math.sqrt(2.0 / math.pi)
MESH = pl.DeviceIdType.MESH
DEVICES = 32
OWNERS = 9 * D // 256
SHARE = (10 * D + FF) // DEVICES
SPATIAL = 16
TOKENS = 256
VMEM_LIMIT = 67_000_000


def dot(a, b):
    return jnp.dot(a, b, preferred_element_type=F32)


def place():
    w, z = lax.axis_index("wide"), lax.axis_index("narrow")
    return w // 4, (w // 2) % 2, w % 2, z


def device_at(y, x, c, z):
    return {"wide": (y * 2 + x) * 2 + c, "narrow": z}


def remote(src, dst, send, recv, target):
    return pltpu.make_async_remote_copy(
        src_ref=src, dst_ref=dst, send_sem=send, recv_sem=recv,
        device_id=target, device_id_type=MESH,
    )


class Sender:
    def __init__(self):
        self.copies = []

    def go(self, src, dst, send, recv, target):
        copy = remote(src, dst, send, recv, target)
        copy.start()
        self.copies.append(copy)

    def drain(self):
        for copy in self.copies:
            copy.wait_send()


def timestep_condition(step_values):
    half_width = D // 2
    frequency = jnp.exp(-math.log(10000.0) * jnp.arange(half_width, dtype=F32) / half_width)
    angles = step_values.astype(F32)[:, None] * frequency
    return jax.nn.silu(jnp.concatenate([jnp.cos(angles), jnp.sin(angles)], axis=-1)).astype(BF16)


class Gather:
    SEMAPHORES = (3, 3, 10, 10, 3, 3, 3, 3)

    def __init__(self, here, sender, own, out, semaphores, local):
        self.here, self.sender, self.own, self.out, self.local = here, sender, own, out, local
        self.zs, self.zr, self.cs, self.cr, self.xs, self.xr, self.ys, self.yr = semaphores
        y, x, c, z = here
        self.sib = device_at(y, x, 1 - c, z)
        self.xn = device_at(y, 1 - x, c, z)
        self.yn = device_at(1 - y, x, c, z)

    @staticmethod
    def scratch(count):
        kinds = [pltpu.SemaphoreType.DMA((count, k)) for k in Gather.SEMAPHORES]
        return kinds + [pltpu.SemaphoreType.DMA((count,))]

    def start(self, i):
        y, x, c, z = self.here
        mine = self.out[i].at[y, x, c, z]
        for step in (2, 1, 3):
            self.sender.go(
                self.own[i], mine, self.zs.at[i, step - 1],
                self.zr.at[i, step - 1], device_at(y, x, c, (z + step) % 4),
            )
        pltpu.make_async_copy(self.own[i], mine, self.local.at[i]).start()
        self.sender.go(self.own[i], mine, self.cs.at[i, 0], self.cr.at[i, 0], self.sib)

    def along(self, ref, send, recv, target):
        self.sender.go(ref, ref, send, recv, target)

    def arrived(self, ref, send, recv):
        remote(ref, ref, send, recv, self.sib).wait_recv()

    def across(self, i, k, ref):
        self.sender.go(ref, ref, self.cs.at[i, k], self.cr.at[i, k], self.sib)

    def stage1(self, i):
        y, x, c, z = self.here
        out = self.out[i]
        pltpu.make_async_copy(self.own[i], out.at[y, x, c, z], self.local.at[i]).wait()
        for step in (1, 2, 3):
            self.arrived(out.at[y, x, c, (z + 4 - step) % 4], self.zs.at[i, step - 1], self.zr.at[i, step - 1])
        low, high = out.at[y, x, c, pl.ds(0, 2)], out.at[y, x, c, pl.ds(2, 2)]
        self.along(low, self.xs.at[i, 0], self.xr.at[i, 0], self.xn)
        self.along(high, self.ys.at[i, 0], self.yr.at[i, 0], self.yn)
        self.along(high, self.xs.at[i, 1], self.xr.at[i, 1], self.xn)
        self.along(low, self.ys.at[i, 1], self.yr.at[i, 1], self.yn)
        for step in (1, 2, 3):
            self.across(i, step, out.at[y, x, c, (z + 4 - step) % 4])

    def stage2(self, i):
        y, x, c, z = self.here
        low_x = self.out[i].at[y, 1 - x, c, pl.ds(0, 2)]
        high_y = self.out[i].at[1 - y, x, c, pl.ds(2, 2)]
        self.arrived(low_x, self.xs.at[i, 0], self.xr.at[i, 0])
        self.along(low_x, self.ys.at[i, 2], self.yr.at[i, 2], self.yn)
        self.arrived(high_y, self.ys.at[i, 0], self.yr.at[i, 0])
        self.along(high_y, self.xs.at[i, 2], self.xr.at[i, 2], self.xn)
        self.across(i, 4, low_x)
        self.across(i, 5, high_y)

    def stage3(self, i):
        y, x, c, z = self.here
        out = self.out[i]
        arrivals = (
            (out.at[y, 1 - x, c, pl.ds(2, 2)], self.xs.at[i, 1], self.xr.at[i, 1]),
            (out.at[1 - y, x, c, pl.ds(0, 2)], self.ys.at[i, 1], self.yr.at[i, 1]),
            (out.at[1 - y, 1 - x, c, pl.ds(2, 2)], self.xs.at[i, 2], self.xr.at[i, 2]),
            (out.at[1 - y, 1 - x, c, pl.ds(0, 2)], self.ys.at[i, 2], self.yr.at[i, 2]),
        )
        for k, (ref, send, recv) in enumerate(arrivals):
            self.arrived(ref, send, recv)
            self.across(i, 6 + k, ref)

    def finish(self, i):
        y, x, c, z = self.here
        o = 1 - c
        out = self.out[i]
        arrivals = [out.at[y, x, o, (z + 4 - step) % 4] for step in (0, 1, 2, 3)]
        arrivals += [
            out.at[y, 1 - x, o, pl.ds(0, 2)],
            out.at[1 - y, x, o, pl.ds(2, 2)],
            out.at[y, 1 - x, o, pl.ds(2, 2)],
            out.at[1 - y, x, o, pl.ds(0, 2)],
            out.at[1 - y, 1 - x, o, pl.ds(2, 2)],
            out.at[1 - y, 1 - x, o, pl.ds(0, 2)],
        ]
        for k, ref in enumerate(arrivals):
            self.arrived(ref, self.cs.at[i, k], self.cr.at[i, k])


class Names:
    def __init__(self, names, refs):
        for name, ref in zip(names, refs, strict=True):
            setattr(self, name, ref)


def rows_of(item, step, size):
    return pl.ds(pl.multiple_of(item * TOKENS + step * size, size), size)


def lane_cols(start, size=128):
    return pl.ds(pl.multiple_of(start, 128), size)


def dot_t(a, b):
    return lax.dot_general(a, b, (((1,), (1,)), ((), ())), preferred_element_type=F32)


def t_dot(a, b):
    return lax.dot_general(a, b, (((0,), (0,)), ((), ())), preferred_element_type=F32)


def weight_block(ref, start, size):
    cols = ref[:, :, :, :, :, pl.ds(start, size)]
    return cols.reshape(-1, size)


def two_heads(x, scale):
    lane = lax.broadcasted_iota(jnp.int32, x.shape, 1)
    x = x * jnp.asarray(scale, x.dtype)
    zero = jnp.zeros_like(x)
    return jnp.concatenate([jnp.where(lane < HD, x, zero), jnp.where(lane >= HD, x, zero)], axis=0)


def pick_heads(first, second):
    lane = lax.broadcasted_iota(jnp.int32, first.shape, 1)
    return jnp.where(lane < HD, first, second)


def norm_rows(v):
    centre = v - jnp.mean(v, axis=-1, keepdims=True)
    inverse = lax.rsqrt(jnp.mean(centre * centre, axis=-1, keepdims=True) + EPS)
    return centre * inverse, inverse


CHUNK = 32
PAIRS = HEADS // 2
TENSORS = ("qs", "ps", "qt", "pt", "up", "down")
SETS = ("n", "r", "h", "q", "p", "c", "a")


def save_shapes(tokens):
    rows = 2 * tokens
    attention = {
        "n": ((rows, D), BF16), "r": ((rows, 1), F32), "h": ((rows, D), BF16),
        "q": ((rows, 3 * D), BF16), "p": ((rows, 2 * PAIRS * tokens), BF16),
        "c": ((rows, D), BF16), "a": ((rows, D), BF16),
    }
    out = {}
    for k in (1, 2):
        out.update({name + str(k): spec for name, spec in attention.items()})
    out.update({
        "n3": ((rows, D), BF16), "r3": ((rows, 1), F32), "h3": ((rows, D), BF16),
        "g": ((rows, FF), BF16), "gp": ((rows, FF), BF16), "mods": ((9, 8, D), F32),
    })
    return out


def norm_into(s, k, shift, scale, rows, item, v):
    n, r = norm_rows(v)
    getattr(s, "n" + k)[rows, :] = n.astype(BF16)
    getattr(s, "r" + k)[rows, :] = r
    h = n * (1.0 + s.mods[scale, item : item + 1, :]) + s.mods[shift, item : item + 1, :]
    getattr(s, "h" + k)[rows, :] = h.astype(BF16)


def project(s, k, weight):
    h, q = getattr(s, "h" + k), getattr(s, "q" + k)
    for j in range(3):
        q[:, j * D : (j + 1) * D] = dot(h[...], weight_block(weight, j * D, D)).astype(BF16)


def attend(s, k, bias_of, first, last):
    q, p, c = getattr(s, "q" + k), getattr(s, "p" + k), getattr(s, "c" + k)

    def body(step, _):
        item, pair = step // PAIRS, step % PAIRS
        rows = pl.ds(pl.multiple_of(item * TOKENS, TOKENS), TOKENS)
        at = [lane_cols(pair * 128 + j * D) for j in range(3)]
        scores = dot_t(two_heads(q[rows, at[0]], HD ** (-0.5)), q[rows, at[1]])
        scores = (scores.reshape(2, TOKENS, TOKENS) + bias_of(item)).reshape(2 * TOKENS, TOKENS)
        expanded = jnp.exp(scores - jnp.max(scores, axis=-1, keepdims=True))
        soft = (expanded * (1.0 / jnp.sum(expanded, axis=-1, keepdims=True))).astype(BF16)
        p[:, lane_cols(step * TOKENS, TOKENS)] = soft
        context = dot(soft, q[rows, at[2]])
        c[rows, at[0]] = pick_heads(context[:TOKENS], context[TOKENS:]).astype(BF16)
        return 0

    lax.fori_loop(first, last, body, 0)


def after_attention(s, k, next_k, weight, gate, shift, scale):
    s.acc[...] = dot(getattr(s, "c" + k)[...], weight_block(weight, 0, D))
    for item in range(2):
        def body(t, _):
            rows = rows_of(item, t, CHUNK)
            a = s.acc[rows, :]
            v = s.x[rows, :] + s.mods[gate, item : item + 1, :] * a
            s.x[rows, :] = v
            getattr(s, "a" + k)[rows, :] = a.astype(BF16)
            norm_into(s, next_k, shift, scale, rows, item, v)
            return 0

        lax.fori_loop(0, TOKENS // CHUNK, body, 0)


def flat_bias(s):
    s.bias[...] = jnp.zeros_like(s.bias)
    for d in range(DEVICES):
        y, x, c, z = d // 16, (d // 8) % 2, (d // 4) % 2, d % 4
        piece = s.small_all[y, x, c, z].astype(F32)[2:3, :512]
        lane = lax.broadcasted_iota(jnp.int32, piece.shape, 1)
        piece = jnp.where(lane < SHARE, piece, 0.0)
        start = d * SHARE
        if start % 128:
            piece = pltpu.roll(piece, start % 128, 1)
        low = start // 128 * 128
        s.bias[:, low : low + 512] = s.bias[:, low : low + 512] + piece


def forward_kernel(names, *refs):
    s = Names(names, refs)
    here = place()
    y, x, c, z = here
    me = ((y * 2 + x) * 2 + c) * 4 + z
    sender = Sender()
    weights = [getattr(s, "w_" + t) for t in TENSORS]
    own = [getattr(s, "own_" + t) for t in TENSORS]
    gather = Gather(here, sender, own, weights, [getattr(s, f"gs{i}") for i in range(8)], s.gs8)
    little = Gather(here, sender, [s.small], [s.small_all], [getattr(s, f"ls{i}") for i in range(8)], s.ls8)
    saves = []

    def save(*names):
        for name in names:
            copy = pltpu.make_async_copy(getattr(s, name), getattr(s, "out_" + name), s.save_sem.at[len(saves)])
            copy.start()
            saves.append(copy)

    def target(k):
        d = (me + k) % DEVICES
        return d, {"wide": d // 4, "narrow": d % 4}

    barrier = pltpu.get_barrier_semaphore()

    def signal(k, _):
        pl.semaphore_signal(barrier, inc=1, device_id=target(k)[1], device_id_type=MESH)
        return 0

    lax.fori_loop(1, DEVICES, signal, 0)
    pl.semaphore_wait(barrier, DEVICES - 1)

    def columns_copy(k):
        d, there = target(k)
        src = s.ada.at[:, lane_cols(d * 256, 256)]
        return d, remote(src, s.ada_cols.at[me], s.a_send.at[k], s.a_recv.at[me], there)

    little.start(0)

    def send_columns(k, _):
        d, copy = columns_copy(k)

        @pl.when(d < OWNERS)
        def _():
            copy.start()

        return 0

    lax.fori_loop(1, DEVICES, send_columns, 0)
    owner = me < OWNERS
    mine = jnp.minimum(me, OWNERS - 1)
    own_columns = pltpu.make_async_copy(s.ada.at[:, lane_cols(mine * 256, 256)], s.ada_cols.at[me], s.own_sem.at[0])
    own_columns.start()
    gather.start(0)
    gather.start(1)

    place_of = lambda n: lax.broadcasted_iota(jnp.int32, (TOKENS, TOKENS), n)
    same_frame = place_of(0) // SPATIAL == place_of(1) // SPATIAL
    same_place = place_of(0) % SPATIAL == place_of(1) % SPATIAL
    for item in range(2):
        s.space_bias[item] = jnp.where(same_frame, s.keys[item : item + 1, :], MASKED)
    s.time_bias[...] = jnp.where(same_place, 0.0, MASKED)

    little.stage1(0)
    little.stage2(0)
    little.stage3(0)
    little.finish(0)
    flat_bias(s)
    own_columns.wait()

    def modulation_copy(k):
        d, there = target(k)
        src = s.mod_cols.at[pl.ds(pl.multiple_of(d * 8, 8), 8)]
        return remote(src, s.mod_all.at[me], s.m_send.at[k], s.m_recv.at[me], there)

    own_mod = pltpu.make_async_copy(
        s.mod_cols.at[pl.ds(pl.multiple_of(me * 8, 8), 8)], s.mod_all.at[mine], s.own_sem.at[1]
    )

    conditions = s.small_all[...].reshape(DEVICES * 8, D)
    part = D // DEVICES
    spot = lambda shape, n: lax.broadcasted_iota(jnp.int32, shape, n)
    col = spot((D, 128), 1)
    wanted = (spot((D, 128), 0) == me * part + col) & (col < part)
    mine_only = dot(conditions, wanted.astype(F32).astype(BF16)).astype(BF16)
    row, item = spot((D, DEVICES * 8), 0), spot((D, DEVICES * 8), 1)
    slot = row % part
    copy_of = (row // part == item // 8) & (slot // 9 == item % 8) & (slot < 18)
    s.chosen[...] = dot(copy_of.astype(F32).astype(BF16), mine_only).astype(BF16)

    @pl.when(owner)
    def _():
        def wait_columns(k, _):
            d, there = target(k)
            remote(s.ada_cols.at[d], s.ada_cols.at[d], s.a_send.at[k], s.a_recv.at[d], there).wait_recv()
            return 0

        lax.fori_loop(1, DEVICES, wait_columns, 0)
        s.mod_cols[...] = dot(conditions, s.ada_cols[...].reshape(D, 256))

        def send_modulation(k, _):
            modulation_copy(k).start()
            return 0

        lax.fori_loop(1, DEVICES, send_modulation, 0)
        own_mod.start()

    gather.start(2)
    gather.stage1(0)
    gather.start(3)
    gather.stage1(1)
    gather.stage2(0)

    @pl.when(owner)
    def _():
        own_mod.wait()

    def wait_modulation(k, _):
        d, there = target(k)

        @pl.when(d < OWNERS)
        def _():
            remote(s.mod_all.at[d], s.mod_all.at[d], s.m_send.at[k], s.m_recv.at[d], there).wait_recv()

        return 0

    lax.fori_loop(1, DEVICES, wait_modulation, 0)
    for j in range(9):
        row = jnp.concatenate([s.mod_all[3 * j + i] for i in range(3)], axis=1)
        s.mods[j] = row + s.bias[:, j * D : (j + 1) * D]
    save("mods")

    for item in range(2):
        def first(t, _):
            rows = rows_of(item, t, CHUNK)
            v = s.latents[rows, :].astype(F32)
            s.x[rows, :] = v
            norm_into(s, "1", 0, 1, rows, item, v)
            return 0

        lax.fori_loop(0, TOKENS // CHUNK, first, 0)
    save("n1", "r1", "h1")

    def ready(i):
        gather.finish(i)
        save("w_" + TENSORS[i])

    gather.stage2(1)
    gather.start(4)
    gather.stage1(2)
    gather.stage3(0)
    ready(0)
    project(s, "1", s.w_qs)
    gather.stage3(1)
    gather.start(5)
    gather.stage1(3)
    gather.stage2(2)
    space = lambda item: s.space_bias[item]
    attend(s, "1", space, 0, 3)
    gather.stage2(3)
    attend(s, "1", space, 3, 6)
    gather.stage1(4)
    attend(s, "1", space, 6, 9)
    gather.stage3(2)
    attend(s, "1", space, 9, 12)
    gather.stage3(3)
    ready(1)
    after_attention(s, "1", "2", s.w_ps, 2, 3, 4)
    save("q1", "p1", "c1", "a1", "n2", "r2", "h2")
    ready(2)
    gather.stage2(4)
    project(s, "2", s.w_qt)
    gather.stage1(5)
    time = lambda item: s.time_bias[...]
    attend(s, "2", time, 0, 3)
    gather.stage3(4)
    attend(s, "2", time, 3, 6)
    gather.stage2(5)
    attend(s, "2", time, 6, 12)
    ready(3)
    after_attention(s, "2", "3", s.w_pt, 5, 6, 7)
    save("q2", "p2", "c2", "a2", "n3", "r3", "h3")
    ready(4)
    for j in range(FF // D):
        s.acc[...] = dot(s.h3[...], weight_block(s.w_up, j * D, D))
        b_up = s.bias[:, (9 + j) * D : (10 + j) * D]

        def activate(t, _):
            rows = rows_of(0, t, CHUNK)
            u = s.acc[rows, :] + b_up
            square = u * u
            th = jnp.tanh(u * (GELU + (GELU * 0.044715) * square))
            half = 0.5 * u
            s.g[rows, j * D : (j + 1) * D] = (half + half * th).astype(BF16)
            slope = 0.5 + 0.5 * th + half * (1.0 - th * th) * (GELU + (3 * GELU * 0.044715) * square)
            s.gp[rows, j * D : (j + 1) * D] = slope.astype(BF16)
            return 0

        lax.fori_loop(0, 2 * TOKENS // CHUNK, activate, 0)
        if j == 1:
            gather.stage3(5)
    save("g", "gp")
    ready(5)
    for j in range(FF // D):
        w = s.w_down[j // 2, j % 2].reshape(D, D)
        part = dot(s.g[:, j * D : (j + 1) * D], w)
        s.acc[...] = part if j == 0 else s.acc[...] + part
    b_down = s.bias[:, (9 + FF // D) * D : (10 + FF // D) * D]
    for item in range(2):
        gate = s.mods[8, item : item + 1, :]

        def last(t, total):
            rows = rows_of(item, t, CHUNK)
            m = s.acc[rows, :] + b_down
            valid = s.valid[rows, :]
            s.output[rows, :] = ((s.x[rows, :] + gate * m) * valid).astype(BF16)
            d3 = s.cotangent[rows, :].astype(F32) * valid
            return total + jnp.sum((d3 * m).reshape(CHUNK // 8, 8, D), axis=0)

        total = lax.fori_loop(0, TOKENS // CHUNK, last, jnp.zeros((8, D), F32))
        s.dga3[item : item + 1, :] = jnp.sum(total, axis=0, keepdims=True)

    def drain(k, _):
        d, copy = columns_copy(k)

        @pl.when(d < OWNERS)
        def _():
            copy.wait_send()

        @pl.when(owner)
        def _():
            modulation_copy(k).wait_send()

        return 0

    lax.fori_loop(1, DEVICES, drain, 0)
    sender.drain()
    for copy in saves:
        copy.wait()


def run_forward(small, ada, shards, latents, cotangent, keys, valid):
    vmem, any_space = pl.BlockSpec(memory_space=pltpu.VMEM), pl.BlockSpec(memory_space=pl.ANY)
    saved = save_shapes(TOKENS)
    weights = {"w_" + t: ((2, 2, 2, 4) + sh.shape, BF16) for t, sh in zip(TENSORS, shards)}
    kept = {**saved, **weights}
    rows = 2 * TOKENS
    ins = ["small", "ada"] + ["own_" + t for t in TENSORS] + ["latents", "cotangent", "keys", "valid"]
    outs = ["output", "dga3", "chosen"] + ["out_" + name for name in kept]
    dma = pltpu.SemaphoreType.DMA
    scratch = {name: pltpu.VMEM(*spec) for name, spec in kept.items()}
    scratch |= {
        "small_all": pltpu.VMEM((2, 2, 2, 4) + small.shape, BF16),
        "ada_cols": pltpu.VMEM((DEVICES, ada.shape[0], 256), BF16),
        "mod_cols": pltpu.VMEM((DEVICES * 8, 256), F32),
        "mod_all": pltpu.VMEM((OWNERS, 8, 256), F32),
        "bias": pltpu.VMEM((1, DEVICES * SHARE + 512), F32),
        "x": pltpu.VMEM((rows, D), F32),
        "acc": pltpu.VMEM((rows, D), F32),
        "space_bias": pltpu.VMEM((2, TOKENS, TOKENS), F32),
        "time_bias": pltpu.VMEM((TOKENS, TOKENS), F32),
        "save_sem": dma((len(kept),)),
        "a_send": dma((DEVICES,)), "a_recv": dma((DEVICES,)),
        "m_send": dma((DEVICES,)), "m_recv": dma((DEVICES,)), "own_sem": dma((2,)),
    }
    scratch |= {f"gs{i}": kind for i, kind in enumerate(Gather.scratch(len(shards)))}
    scratch |= {f"ls{i}": kind for i, kind in enumerate(Gather.scratch(1))}
    names = ins + outs + list(scratch)
    results = pl.pallas_call(
        lambda *refs: forward_kernel(names, *refs),
        out_shape=(jax.ShapeDtypeStruct((rows, D), BF16), jax.ShapeDtypeStruct((2, D), F32), jax.ShapeDtypeStruct((D, 128), BF16))
        + tuple(jax.ShapeDtypeStruct(*spec) for spec in kept.values()),
        in_specs=[vmem] * len(ins),
        out_specs=(vmem,) * 3 + (any_space,) * len(kept),
        scratch_shapes=list(scratch.values()),
        compiler_params=pltpu.CompilerParams(
            collective_id=1, has_side_effects=True, vmem_limit_bytes=VMEM_LIMIT
        ),
        name="forward",
    )(small, ada, *shards, latents, cotangent, keys, valid)
    return results[0], results[1], results[2], dict(zip(kept, results[3:]))


class Scatter:
    SEMAPHORES = ((), (), (2,), (2,), (2,), (2,), (3,), (3,))
    LEADING = ((2, 2, 4), (2, 2), (2, 2), (2,), (2,), (3,))

    def __init__(self, here, part, out, buffers, semaphores):
        self.here, self.part, self.out = here, part, out
        self.r0, self.r1a, self.r1b, self.r2a, self.r2b, self.r3 = buffers
        self.cs, self.cr, self.s1, self.v1, self.s2, self.v2, self.s3, self.v3 = semaphores
        y, x, c, z = here
        self.sib = device_at(y, x, 1 - c, z)
        self.xn = device_at(y, 1 - x, c, z)
        self.yn = device_at(1 - y, x, c, z)
        self.copies = [[] for _ in part]

    def hop(self, i, stage, k):
        y, x, c, z = self.here
        part = self.part[i]
        if stage == 0:
            return (part.at[:, :, 1 - c], self.r0[i], self.cs.at[i], self.cr.at[i], self.sib)
        if stage == 1:
            if k == 0:
                return (part.at[1 - y, :, c, pl.ds(0, 2)], self.r1a[i], self.s1.at[i, 0], self.v1.at[i, 0], self.yn)
            return (part.at[:, 1 - x, c, pl.ds(2, 2)], self.r1b[i], self.s1.at[i, 1], self.v1.at[i, 1], self.xn)
        if stage == 2:
            if k == 0:
                return (part.at[y, 1 - x, c, pl.ds(0, 2)], self.r2a[i], self.s2.at[i, 0], self.v2.at[i, 0], self.xn)
            return (part.at[1 - y, x, c, pl.ds(2, 2)], self.r2b[i], self.s2.at[i, 1], self.v2.at[i, 1], self.yn)
        there = (z + k + 1) % 4
        return (part.at[y, x, c, there], self.r3[i].at[k], self.s3.at[i, k], self.v3.at[i, k], device_at(y, x, c, there))

    def send(self, i, stage, k):
        copy = remote(*self.hop(i, stage, k))
        copy.start()
        self.copies[i].append(copy)

    def wait(self, i, stage, k):
        remote(*self.hop(i, stage, k)).wait_recv()

    def drain(self, i):
        for copy in self.copies[i]:
            copy.wait_send()
        self.copies[i] = []

    def start(self, i):
        self.send(i, 0, 0)

    def stage1(self, i):
        c = self.here[2]
        part, r0 = self.part[i], self.r0[i]
        self.wait(i, 0, 0)

        def add(k, _):
            a, b, q = k // 8, (k // 4) % 2, k % 4
            part[a, b, c, q] = part[a, b, c, q] + r0[a, b, q]
            return 0

        lax.fori_loop(0, 16, add, 0)
        self.send(i, 1, 0)
        self.send(i, 1, 1)

    def stage2(self, i):
        y, x, c, z = self.here
        part, r1a, r1b = self.part[i], self.r1a[i], self.r1b[i]
        self.wait(i, 1, 0)
        self.wait(i, 1, 1)

        def add(k, _):
            a, q = k // 2, k % 2
            part[y, a, c, q] = part[y, a, c, q] + r1a[a, q]
            part[a, x, c, q + 2] = part[a, x, c, q + 2] + r1b[a, q]
            return 0

        lax.fori_loop(0, 4, add, 0)
        self.send(i, 2, 0)
        self.send(i, 2, 1)

    def stage3(self, i):
        y, x, c, z = self.here
        part = self.part[i]
        self.wait(i, 2, 0)
        self.wait(i, 2, 1)
        for q in range(2):
            part[y, x, c, q] = part[y, x, c, q] + self.r2a[i][q]
            part[y, x, c, q + 2] = part[y, x, c, q + 2] + self.r2b[i][q]
        for k in (1, 0, 2):
            self.send(i, 3, k)

    def stage4(self, i):
        y, x, c, z = self.here
        for k in range(3):
            self.wait(i, 3, k)
        part, r3 = self.part[i], self.r3[i]
        flatten_into(
            self.out[i],
            (part[y, x, c, z].astype(F32) + r3[0].astype(F32)) + (r3[1].astype(F32) + r3[2].astype(F32)),
            0,
            part.shape[-1] // 128,
        )


def flatten_into(out, value, start, stride):
    rows, size = value.shape
    for k in range(size // 128):
        out[pl.ds(start + k, rows, stride=stride), :] = value[:, k * 128 : (k + 1) * 128]


GRADS = ("down", "up", "pt", "qt", "ps", "qs")
WIDTHS = {"down": D, "up": FF, "pt": D, "qt": 3 * D, "ps": D, "qs": 3 * D}
BLOCKS = [("down", j) for j in range(4)] + [("up", j) for j in range(4)]
BLOCKS += [("pt", 0)] + [("qt", j) for j in range(3)] + [("ps", 0)] + [("qs", j) for j in range(3)]
SLOTS = 4


def attend_back(s, q, p, c_grad, first, last):
    def body(step, _):
        item, pair = step // PAIRS, step % PAIRS
        rows = pl.ds(pl.multiple_of(item * TOKENS, TOKENS), TOKENS)
        at = [lane_cols(pair * 128 + j * D) for j in range(3)]
        soft = p[:, lane_cols(step * TOKENS, TOKENS)]
        dc = c_grad[rows, at[0]]
        queries, keys, values = (q[rows, where] for where in at)
        v_grad = pick_heads(t_dot(soft[:TOKENS], dc), t_dot(soft[TOKENS:], dc))
        soft_grad = dot_t(two_heads(dc, 1.0), values)
        wide = soft.astype(F32)
        product = soft_grad * wide
        score = (product - wide * jnp.sum(product, axis=-1, keepdims=True)).astype(BF16)
        q_both = dot(score, keys)
        q_grad = pick_heads(q_both[:TOKENS], q_both[TOKENS:]) * HD ** (-0.5)
        k_grad = pick_heads(t_dot(score[:TOKENS], queries), t_dot(score[TOKENS:], queries)) * HD ** (-0.5)
        q[rows, at[0]] = q_grad.astype(BF16)
        q[rows, at[1]] = k_grad.astype(BF16)
        q[rows, at[2]] = v_grad.astype(BF16)
        return 0

    lax.fori_loop(first, last, body, 0)


def backward_kernel(names, *refs):
    s = Names(names, refs)
    here = place()
    y, x, c, z = here
    me = ((y * 2 + x) * 2 + c) * 4 + z
    loads = {}

    def fetch(name, src, dst, k):
        loads[name] = pltpu.make_async_copy(src, dst, s.load_sem.at[k])
        loads[name].start()

    def have(*wanted):
        for name in wanted:
            loads.pop(name).wait()

    def fetch_block(k):
        tensor, j = BLOCKS[k]
        src = getattr(s, "w_" + tensor)
        src = src.at[j] if tensor == "down" else src.at[:, :, pl.ds(j * D, D)]
        fetch(("w", k), src, s.blocks.at[k % SLOTS], 16 + k % SLOTS)

    def block(k):
        have(("w", k))
        return s.blocks[k % SLOTS].reshape(D, D)

    def used(k):
        if k + SLOTS < len(BLOCKS):
            fetch_block(k + SLOTS)

    fetch("g", s.in_g, s.g, 0)
    fetch("mods", s.in_mods, s.mods, 1)
    fetch_block(0)
    fetch_block(1)
    fetch("gp", s.in_gp, s.gp, 2)
    fetch("h3", s.in_h3, s.h3, 3)
    fetch_block(2)
    fetch_block(3)
    fetch("n3", s.in_n3, s.n3, 4)
    fetch("r3", s.in_r3, s.r3, 5)

    def fetch_rest(k):
        for i, (name, dst) in enumerate((("a", s.a), ("c", s.c), ("h", s.h), ("n", s.n), ("r", s.r))):
            fetch(name, getattr(s, f"in_{name}{k}"), dst, 6 + i)

    fetch_rest(2)

    parts = [s.b0, s.b1]
    parts += [s.b2.at[:, :, :, :, :, pl.ds(0, D)], s.b2.at[:, :, :, :, :, pl.ds(D, 3 * D)]]
    parts += [s.b3, s.b1.at[:, :, :, :, :, pl.ds(0, 3 * D)]]
    outs = [getattr(s, "grad_" + t) for t in GRADS]
    buffers = [[getattr(s, f"r{k}_{t}") for t in GRADS] for k in range(6)]
    scatter = Scatter(here, parts, outs, buffers, [getattr(s, f"ss{k}") for k in range(8)])
    sender = Sender()
    little = Gather(here, sender, [s.small], [s.small_all], [getattr(s, f"ls{i}") for i in range(8)], s.ls8)

    barrier = pltpu.get_barrier_semaphore()
    partners = [device_at(y, x, 1 - c, z), device_at(y, 1 - x, c, z), device_at(1 - y, x, c, z)]
    partners += [device_at(y, x, c, (z + step) % 4) for step in (1, 2, 3)]
    for partner in partners:
        pl.semaphore_signal(barrier, inc=1, device_id=partner, device_id_type=MESH)
    pl.semaphore_wait(barrier, 6)

    s.rows[...] = jnp.zeros_like(s.rows)
    ones = jnp.ones((8, 2 * TOKENS), BF16)
    have("mods")
    for item in range(2):
        gate = s.mods[8, item : item + 1, :]

        def first(t, _):
            rows = rows_of(item, t, CHUNK)
            d3 = s.cotangent[rows, :].astype(F32) * s.valid[rows, :]
            s.d[rows, :] = d3
            s.dm[rows, :] = (gate * d3).astype(BF16)
            return 0

        lax.fori_loop(0, TOKENS // CHUNK, first, 0)
        s.rows[9 * item + 8 : 9 * item + 9, :] = s.dga3[item : item + 1, :]
    s.rows[22:23, :] = dot(ones, s.dm[...])[:1]

    have("g")
    for j in range(4):
        grad = t_dot(s.g[:, j * D : (j + 1) * D], s.dm[...]).astype(BF16)
        s.b0[j // 2, j % 2] = grad.reshape(2, 4, 4 * D // DEVICES, D)
    scatter.start(0)
    fetch("p", s.in_p2, s.g, 0)

    have("gp", "h3")
    for j in range(4):
        cols = slice(j * D, (j + 1) * D)
        s.acc[...] = dot_t(s.dm[...], block(j))
        used(j)

        def slope(t, _):
            rows = rows_of(0, t, CHUNK)
            s.gp[rows, cols] = (s.acc[rows, :] * s.gp[rows, cols].astype(F32)).astype(BF16)
            return 0

        lax.fori_loop(0, 2 * TOKENS // CHUNK, slope, 0)
        s.rows[18 + j : 19 + j, :] = dot(ones, s.gp[:, cols])[:1]
        if j == 1:
            scatter.stage1(0)
    for j in range(4):
        cols = slice(j * D, (j + 1) * D)
        grad = t_dot(s.h3[...], s.gp[:, cols]).astype(BF16)
        s.b1[:, :, :, :, :, cols] = grad.reshape(2, 2, 2, 4, D // DEVICES, D)
    scatter.start(1)

    def back_through(first_block, source, count):
        for j in range(count):
            part = dot_t(source[:, j * D : (j + 1) * D], block(first_block + j))
            used(first_block + j)
            s.acc[...] = part if j == 0 else s.acc[...] + part

    back_through(4, s.gp, 4)
    fetch("q", s.in_q2, s.gp.at[:, pl.ds(0, 3 * D)], 2)
    scatter.stage1(1)

    def norm_back(n_ref, r_ref, base, a_ref, gate_row):
        for item in range(2):
            scale = 1.0 + s.mods[base + 1, item : item + 1, :]
            gate = None if gate_row is None else s.mods[gate_row, item : item + 1, :]

            def body(t, totals):
                rows = rows_of(item, t, CHUNK)
                dh, n = s.acc[rows, :], n_ref[rows, :].astype(F32)
                g = dh * scale
                dhn = dh * n
                mean_g = jnp.mean(g, axis=-1, keepdims=True)
                mean_gn = jnp.mean(g * n, axis=-1, keepdims=True)
                d = s.d[rows, :] + r_ref[rows, :] * (g - mean_g - n * mean_gn)
                s.d[rows, :] = d
                fold = lambda v: jnp.sum(v.reshape(CHUNK // 8, 8, D), axis=0)
                new = [totals[0] + fold(dh), totals[1] + fold(dhn)]
                if gate is not None:
                    s.dm[rows, :] = (gate * d).astype(BF16)
                    new.append(totals[2] + fold(d * a_ref[rows, :].astype(F32)))
                return tuple(new)

            count = 2 if gate is None else 3
            totals = lax.fori_loop(0, TOKENS // CHUNK, body, (jnp.zeros((8, D), F32),) * count)
            for where, total in zip((base, base + 1, base - 1), totals):
                row = 9 * item + where
                s.rows[row : row + 1, :] = jnp.sum(total, axis=0, keepdims=True)

    have("n3", "r3", "a")
    norm_back(s.n3, s.r3, 6, s.a, 5)
    have("c")
    s.b2[:, :, :, :, :, :D] = t_dot(s.c[...], s.dm[...]).astype(BF16).reshape(2, 2, 2, 4, D // DEVICES, D)
    scatter.start(2)
    s.dc[...] = dot_t(s.dm[...], block(8)).astype(BF16)
    used(8)
    scatter.stage2(0)
    have("q", "p")
    attend_back(s, s.gp, s.g, s.dc, 0, 4)
    scatter.stage1(2)
    attend_back(s, s.gp, s.g, s.dc, 4, 8)
    scatter.stage3(0)
    attend_back(s, s.gp, s.g, s.dc, 8, 12)
    fetch("p", s.in_p1, s.g, 0)
    have("h")
    for j in range(3):
        cols = slice(D + j * D, 2 * D + j * D)
        grad = t_dot(s.h[...], s.gp[:, j * D : (j + 1) * D]).astype(BF16)
        s.b2[:, :, :, :, :, cols] = grad.reshape(2, 2, 2, 4, D // DEVICES, D)
    scatter.start(3)
    scatter.stage2(1)
    back_through(9, s.gp, 3)
    scatter.stage2(2)
    scatter.stage1(3)
    fetch("q", s.in_q1, s.gp.at[:, pl.ds(0, 3 * D)], 2)
    have("n", "r")
    fetch("a", s.in_a1, s.a, 6)
    fetch("c", s.in_c1, s.c, 7)
    fetch("h", s.in_h1, s.h, 8)
    have("a")
    norm_back(s.n, s.r, 3, s.a, 2)
    fetch("n", s.in_n1, s.n, 9)
    fetch("r", s.in_r1, s.r, 10)
    scatter.stage3(1)
    have("c")
    s.b3[...] = t_dot(s.c[...], s.dm[...]).astype(BF16).reshape(2, 2, 2, 4, D // DEVICES, D)
    scatter.start(4)
    s.dc[...] = dot_t(s.dm[...], block(12)).astype(BF16)
    used(12)
    scatter.stage4(0)
    scatter.stage3(2)
    have("q", "p")
    attend_back(s, s.gp, s.g, s.dc, 0, 4)
    scatter.stage1(4)
    scatter.stage2(3)
    attend_back(s, s.gp, s.g, s.dc, 4, 8)
    scatter.stage4(1)
    attend_back(s, s.gp, s.g, s.dc, 8, 12)
    scatter.stage4(2)
    scatter.stage3(3)
    scatter.drain(1)
    have("h")
    for j in range(3):
        cols = slice(j * D, (j + 1) * D)
        grad = t_dot(s.h[...], s.gp[:, cols]).astype(BF16)
        s.b1[:, :, :, :, :, cols] = grad.reshape(2, 2, 2, 4, D // DEVICES, D)
    scatter.start(5)
    scatter.stage2(4)
    back_through(13, s.gp, 3)
    scatter.stage1(5)
    have("n", "r")
    norm_back(s.n, s.r, 0, None, None)
    s.small[...] = s.rows[...].astype(BF16)
    little.start(0)
    scatter.stage3(4)
    little.stage1(0)
    scatter.stage4(3)
    little.stage2(0)
    scatter.stage4(4)
    little.stage3(0)
    scatter.stage2(5)
    little.finish(0)

    gathered = s.small_all[...].reshape(D, D)
    slot = lax.broadcasted_iota(jnp.int32, (D, 128), 0) % (D // DEVICES)
    for j in range(9):
        chosen = jnp.where((slot == j) | (slot == j + 9), s.chosen[...], jnp.zeros((D, 128), BF16))
        grad = t_dot(chosen, gathered)[: D // DEVICES]
        flatten_into(s.grad_ada, grad, j * (D // 128), 9 * D // 128)
        if j == 5:
            scatter.stage3(5)
    row = lax.broadcasted_iota(jnp.int32, (16, D), 0)
    slot = lax.broadcasted_iota(jnp.int32, (16, D), 1) % (D // DEVICES)
    take = ((row < 9) & ((slot == row) | (slot == row + 9))) | ((row >= 9) & (slot == row + 9))
    s.grad_bias[...] = dot(take.astype(F32).astype(BF16), gathered)
    scatter.stage4(5)
    for i in range(len(GRADS)):
        scatter.drain(i)
    sender.drain()


def run_backward(cotangent, valid, dga3, chosen, kept):
    vmem, any_space = pl.BlockSpec(memory_space=pltpu.VMEM), pl.BlockSpec(memory_space=pl.ANY)
    rows, part = 2 * TOKENS, D // DEVICES
    ins = {"cotangent": cotangent, "valid": valid, "dga3": dga3, "chosen": chosen}
    fetched = {"in_" + name: kept[name] for name in save_shapes(TOKENS)}
    for t in GRADS:
        shape = (4, DEVICES, part, D) if t == "down" else (DEVICES, part, WIDTHS[t])
        fetched["w_" + t] = kept["w_" + t].reshape(shape)
    ins |= fetched
    block_of = {t: (4 * part, D) if t == "down" else (part, WIDTHS[t]) for t in GRADS}
    outs = {"grad_" + t: (DEVICES * part * WIDTHS[t] * (4 if t == "down" else 1) // DEVICES // 128, 128) for t in GRADS}
    outs |= {"grad_ada": (part * 9 * D // 128, 128), "grad_bias": (16, D), "d": (rows, D)}
    dma = pltpu.SemaphoreType.DMA
    big = lambda *block: pltpu.VMEM((2, 2, 2, 4) + block, BF16)
    scratch = {
        "b0": big(4 * part, D), "b1": big(part, FF), "b2": big(part, FF), "b3": big(part, D),
        "blocks": pltpu.VMEM((SLOTS, DEVICES, part, D), BF16),
        "g": pltpu.VMEM((rows, FF), BF16), "gp": pltpu.VMEM((rows, FF), BF16),
        "acc": pltpu.VMEM((rows, D), F32),
        "mods": pltpu.VMEM((9, 8, D), F32), "rows": pltpu.VMEM((24, D), F32),
        "small": pltpu.VMEM((24, D), BF16), "small_all": big(24, D),
        "r3": pltpu.VMEM((rows, 1), F32), "r": pltpu.VMEM((rows, 1), F32),
        "load_sem": dma((16 + SLOTS,)),
    }
    scratch |= {name: pltpu.VMEM((rows, D), BF16) for name in ("dm", "dc", "h3", "n3", "a", "c", "h", "n")}
    for k, lead in enumerate(Scatter.LEADING):
        scratch |= {f"r{k}_{t}": pltpu.VMEM(lead + block_of[t], BF16) for t in GRADS}
    scratch |= {f"ss{k}": dma((len(GRADS),) + extra) for k, extra in enumerate(Scatter.SEMAPHORES)}
    scratch |= {f"ls{i}": kind for i, kind in enumerate(Gather.scratch(1))}
    names = list(ins) + list(outs) + list(scratch)
    results = pl.pallas_call(
        lambda *refs: backward_kernel(names, *refs),
        out_shape=tuple(jax.ShapeDtypeStruct(shape, F32) for shape in outs.values()),
        in_specs=[vmem] * 4 + [any_space] * len(fetched),
        out_specs=(vmem,) * len(outs),
        scratch_shapes=list(scratch.values()),
        compiler_params=pltpu.CompilerParams(
            collective_id=2, has_side_effects=True, vmem_limit_bytes=VMEM_LIMIT
        ),
        name="backward",
    )(*ins.values())
    return dict(zip(outs, results))


def norm_parts(rows):
    centre = rows - jnp.mean(rows, axis=-1, keepdims=True)
    inverse = lax.rsqrt(jnp.mean(centre * centre, axis=-1, keepdims=True) + EPS)
    return centre * inverse, inverse


def norm_back(grad, normed, inverse, scale):
    shift_grad = jnp.sum(grad, axis=1)
    scale_grad = jnp.sum(grad * normed, axis=1)
    pulled = grad * (1.0 + scale)
    back = inverse * (
        pulled
        - jnp.mean(pulled, axis=-1, keepdims=True)
        - normed * jnp.mean(pulled * normed, axis=-1, keepdims=True)
    )
    return back, shift_grad, scale_grad


def heads(x):
    return x.reshape(x.shape[0], x.shape[1], HEADS, HD)


def attention(low, qkv_w, proj_w, mask):
    packed = dot(low, qkv_w).astype(BF16)
    q, k, v = (heads(part) for part in jnp.split(packed, 3, axis=-1))
    scores = jnp.einsum("bqhd,bkhd->bhqk", q, k, preferred_element_type=F32) * HD ** (-0.5)
    scores = jnp.where(mask, scores, MASKED)
    soft = jax.nn.softmax(scores, axis=-1)
    context = jnp.einsum("bhqk,bkhd->bqhd", soft.astype(BF16), v, preferred_element_type=F32)
    context = context.astype(BF16).reshape(low.shape)
    return dot(context, proj_w), (q, k, v, soft, context)


def attention_back(grad_low, low, qkv_w, proj_w, kept):
    q, k, v, soft, context = kept
    proj_grad = jnp.einsum("bld,ble->de", context, grad_low, preferred_element_type=F32)
    ctx = heads(jnp.einsum("ble,de->bld", grad_low, proj_w, preferred_element_type=F32).astype(BF16))
    v_grad = jnp.einsum("bhqk,bqhd->bkhd", soft.astype(BF16), ctx, preferred_element_type=F32)
    soft_grad = jnp.einsum("bqhd,bkhd->bhqk", ctx, v, preferred_element_type=F32)
    row_dot = jnp.sum(soft_grad * soft, axis=-1, keepdims=True)
    score_grad = (soft * (soft_grad - row_dot)).astype(BF16)
    q_grad = jnp.einsum("bhqk,bkhd->bqhd", score_grad, k, preferred_element_type=F32) * HD ** (-0.5)
    k_grad = jnp.einsum("bhqk,bqhd->bkhd", score_grad, q, preferred_element_type=F32) * HD ** (-0.5)
    packed = jnp.concatenate(
        [part.astype(BF16).reshape(low.shape) for part in (q_grad, k_grad, v_grad)], axis=-1
    )
    qkv_grad = jnp.einsum("bld,ble->de", low, packed, preferred_element_type=F32)
    low_grad = jnp.einsum("ble,de->bld", packed, qkv_w, preferred_element_type=F32)
    return low_grad, qkv_grad, proj_grad


def gather_plain(shards):
    return tuple(lax.all_gather(s, AXES, axis=0) for s in shards)


def scatter_plain(parts, small):
    devices = lax.axis_size(AXES)
    sums = tuple(
        lax.psum_scatter(p.reshape((devices,) + p.shape[-2:]), AXES, scatter_dimension=0, tiled=True)[
            0
        ].astype(F32)
        for p in parts
    )
    return sums + (lax.all_gather(small, AXES, axis=0),)


def per_device_plain(latents, buckets, step_ids, qs, ps, qt, pt, up, down, ada, biases, cotangent):
    devices = lax.axis_size(AXES)
    micro = latents.shape[0]
    frames, spatial = latents.shape[2], latents.shape[3]
    tokens = frames * spatial
    rows = D // devices

    gather, scatter = gather_plain, scatter_plain

    ada_columns = lax.all_to_all(
        ada.reshape(rows, 9 * D), AXES, split_axis=1, concat_axis=0, tiled=True
    )
    own_bias = jnp.pad(biases, (0, D - biases.shape[0]))[None]
    small = jnp.concatenate([timestep_condition(step_ids[:, 0]), own_bias], axis=0)
    shards = [small] + [w.reshape(rows, -1) for w in (qs, ps, qt, pt, up)] + [down.reshape(-1, D)]
    small, *gathered = gather(shards)
    w_qs, w_ps, w_qt, w_pt, w_up = (w.reshape(D, -1) for w in gathered[:5])
    w_down = gathered[5].reshape(-1, D)
    small = small.reshape(devices, micro + 1, D)
    condition = small[:, :micro].reshape(devices * micro, D)
    bias = small[:, micro, : biases.shape[0]].reshape(-1).astype(F32)
    modulation = lax.all_to_all(
        dot(condition, ada_columns), AXES, split_axis=0, concat_axis=1, tiled=True
    )
    modulation = (modulation + bias[: 9 * D]).reshape(micro, 9, 1, D)
    b_up, b_down = bias[9 * D : 9 * D + FF], bias[9 * D + FF :]

    positions = jnp.arange(tokens)
    frame, place = positions // spatial, positions % spatial
    bucket = buckets[:, 0]
    length = jnp.where(bucket == 0, spatial, jnp.where(bucket == 1, spatial // 2, spatial // 8))
    valid = place[None, :] < length[:, None]
    space_mask = (frame[:, None] == frame[None, :])[None, None] & valid[:, None, None, :]
    time_mask = (place[:, None] == place[None, :])[None, None]
    valid_rows = valid.astype(F32)[:, :, None]

    sh1, sc1, ga1, sh2, sc2, ga2, sh3, sc3, ga3 = (modulation[:, i] for i in range(9))
    x = latents.reshape(micro, tokens, D).astype(F32)
    n1, r1 = norm_parts(x)
    h1 = (n1 * (1.0 + sc1) + sh1).astype(BF16)
    a1, kept1 = attention(h1, w_qs, w_ps, space_mask)
    x1 = x + ga1 * a1
    n2, r2 = norm_parts(x1)
    h2 = (n2 * (1.0 + sc2) + sh2).astype(BF16)
    a2, kept2 = attention(h2, w_qt, w_pt, time_mask)
    x2 = x1 + ga2 * a2
    n3, r3 = norm_parts(x2)
    h3 = (n3 * (1.0 + sc3) + sh3).astype(BF16)
    hidden = dot(h3, w_up) + b_up
    gelu, pull = jax.vjp(lambda u: jax.nn.gelu(u, approximate=True), hidden)
    g = gelu.astype(BF16)
    m = dot(g, w_down) + b_down
    x3 = x2 + ga3 * m
    output = (x3 * valid_rows).astype(BF16)

    d3 = cotangent.reshape(micro, tokens, D).astype(F32) * valid_rows
    dm = (ga3 * d3).astype(BF16)
    dga3 = jnp.sum(d3 * m, axis=1)
    db_down = jnp.sum(dm.astype(F32), axis=(0, 1))
    dw_down = jnp.einsum("bsk,bsd->kd", g, dm, preferred_element_type=F32)
    dg = jnp.einsum("bsd,kd->bsk", dm, w_down, preferred_element_type=F32)
    du = pull(dg)[0].astype(BF16)
    db_up = jnp.sum(du.astype(F32), axis=(0, 1))
    dw_up = jnp.einsum("bsd,bsk->dk", h3, du, preferred_element_type=F32)
    dh3 = jnp.einsum("bsk,dk->bsd", du, w_up, preferred_element_type=F32)
    dv, dsh3, dsc3 = norm_back(dh3, n3, r3, sc3)
    d2 = d3 + dv
    da2 = (ga2 * d2).astype(BF16)
    dga2 = jnp.sum(d2 * a2, axis=1)
    dh2, dw_qt, dw_pt = attention_back(da2, h2, w_qt, w_pt, kept2)
    dv, dsh2, dsc2 = norm_back(dh2, n2, r2, sc2)
    d1 = d2 + dv
    da1 = (ga1 * d1).astype(BF16)
    dga1 = jnp.sum(d1 * a1, axis=1)
    dh1, dw_qs, dw_ps = attention_back(da1, h1, w_qs, w_ps, kept1)
    dv, dsh1, dsc1 = norm_back(dh1, n1, r1, sc1)
    latents_grad = d1 + dv

    dmod = jnp.stack([dsh1, dsc1, dga1, dsh2, dsc2, dga2, dsh3, dsc3, dga3], axis=1)
    small = jnp.concatenate(
        [dmod.reshape(micro * 9, D), db_up.reshape(-1, D), db_down.reshape(-1, D)], axis=0
    ).astype(BF16)
    parts = [
        part.astype(BF16).reshape(tuple(gathered[i].shape))
        for i, part in ((5, dw_down), (4, dw_up), (3, dw_pt), (2, dw_qt), (1, dw_ps), (0, dw_qs))
    ]
    ddown, dup, dpt, dqt, dps, dqs, small = scatter(parts, small)
    flat = tuple(part.reshape(-1) for part in (dqs, dps, dqt, dpt, dup))
    small = small.reshape(devices, -1, D)
    dmod_all = small[:, : micro * 9].reshape(devices * micro, 9 * D)
    me = lax.axis_index(AXES)
    my_condition = lax.dynamic_slice_in_dim(condition, me * rows, rows, axis=1)
    dw_ada = lax.dot_general(
        my_condition, dmod_all, (((0,), (0,)), ((), ())), preferred_element_type=F32
    )
    db = jnp.concatenate(
        [
            jnp.sum(dmod_all.astype(F32), axis=0),
            jnp.sum(small[:, micro * 9 :].astype(F32), axis=0).reshape(-1),
        ]
    )
    db = lax.dynamic_slice_in_dim(db, me * biases.shape[0], biases.shape[0])

    shape = latents.shape
    return (
        output.reshape(shape),
        latents_grad.reshape(shape),
        *flat,
        ddown.reshape(-1),
        dw_ada.reshape(-1),
        db,
    )


def per_device(latents, buckets, step_ids, qs, ps, qt, pt, up, down, ada, biases, cotangent):
    devices = lax.axis_size(AXES)
    part = D // devices
    rows = 2 * TOKENS
    own_bias = jnp.pad(biases, (0, D - biases.shape[0]))[None]
    conditions = timestep_condition(step_ids[:, 0])
    small = jnp.concatenate([conditions, own_bias, jnp.zeros((5, D), BF16)], axis=0)
    bucket = buckets[:, 0]
    length = jnp.where(bucket == 0, SPATIAL, jnp.where(bucket == 1, SPATIAL // 2, SPATIAL // 8))
    valid = (jnp.arange(TOKENS) % SPATIAL)[None] < length[:, None]
    keys = jnp.where(valid, 0.0, MASKED).astype(F32)
    valid = valid.astype(F32).reshape(rows, 1)
    shards = [w.reshape(part, -1) for w in (qs, ps, qt, pt, up)] + [down.reshape(-1, D)]
    tokens = latents.reshape(rows, D)
    grads_in = cotangent.reshape(rows, D)
    output, dga3, chosen, kept = run_forward(
        small, ada.reshape(part, -1), shards, tokens, grads_in, keys, valid
    )
    grads = run_backward(grads_in, valid, dga3, chosen, kept)
    me = lax.axis_index(AXES)
    bias_grad = grads["grad_bias"][:14].reshape(-1)
    return (
        output.reshape(latents.shape),
        grads["d"].reshape(latents.shape),
        *(grads["grad_" + t].reshape(-1) for t in ("qs", "ps", "qt", "pt", "up", "down", "ada")),
        lax.dynamic_slice_in_dim(bias_grad, me * SHARE, SHARE),
    )


def solution(mesh):
    items = P(None, AXES, None, None, None)
    flat = P(AXES)
    known = mesh.shape["wide"] == 8 and mesh.shape["narrow"] == 4
    return jax.shard_map(
        per_device if known else per_device_plain,
        mesh=mesh,
        in_specs=(items, P(None, AXES), P(None, AXES)) + (flat,) * 8 + (items,),
        out_specs=(items, items) + (flat,) * 8,
        check_vma=False,
    )
```

```python
import math

import jax
import jax.numpy as jnp
from jax import lax
from jax.experimental import pallas as pl
from jax.experimental.pallas import tpu as pltpu
from jax.sharding import PartitionSpec as P

D = 768
HEADS = 12
HD = 64
FF = 3072
AXES = ("wide", "narrow")
EPS = 1e-06
MASKED = -1e30
F32 = jnp.float32
BF16 = jnp.bfloat16
GELU = math.sqrt(2.0 / math.pi)
MESH = pl.DeviceIdType.MESH
DEVICES = 32
OWNERS = 9 * D // 256
SHARE = (10 * D + FF) // DEVICES
SPATIAL = 16
TOKENS = 256
VMEM_LIMIT = 67_000_000


def dot(a, b):
    return jnp.dot(a, b, preferred_element_type=F32)


def place():
    w, z = lax.axis_index("wide"), lax.axis_index("narrow")
    return w // 4, (w // 2) % 2, w % 2, z


def device_at(y, x, c, z):
    return {"wide": (y * 2 + x) * 2 + c, "narrow": z}


def remote(src, dst, send, recv, target):
    return pltpu.make_async_remote_copy(
        src_ref=src, dst_ref=dst, send_sem=send, recv_sem=recv,
        device_id=target, device_id_type=MESH,
    )


class Sender:
    def __init__(self):
        self.copies = []

    def go(self, src, dst, send, recv, target):
        copy = remote(src, dst, send, recv, target)
        copy.start()
        self.copies.append(copy)

    def drain(self):
        for copy in self.copies:
            copy.wait_send()


def timestep_condition(step_values):
    half_width = D // 2
    frequency = jnp.exp(-math.log(10000.0) * jnp.arange(half_width, dtype=F32) / half_width)
    angles = step_values.astype(F32)[:, None] * frequency
    return jax.nn.silu(jnp.concatenate([jnp.cos(angles), jnp.sin(angles)], axis=-1)).astype(BF16)


class Gather:
    SEMAPHORES = (3, 3, 10, 10, 3, 3, 3, 3)

    def __init__(self, here, sender, own, out, semaphores, local):
        self.here, self.sender, self.own, self.out, self.local = here, sender, own, out, local
        self.zs, self.zr, self.cs, self.cr, self.xs, self.xr, self.ys, self.yr = semaphores
        y, x, c, z = here
        self.sib = device_at(y, x, 1 - c, z)
        self.xn = device_at(y, 1 - x, c, z)
        self.yn = device_at(1 - y, x, c, z)

    @staticmethod
    def scratch(count):
        kinds = [pltpu.SemaphoreType.DMA((count, k)) for k in Gather.SEMAPHORES]
        return kinds + [pltpu.SemaphoreType.DMA((count,))]

    def start(self, i):
        y, x, c, z = self.here
        mine = self.out[i].at[y, x, c, z]
        for step in (2, 1, 3):
            self.sender.go(
                self.own[i], mine, self.zs.at[i, step - 1],
                self.zr.at[i, step - 1], device_at(y, x, c, (z + step) % 4),
            )
        pltpu.make_async_copy(self.own[i], mine, self.local.at[i]).start()
        self.sender.go(self.own[i], mine, self.cs.at[i, 0], self.cr.at[i, 0], self.sib)

    def along(self, ref, send, recv, target):
        self.sender.go(ref, ref, send, recv, target)

    def arrived(self, ref, send, recv):
        remote(ref, ref, send, recv, self.sib).wait_recv()

    def across(self, i, k, ref):
        self.sender.go(ref, ref, self.cs.at[i, k], self.cr.at[i, k], self.sib)

    def stage1(self, i):
        y, x, c, z = self.here
        out = self.out[i]
        pltpu.make_async_copy(self.own[i], out.at[y, x, c, z], self.local.at[i]).wait()
        for step in (1, 2, 3):
            self.arrived(out.at[y, x, c, (z + 4 - step) % 4], self.zs.at[i, step - 1], self.zr.at[i, step - 1])
        low, high = out.at[y, x, c, pl.ds(0, 2)], out.at[y, x, c, pl.ds(2, 2)]
        self.along(low, self.xs.at[i, 0], self.xr.at[i, 0], self.xn)
        self.along(high, self.ys.at[i, 0], self.yr.at[i, 0], self.yn)
        self.along(high, self.xs.at[i, 1], self.xr.at[i, 1], self.xn)
        self.along(low, self.ys.at[i, 1], self.yr.at[i, 1], self.yn)
        for step in (1, 2, 3):
            self.across(i, step, out.at[y, x, c, (z + 4 - step) % 4])

    def stage2(self, i):
        y, x, c, z = self.here
        low_x = self.out[i].at[y, 1 - x, c, pl.ds(0, 2)]
        high_y = self.out[i].at[1 - y, x, c, pl.ds(2, 2)]
        self.arrived(low_x, self.xs.at[i, 0], self.xr.at[i, 0])
        self.along(low_x, self.ys.at[i, 2], self.yr.at[i, 2], self.yn)
        self.arrived(high_y, self.ys.at[i, 0], self.yr.at[i, 0])
        self.along(high_y, self.xs.at[i, 2], self.xr.at[i, 2], self.xn)
        self.across(i, 4, low_x)
        self.across(i, 5, high_y)

    def stage3(self, i):
        y, x, c, z = self.here
        out = self.out[i]
        arrivals = (
            (out.at[y, 1 - x, c, pl.ds(2, 2)], self.xs.at[i, 1], self.xr.at[i, 1]),
            (out.at[1 - y, x, c, pl.ds(0, 2)], self.ys.at[i, 1], self.yr.at[i, 1]),
            (out.at[1 - y, 1 - x, c, pl.ds(2, 2)], self.xs.at[i, 2], self.xr.at[i, 2]),
            (out.at[1 - y, 1 - x, c, pl.ds(0, 2)], self.ys.at[i, 2], self.yr.at[i, 2]),
        )
        for k, (ref, send, recv) in enumerate(arrivals):
            self.arrived(ref, send, recv)
            self.across(i, 6 + k, ref)

    def finish(self, i):
        y, x, c, z = self.here
        o = 1 - c
        out = self.out[i]
        arrivals = [out.at[y, x, o, (z + 4 - step) % 4] for step in (0, 1, 2, 3)]
        arrivals += [
            out.at[y, 1 - x, o, pl.ds(0, 2)],
            out.at[1 - y, x, o, pl.ds(2, 2)],
            out.at[y, 1 - x, o, pl.ds(2, 2)],
            out.at[1 - y, x, o, pl.ds(0, 2)],
            out.at[1 - y, 1 - x, o, pl.ds(2, 2)],
            out.at[1 - y, 1 - x, o, pl.ds(0, 2)],
        ]
        for k, ref in enumerate(arrivals):
            self.arrived(ref, self.cs.at[i, k], self.cr.at[i, k])


class Spread:
    SEMAPHORES = (3, 3, 6, 6, 6, 6, 2, 2, 16, 16)

    def __init__(self, here, sender, own, out, semaphores, local, pairs):
        self.here, self.sender, self.own, self.out, self.local = here, sender, own, out, local
        self.pairs = pairs
        self.zs, self.zr, self.xs, self.xr, self.ys, self.yr, self.ps, self.pr, self.cs, self.cr = semaphores
        y, x, c, z = here
        self.sib = device_at(y, x, 1 - c, z)
        self.xn = device_at(y, 1 - x, c, z)
        self.yn = device_at(1 - y, x, c, z)
        self.partner = z + 1 - 2 * (z % 2)
        self.opposite = (z + 2) % 4
        self.zp = device_at(y, x, c, self.partner)

    @staticmethod
    def scratch(count):
        kinds = [pltpu.SemaphoreType.DMA((count, k)) for k in Spread.SEMAPHORES]
        return kinds + [pltpu.SemaphoreType.DMA((count,))]

    def to_x(self, i, k, ref):
        self.sender.go(ref, ref, self.xs.at[i, k], self.xr.at[i, k], self.xn)

    def to_y(self, i, k, ref):
        self.sender.go(ref, ref, self.ys.at[i, k], self.yr.at[i, k], self.yn)

    def across(self, i, k, ref):
        self.sender.go(ref, ref, self.cs.at[i, k], self.cr.at[i, k], self.sib)

    def arrived(self, ref, send, recv):
        remote(ref, ref, send, recv, self.sib).wait_recv()

    def from_z(self, step):
        return (self.here[3] + 4 - step) % 4

    def beside(self, i):
        y, x, c, z = self.here
        own, mine = self.own[i], self.out[i].at[y, x, c, z]
        pltpu.make_async_copy(own, mine, self.local.at[i]).start()
        self.sender.go(own, mine, self.xs.at[i, 0], self.xr.at[i, 0], self.xn)
        self.sender.go(own, mine, self.ys.at[i, 0], self.yr.at[i, 0], self.yn)
        self.sender.go(own, mine, self.cs.at[i, 0], self.cr.at[i, 0], self.sib)

    def along(self, i):
        y, x, c, z = self.here
        own, mine = self.own[i], self.out[i].at[y, x, c, z]
        for step in (2, 1, 3):
            there = device_at(y, x, c, (z + step) % 4)
            self.sender.go(own, mine, self.zs.at[i, step - 1], self.zr.at[i, step - 1], there)

    def column(self, i):
        y, x, c, z = self.here
        for step in (2, 1, 3):
            ref = self.out[i].at[y, x, c, self.from_z(step)]
            self.arrived(ref, self.zs.at[i, step - 1], self.zr.at[i, step - 1])
            self.to_x(i, step, ref)
            self.to_y(i, step, ref)
            self.across(i, step, ref)

    def sides(self, i):
        y, x, c, z = self.here
        for step in (0, 2, 1, 3):
            from_x = self.out[i].at[y, 1 - x, c, self.from_z(step)]
            self.arrived(from_x, self.xs.at[i, step], self.xr.at[i, step])
            if step == 0 or step == 2 and not self.pairs[i]:
                self.to_y(i, 4 + step // 2, from_x)
            self.across(i, 4 + step, from_x)
            from_y = self.out[i].at[1 - y, x, c, self.from_z(step)]
            self.arrived(from_y, self.ys.at[i, step], self.yr.at[i, step])
            if step == 2 and self.pairs[i]:
                self.to_x(i, 4, from_y)
            if step % 2 and not self.pairs[i]:
                self.to_x(i, 4 + step // 2, from_y)
            self.across(i, 8 + step, from_y)

    def diagonal(self, i):
        y, x, c, z = self.here
        where = self.out[i].at[1 - y, 1 - x, c]
        blocks = self.corner(i)
        if self.pairs[i]:
            lanes = ((self.ys, self.yr, 4), (self.xs, self.xr, 4))
        else:
            lanes = ((self.ys, self.yr, 4), (self.ys, self.yr, 5), (self.xs, self.xr, 4), (self.xs, self.xr, 5))
        for k, (send, recv, n) in enumerate(lanes):
            ref = where.at[blocks[k]]
            self.arrived(ref, send.at[i, n], recv.at[i, n])
            if self.pairs[i]:
                self.sender.go(ref, ref, self.ps.at[i, k], self.pr.at[i, k], self.zp)
            self.across(i, 12 + k, ref)

    def corner(self, i):
        if self.pairs[i]:
            return self.here[3], self.opposite, self.partner, (self.partner + 2) % 4
        return self.from_z(0), self.from_z(2), self.from_z(1), self.from_z(3)

    def pair(self, i):
        y, x, c, z = self.here
        where = self.out[i].at[1 - y, 1 - x, c]
        for k, block in enumerate(self.corner(i)[2:] if self.pairs[i] else ()):
            ref = where.at[block]
            self.arrived(ref, self.ps.at[i, k], self.pr.at[i, k])
            self.across(i, 14 + k, ref)

    def finish(self, i):
        y, x, c, z = self.here
        out, o = self.out[i], 1 - c
        pltpu.make_async_copy(self.own[i], out.at[y, x, c, z], self.local.at[i]).wait()
        arrivals = [out.at[y, x, o, self.from_z(step)] for step in range(4)]
        arrivals += [out.at[y, 1 - x, o, self.from_z(step)] for step in range(4)]
        arrivals += [out.at[1 - y, x, o, self.from_z(step)] for step in range(4)]
        arrivals += [out.at[1 - y, 1 - x, o, block] for block in self.corner(i)]
        for k, ref in enumerate(arrivals):
            self.arrived(ref, self.cs.at[i, k], self.cr.at[i, k])


PAIRED = (False, True, True, True, True, False)
SPREAD_STEPS = (
    (("A", 0), ("B", 0),), (("B", 1),), (("A", 3), ("A", 4),), (), (), (), (("B", 2),), (), (("B", 4),),
    (("A", 1),), (("A", 2), ("C", 0),), (), (), (("B", 3),), (("C", 1),), (), (("B", 5), ("X", 0),), (),
    (("C", 2), ("X", 1), ("D", 0),), (), (), (), (("X", 2), ("C", 4), ("D", 1),), (("C", 3), ("D", 2),),
    (("P", 1),), (), (), (("P", 2),), (), (("X", 4),), (), (("X", 3), ("A", 5), ("C", 5),), (("D", 4), ("D", 3),),
    (), (), (), (("P", 4), ("P", 3),), (("X", 5),), (), (), (), (), (("D", 5),), (),
)


class Steps:
    def __init__(self, calls, table):
        self.calls, self.table = calls, list(table)

    def __call__(self):
        for kind, i in self.table.pop(0):
            self.calls[kind](i)


class Names:
    def __init__(self, names, refs):
        for name, ref in zip(names, refs, strict=True):
            setattr(self, name, ref)


def rows_of(item, step, size):
    return pl.ds(pl.multiple_of(item * TOKENS + step * size, size), size)


def lane_cols(start, size=128):
    return pl.ds(pl.multiple_of(start, 128), size)


def dot_t(a, b):
    return lax.dot_general(a, b, (((1,), (1,)), ((), ())), preferred_element_type=F32)


def t_dot(a, b):
    return lax.dot_general(a, b, (((0,), (0,)), ((), ())), preferred_element_type=F32)


def weight_block(ref, start, size):
    cols = ref[:, :, :, :, :, pl.ds(start, size)]
    return cols.reshape(-1, size)


def two_heads(x, scale):
    lane = lax.broadcasted_iota(jnp.int32, x.shape, 1)
    x = x * jnp.asarray(scale, x.dtype)
    zero = jnp.zeros_like(x)
    return jnp.concatenate([jnp.where(lane < HD, x, zero), jnp.where(lane >= HD, x, zero)], axis=0)


def pick_heads(first, second):
    lane = lax.broadcasted_iota(jnp.int32, first.shape, 1)
    return jnp.where(lane < HD, first, second)


def norm_rows(v):
    centre = v - jnp.mean(v, axis=-1, keepdims=True)
    inverse = lax.rsqrt(jnp.mean(centre * centre, axis=-1, keepdims=True) + EPS)
    return centre * inverse, inverse


CHUNK = 32
PAIRS = HEADS // 2
TENSORS = ("qs", "ps", "qt", "pt", "up", "down")
SETS = ("n", "r", "h", "q", "p", "c", "a")


def save_shapes(tokens):
    rows = 2 * tokens
    attention = {
        "n": ((rows, D), BF16), "r": ((rows, 1), F32), "h": ((rows, D), BF16),
        "q": ((rows, 3 * D), BF16), "p": ((rows, 2 * PAIRS * tokens), BF16),
        "c": ((rows, D), BF16), "a": ((rows, D), BF16),
    }
    out = {}
    for k in (1, 2):
        out.update({name + str(k): spec for name, spec in attention.items()})
    out.update({
        "n3": ((rows, D), BF16), "r3": ((rows, 1), F32), "h3": ((rows, D), BF16),
        "g": ((rows, FF), BF16), "gp": ((rows, FF), BF16), "mods": ((9, 8, D), F32),
    })
    return out


def unflatten(s, flat, own):
    rows, size = own.shape
    stride = size // 128
    s.stage[pl.ds(0, flat.shape[0]), :] = flat[...].astype(F32)
    for k in range(stride):
        own[:, k * 128 : (k + 1) * 128] = s.stage[pl.ds(k, rows, stride=stride), :].astype(BF16)


def lengths(buckets):
    return jnp.where(buckets == 0, SPATIAL, jnp.where(buckets == 1, SPATIAL // 2, SPATIAL // 8))


def valid_rows(s):
    length = lengths(s.buckets[...])
    spot = lax.broadcasted_iota(jnp.int32, (TOKENS, 1), 0) % SPATIAL
    for item in range(2):
        s.valid[item * TOKENS : (item + 1) * TOKENS, :] = (spot < length[item : item + 1, :]).astype(F32)


def norm_into(s, k, shift, scale, rows, item, v):
    n, r = norm_rows(v)
    getattr(s, "n" + k)[rows, :] = n.astype(BF16)
    getattr(s, "r" + k)[rows, :] = r
    h = n * (1.0 + s.mods[scale, item : item + 1, :]) + s.mods[shift, item : item + 1, :]
    getattr(s, "h" + k)[rows, :] = h.astype(BF16)


def project(s, k, weight, point):
    h, q = getattr(s, "h" + k), getattr(s, "q" + k)
    for j in range(3):
        q[:, j * D : (j + 1) * D] = dot(h[...], weight_block(weight, j * D, D)).astype(BF16)
        point()


def attend(s, k, bias_of, first, last):
    q, p, c = getattr(s, "q" + k), getattr(s, "p" + k), getattr(s, "c" + k)

    def body(step, _):
        item, pair = step // PAIRS, step % PAIRS
        rows = pl.ds(pl.multiple_of(item * TOKENS, TOKENS), TOKENS)
        at = [lane_cols(pair * 128 + j * D) for j in range(3)]
        scores = dot_t(two_heads(q[rows, at[0]], HD ** (-0.5)), q[rows, at[1]])
        scores = (scores.reshape(2, TOKENS, TOKENS) + bias_of(item)).reshape(2 * TOKENS, TOKENS)
        expanded = jnp.exp(scores - jnp.max(scores, axis=-1, keepdims=True))
        soft = (expanded * (1.0 / jnp.sum(expanded, axis=-1, keepdims=True))).astype(BF16)
        p[:, lane_cols(step * TOKENS, TOKENS)] = soft
        context = dot(soft, q[rows, at[2]])
        c[rows, at[0]] = pick_heads(context[:TOKENS], context[TOKENS:]).astype(BF16)
        return 0

    lax.fori_loop(first, last, body, 0)


def after_attention(s, k, next_k, weight, gate, shift, scale):
    s.acc[...] = dot(getattr(s, "c" + k)[...], weight_block(weight, 0, D))
    for item in range(2):
        def body(t, _):
            rows = rows_of(item, t, CHUNK)
            a = s.acc[rows, :]
            v = s.x[rows, :] + s.mods[gate, item : item + 1, :] * a
            s.x[rows, :] = v
            getattr(s, "a" + k)[rows, :] = a.astype(BF16)
            norm_into(s, next_k, shift, scale, rows, item, v)
            return 0

        lax.fori_loop(0, TOKENS // CHUNK, body, 0)


def flat_bias(s):
    s.bias[...] = jnp.zeros_like(s.bias)
    for d in range(DEVICES):
        y, x, c, z = d // 16, (d // 8) % 2, (d // 4) % 2, d % 4
        piece = s.small_all[y, x, c, z].astype(F32)[2:3, :512]
        lane = lax.broadcasted_iota(jnp.int32, piece.shape, 1)
        piece = jnp.where(lane < SHARE, piece, 0.0)
        start = d * SHARE
        if start % 128:
            piece = pltpu.roll(piece, start % 128, 1)
        low = start // 128 * 128
        s.bias[:, low : low + 512] = s.bias[:, low : low + 512] + piece


def forward_kernel(names, *refs):
    s = Names(names, refs)
    here = place()
    y, x, c, z = here
    me = ((y * 2 + x) * 2 + c) * 4 + z
    sender = Sender()
    weights = [getattr(s, "w_" + t) for t in TENSORS]
    s.flat = [getattr(s, "flat_" + t) for t in TENSORS]
    own = [getattr(s, "own_" + t) for t in TENSORS]
    gather = Spread(here, sender, own, weights, [getattr(s, f"gs{i}") for i in range(10)], s.gs10, PAIRED)
    calls = {"A": gather.beside, "B": gather.along, "C": gather.column}
    calls |= {"X": gather.sides, "D": gather.diagonal, "P": gather.pair}
    point = Steps(calls, SPREAD_STEPS)
    little = Gather(here, sender, [s.small], [s.small_all], [getattr(s, f"ls{i}") for i in range(8)], s.ls8)
    saves = []

    def save(*names):
        for name in names:
            copy = pltpu.make_async_copy(getattr(s, name), getattr(s, "out_" + name), s.save_sem.at[len(saves)])
            copy.start()
            saves.append(copy)

    def target(k):
        d = (me + k) % DEVICES
        return d, {"wide": d // 4, "narrow": d % 4}

    barrier = pltpu.get_barrier_semaphore()

    def signal(k, _):
        pl.semaphore_signal(barrier, inc=1, device_id=target(k)[1], device_id_type=MESH)
        return 0

    lax.fori_loop(1, DEVICES, signal, 0)
    s.little[...] = jnp.zeros_like(s.little)
    s.little[0:2, :] = s.conditions[...].astype(F32)
    s.little[2:3, :SHARE] = s.biases[...].astype(F32)
    s.small[...] = s.little[...].astype(BF16)
    unflatten(s, s.flat_ada, s.ada)
    pl.semaphore_wait(barrier, DEVICES - 1)

    def columns_copy(k):
        d, there = target(k)
        src = s.ada.at[:, lane_cols(d * 256, 256)]
        return d, remote(src, s.ada_cols.at[me], s.a_send.at[k], s.a_recv.at[me], there)

    little.start(0)

    def send_columns(k, _):
        d, copy = columns_copy(k)

        @pl.when(d < OWNERS)
        def _():
            copy.start()

        return 0

    lax.fori_loop(1, DEVICES, send_columns, 0)
    owner = me < OWNERS
    mine = jnp.minimum(me, OWNERS - 1)
    own_columns = pltpu.make_async_copy(s.ada.at[:, lane_cols(mine * 256, 256)], s.ada_cols.at[me], s.own_sem.at[0])
    own_columns.start()
    for i in range(len(own)):
        unflatten(s, s.flat[i], own[i])
    point()

    place_of = lambda n: lax.broadcasted_iota(jnp.int32, (TOKENS, TOKENS), n)
    same_frame = place_of(0) // SPATIAL == place_of(1) // SPATIAL
    same_place = place_of(0) % SPATIAL == place_of(1) % SPATIAL
    for item in range(2):
        seen = lax.broadcasted_iota(jnp.int32, (1, TOKENS), 1) % SPATIAL < lengths(s.buckets[...])[item : item + 1, :]
        s.space_bias[item] = jnp.where(same_frame, jnp.where(seen, 0.0, MASKED), MASKED)
    s.time_bias[...] = jnp.where(same_place, 0.0, MASKED)
    valid_rows(s)
    point()
    point()
    little.stage1(0)
    point()
    little.stage2(0)
    point()
    little.stage3(0)
    point()
    little.finish(0)
    point()
    own_columns.wait()

    def modulation_copy(k):
        d, there = target(k)
        src = s.mod_cols.at[pl.ds(pl.multiple_of(d * 8, 8), 8)]
        return remote(src, s.mod_all.at[me], s.m_send.at[k], s.m_recv.at[me], there)

    own_mod = pltpu.make_async_copy(
        s.mod_cols.at[pl.ds(pl.multiple_of(me * 8, 8), 8)], s.mod_all.at[mine], s.own_sem.at[1]
    )

    conditions = s.small_all[...].reshape(DEVICES * 8, D)
    point()

    @pl.when(owner)
    def _():
        def wait_columns(k, _):
            d, there = target(k)
            remote(s.ada_cols.at[d], s.ada_cols.at[d], s.a_send.at[k], s.a_recv.at[d], there).wait_recv()
            return 0

        lax.fori_loop(1, DEVICES, wait_columns, 0)
        s.mod_cols[...] = dot(conditions, s.ada_cols[...].reshape(D, 256))

        def send_modulation(k, _):
            modulation_copy(k).start()
            return 0

        lax.fori_loop(1, DEVICES, send_modulation, 0)
        own_mod.start()

    point()
    flat_bias(s)
    point()
    part = D // DEVICES
    spot = lambda shape, n: lax.broadcasted_iota(jnp.int32, shape, n)
    col = spot((D, 128), 1)
    wanted = (spot((D, 128), 0) == me * part + col) & (col < part)
    mine_only = dot(conditions, wanted.astype(F32).astype(BF16)).astype(BF16)
    row, item = spot((D, DEVICES * 8), 0), spot((D, DEVICES * 8), 1)
    slot = row % part
    copy_of = (row // part == item // 8) & (slot // 9 == item % 8) & (slot < 18)
    s.chosen[...] = dot(copy_of.astype(F32).astype(BF16), mine_only).astype(BF16)
    for _ in range(6):
        point()

    @pl.when(owner)
    def _():
        own_mod.wait()

    def wait_modulation(k, _):
        d, there = target(k)

        @pl.when(d < OWNERS)
        def _():
            remote(s.mod_all.at[d], s.mod_all.at[d], s.m_send.at[k], s.m_recv.at[d], there).wait_recv()

        return 0

    lax.fori_loop(1, DEVICES, wait_modulation, 0)
    for j in range(9):
        row = jnp.concatenate([s.mod_all[3 * j + i] for i in range(3)], axis=1)
        s.mods[j] = row + s.bias[:, j * D : (j + 1) * D]
    save("mods")

    for item in range(2):
        def first(t, _):
            rows = rows_of(item, t, CHUNK)
            v = s.latents[rows, :].astype(F32)
            s.x[rows, :] = v
            norm_into(s, "1", 0, 1, rows, item, v)
            return 0

        lax.fori_loop(0, TOKENS // CHUNK, first, 0)
        point()
    save("n1", "r1", "h1")

    def ready(i):
        point()
        gather.finish(i)
        save("w_" + TENSORS[i])

    ready(0)
    project(s, "1", s.w_qs, point)
    space = lambda item: s.space_bias[item]
    for k in range(4):
        attend(s, "1", space, 3 * k, 3 * k + 3)
        point()
    ready(1)
    after_attention(s, "1", "2", s.w_ps, 2, 3, 4)
    save("q1", "p1", "c1", "a1", "n2", "r2", "h2")
    point()
    ready(2)
    project(s, "2", s.w_qt, point)
    time = lambda item: s.time_bias[...]
    for k in range(4):
        attend(s, "2", time, 3 * k, 3 * k + 3)
        point()
    ready(3)
    after_attention(s, "2", "3", s.w_pt, 5, 6, 7)
    save("q2", "p2", "c2", "a2", "n3", "r3", "h3")
    point()
    ready(4)
    for j in range(FF // D):
        s.acc[...] = dot(s.h3[...], weight_block(s.w_up, j * D, D))
        b_up = s.bias[:, (9 + j) * D : (10 + j) * D]

        def activate(t, _):
            rows = rows_of(0, t, CHUNK)
            u = s.acc[rows, :] + b_up
            square = u * u
            th = jnp.tanh(u * (GELU + (GELU * 0.044715) * square))
            half = 0.5 * u
            s.g[rows, j * D : (j + 1) * D] = (half + half * th).astype(BF16)
            slope = 0.5 + 0.5 * th + half * (1.0 - th * th) * (GELU + (3 * GELU * 0.044715) * square)
            s.gp[rows, j * D : (j + 1) * D] = slope.astype(BF16)
            return 0

        lax.fori_loop(0, 2 * TOKENS // CHUNK, activate, 0)
        point()
    save("g", "gp")
    ready(5)
    for j in range(FF // D):
        w = s.w_down[j // 2, j % 2].reshape(D, D)
        part = dot(s.g[:, j * D : (j + 1) * D], w)
        s.acc[...] = part if j == 0 else s.acc[...] + part
    b_down = s.bias[:, (9 + FF // D) * D : (10 + FF // D) * D]
    for item in range(2):
        gate = s.mods[8, item : item + 1, :]

        def last(t, total):
            rows = rows_of(item, t, CHUNK)
            m = s.acc[rows, :] + b_down
            valid = s.valid[rows, :]
            s.output[rows, :] = ((s.x[rows, :] + gate * m) * valid).astype(BF16)
            d3 = s.cotangent[rows, :].astype(F32) * valid
            return total + jnp.sum((d3 * m).reshape(CHUNK // 8, 8, D), axis=0)

        total = lax.fori_loop(0, TOKENS // CHUNK, last, jnp.zeros((8, D), F32))
        s.dga3[item : item + 1, :] = jnp.sum(total, axis=0, keepdims=True)

    def drain(k, _):
        d, copy = columns_copy(k)

        @pl.when(d < OWNERS)
        def _():
            copy.wait_send()

        @pl.when(owner)
        def _():
            modulation_copy(k).wait_send()

        return 0

    lax.fori_loop(1, DEVICES, drain, 0)
    sender.drain()
    for copy in saves:
        copy.wait()


def run_forward(conditions, biases, buckets, ada, shards, latents, cotangent):
    vmem, any_space = pl.BlockSpec(memory_space=pltpu.VMEM), pl.BlockSpec(memory_space=pl.ANY)
    saved = save_shapes(TOKENS)
    part = D // DEVICES
    own = {t: (4 * part, D) if t == "down" else (part, WIDTHS[t]) for t in TENSORS}
    weights = {"w_" + t: ((2, 2, 2, 4) + own[t], BF16) for t in TENSORS}
    kept = {**saved, **weights}
    rows = 2 * TOKENS
    ins = ["conditions", "biases", "buckets", "flat_ada"] + ["flat_" + t for t in TENSORS] + ["latents", "cotangent"]
    outs = ["output", "dga3", "chosen"] + ["out_" + name for name in kept]
    dma = pltpu.SemaphoreType.DMA
    scratch = {name: pltpu.VMEM(*spec) for name, spec in kept.items()}
    scratch |= {"own_" + t: pltpu.VMEM(shape, BF16) for t, shape in own.items()}
    scratch |= {
        "small": pltpu.VMEM((8, D), BF16), "little": pltpu.VMEM((8, D), F32),
        "stage": pltpu.VMEM(ada.shape, F32), "ada": pltpu.VMEM((part, 9 * D), BF16),
        "valid": pltpu.VMEM((rows, 1), F32),
        "small_all": pltpu.VMEM((2, 2, 2, 4, 8, D), BF16),
        "ada_cols": pltpu.VMEM((DEVICES, part, 256), BF16),
        "mod_cols": pltpu.VMEM((DEVICES * 8, 256), F32),
        "mod_all": pltpu.VMEM((OWNERS, 8, 256), F32),
        "bias": pltpu.VMEM((1, DEVICES * SHARE + 512), F32),
        "x": pltpu.VMEM((rows, D), F32),
        "acc": pltpu.VMEM((rows, D), F32),
        "space_bias": pltpu.VMEM((2, TOKENS, TOKENS), F32),
        "time_bias": pltpu.VMEM((TOKENS, TOKENS), F32),
        "save_sem": dma((len(kept),)),
        "a_send": dma((DEVICES,)), "a_recv": dma((DEVICES,)),
        "m_send": dma((DEVICES,)), "m_recv": dma((DEVICES,)), "own_sem": dma((2,)),
    }
    scratch |= {f"gs{i}": kind for i, kind in enumerate(Spread.scratch(len(shards)))}
    scratch |= {f"ls{i}": kind for i, kind in enumerate(Gather.scratch(1))}
    names = ins + outs + list(scratch)
    results = pl.pallas_call(
        lambda *refs: forward_kernel(names, *refs),
        out_shape=(jax.ShapeDtypeStruct((rows, D), BF16), jax.ShapeDtypeStruct((2, D), F32), jax.ShapeDtypeStruct((D, 128), BF16))
        + tuple(jax.ShapeDtypeStruct(*spec) for spec in kept.values()),
        in_specs=[vmem] * len(ins),
        out_specs=(vmem,) * 3 + (any_space,) * len(kept),
        scratch_shapes=list(scratch.values()),
        compiler_params=pltpu.CompilerParams(
            collective_id=1, has_side_effects=True, vmem_limit_bytes=VMEM_LIMIT
        ),
        name="forward",
    )(conditions, biases, buckets, ada, *shards, latents, cotangent)
    return results[0], results[1], results[2], dict(zip(kept, results[3:]))


class Scatter:
    SEMAPHORES = ((), (), (2,), (2,), (4,), (4,), (4,), (4,), (4,), (4,), (3,), (3,))
    LEADING = ((2, 2, 4), (2,), (4,), (4,), (4,), (3,))

    def __init__(self, here, part, store, buffers, semaphores):
        self.here, self.part, self.store = here, part, store
        self.point = Steps({k: call for k, call in enumerate(self.stages())}, SCATTER_STEPS)
        self.r0, self.rp, self.rd, self.rx, self.ry, self.r3 = buffers
        self.cs, self.cr, self.ps, self.pr, self.ds, self.dr = semaphores[:6]
        self.xs, self.xr, self.ys, self.yr, self.zs, self.zr = semaphores[6:]
        y, x, c, z = here
        self.sib = device_at(y, x, 1 - c, z)
        self.xn = device_at(y, 1 - x, c, z)
        self.yn = device_at(1 - y, x, c, z)
        self.partner = z + 1 - 2 * (z % 2)
        self.opposite = (z + 2) % 4
        self.zp = device_at(y, x, c, self.partner)
        self.copies = [[] for _ in part]

    def stages(self):
        return self.chip, self.pair, self.diagonal, self.sides, self.last

    def by_y(self, i):
        return ((0,), (2,)) if SUMMED_IN_PAIRS[i] else ((0, 2), (1, 3))

    def hop(self, i, kind, k):
        y, x, c, z = self.here
        part = self.part[i]
        if kind == "c":
            return part.at[:, :, 1 - c], self.r0[i], self.cs.at[i], self.cr.at[i], self.sib
        if kind == "p":
            block = (self.partner + 2 * k) % 4
            return part.at[1 - y, 1 - x, c, block], self.rp[i].at[k], self.ps.at[i, k], self.pr.at[i, k], self.zp
        if kind == "d":
            block = (z + k) % 4
            there = self.yn if k in self.by_y(i)[0] else self.xn
            return part.at[1 - y, 1 - x, c, block], self.rd[i].at[k], self.ds.at[i, k], self.dr.at[i, k], there
        if kind == "x":
            block = (z + k) % 4
            return part.at[y, 1 - x, c, block], self.rx[i].at[block], self.xs.at[i, k], self.xr.at[i, k], self.xn
        if kind == "y":
            block = (z + k) % 4
            return part.at[1 - y, x, c, block], self.ry[i].at[block], self.ys.at[i, k], self.yr.at[i, k], self.yn
        there = (z + k + 1) % 4
        return part.at[y, x, c, there], self.r3[i].at[k], self.zs.at[i, k], self.zr.at[i, k], device_at(y, x, c, there)

    def send(self, i, kind, *which):
        for k in which:
            copy = remote(*self.hop(i, kind, k))
            copy.start()
            self.copies[i].append(copy)

    def wait(self, i, kind, *which):
        for k in which:
            remote(*self.hop(i, kind, k)).wait_recv()

    def drain(self, i):
        for copy in self.copies[i]:
            copy.wait_send()
        self.copies[i] = []

    def start(self, i):
        self.send(i, "c", 0)

    def chip(self, i):
        c = self.here[2]
        part, r0 = self.part[i], self.r0[i]
        self.wait(i, "c", 0)

        def add(k, _):
            a, b, q = k // 8, (k // 4) % 2, k % 4
            part[a, b, c, q] = part[a, b, c, q] + r0[a, b, q]
            return 0

        lax.fori_loop(0, 16, add, 0)
        first, second = self.by_y(i)
        if SUMMED_IN_PAIRS[i]:
            self.send(i, "p", 0, 1)
        else:
            self.send(i, "d", *first, *second)
        self.send(i, "x", *[k for k in (1, 3, 0, 2) if k not in first])
        self.send(i, "y", *[k for k in (0, 2, 1, 3) if k not in second])

    def pair(self, i):
        if not SUMMED_IN_PAIRS[i]:
            return
        y, x, c, z = self.here
        part = self.part[i]
        for k, block in enumerate((z, self.opposite)):
            self.wait(i, "p", k)
            part[1 - y, 1 - x, c, block] = part[1 - y, 1 - x, c, block] + self.rp[i][k]
            self.send(i, "d", 2 * k)

    def diagonal(self, i):
        y, x, c, z = self.here
        part = self.part[i]
        first, second = self.by_y(i)
        for k in first:
            self.wait(i, "d", k)
            block = (z + k) % 4
            part[y, 1 - x, c, block] = part[y, 1 - x, c, block] + self.rd[i][k]
            self.send(i, "x", k)
        for k in second:
            self.wait(i, "d", k)
            block = (z + k) % 4
            part[1 - y, x, c, block] = part[1 - y, x, c, block] + self.rd[i][k]
            self.send(i, "y", k)

    def sides(self, i):
        y, x, c, z = self.here
        part, rx, ry = self.part[i], self.rx[i], self.ry[i]
        self.wait(i, "x", 1, 2, 3, 0)
        self.wait(i, "y", 1, 3, 0, 2)

        def add(q, _):
            both = rx[q].astype(F32) + ry[q].astype(F32)
            part[y, x, c, q] = (part[y, x, c, q].astype(F32) + both).astype(BF16)
            return 0

        lax.fori_loop(0, 4, add, 0)
        self.send(i, "z", 1, 0, 2)

    def last(self, i):
        y, x, c, z = self.here
        self.wait(i, "z", 0, 1, 2)
        part, r3 = self.part[i], self.r3[i]
        total = (part[y, x, c, z].astype(F32) + r3[0].astype(F32)) + (r3[1].astype(F32) + r3[2].astype(F32))
        out, start, stride = self.store[i]
        flatten_into(out, total, start, stride)

    def rest(self):
        while self.point.table:
            self.point()


def flatten_into(out, value, start, stride):
    rows, size = value.shape
    for k in range(size // 128):
        out[pl.ds(start + k, rows, stride=stride), :] = value[:, k * 128 : (k + 1) * 128]


GRADS = ("down", "up", "pt", "qt", "ps", "qs")
WIDTHS = {"down": D, "up": FF, "pt": D, "qt": 3 * D, "ps": D, "qs": 3 * D}
ENTRIES = [("down", k * D // 2, D // 2) for k in range(2)] + [("up", k * FF // 2, FF // 2) for k in range(2)]
ENTRIES += [("pt", 0, D)] + [("qt", k * D, D) for k in range(3)] + [("ps", 0, D)] + [("qs", k * D, D) for k in range(3)]
DOWN, UP, PT, QT, PS, QS = 0, 2, 4, 5, 8, 9
SUMMED_IN_PAIRS = (True, True, True, True, False, False, True, True, True, False, True, False)
SCATTER_STEPS = (
    (), (), (), (), ((0, 0),), (), ((0, 1),), (), ((1, 0), (0, 2),), ((1, 1),), (), (), ((2, 0), (1, 2), (0, 3),),
    (), ((0, 4), (2, 1), (1, 4),), ((3, 0), (2, 2), (1, 3),), (), (), (), (), ((2, 4),), ((0, 5), (4, 0), (1, 5),),
    ((3, 1), (0, 6),), ((3, 2), (0, 7),), ((2, 3), (3, 4),), ((2, 5),), ((4, 1), (1, 6), (0, 8),), (),
    ((3, 3), (1, 7), (4, 2), (3, 5),), ((2, 6), (1, 8), (4, 4),), ((2, 7),), ((3, 6),),
    ((2, 8), (3, 7), (0, 9), (1, 9),), ((0, 10), (4, 3), (3, 8),), ((2, 9), (0, 11), (1, 11),), ((4, 5),), (), (),
    ((4, 6), (3, 9), (1, 10),), ((4, 7), (2, 11),), ((2, 10),), ((4, 8), (3, 11),), ((3, 10),), (), ((4, 9),), (),
    (), (), (), (), ((4, 11),), ((4, 10),),
)
BLOCKS = [("down", j) for j in range(4)] + [("up", j) for j in range(4)]
BLOCKS += [("pt", 0)] + [("qt", j) for j in range(3)] + [("ps", 0)] + [("qs", j) for j in range(3)]
SLOTS = 4


def attend_back(s, q, p, c_grad, first, last):
    def body(step, _):
        item, pair = step // PAIRS, step % PAIRS
        rows = pl.ds(pl.multiple_of(item * TOKENS, TOKENS), TOKENS)
        at = [lane_cols(pair * 128 + j * D) for j in range(3)]
        soft = p[:, lane_cols(step * TOKENS, TOKENS)]
        dc = c_grad[rows, at[0]]
        queries, keys, values = (q[rows, where] for where in at)
        v_grad = pick_heads(t_dot(soft[:TOKENS], dc), t_dot(soft[TOKENS:], dc))
        soft_grad = dot_t(two_heads(dc, 1.0), values)
        wide = soft.astype(F32)
        product = soft_grad * wide
        score = (product - wide * jnp.sum(product, axis=-1, keepdims=True)).astype(BF16)
        q_both = dot(score, keys)
        q_grad = pick_heads(q_both[:TOKENS], q_both[TOKENS:]) * HD ** (-0.5)
        k_grad = pick_heads(t_dot(score[:TOKENS], queries), t_dot(score[TOKENS:], queries)) * HD ** (-0.5)
        q[rows, at[0]] = q_grad.astype(BF16)
        q[rows, at[1]] = k_grad.astype(BF16)
        q[rows, at[2]] = v_grad.astype(BF16)
        return 0

    lax.fori_loop(first, last, body, 0)


def backward_kernel(names, *refs):
    s = Names(names, refs)
    here = place()
    y, x, c, z = here
    me = ((y * 2 + x) * 2 + c) * 4 + z
    loads = {}

    def fetch(name, src, dst, k):
        loads[name] = pltpu.make_async_copy(src, dst, s.load_sem.at[k])
        loads[name].start()

    def have(*wanted):
        for name in wanted:
            loads.pop(name).wait()

    def fetch_block(k):
        tensor, j = BLOCKS[k]
        src = getattr(s, "w_" + tensor)
        src = src.at[j] if tensor == "down" else src.at[:, :, pl.ds(j * D, D)]
        fetch(("w", k), src, s.blocks.at[k % SLOTS], 16 + k % SLOTS)

    def block(k):
        have(("w", k))
        return s.blocks[k % SLOTS].reshape(D, D)

    def used(k):
        if k + SLOTS < len(BLOCKS):
            fetch_block(k + SLOTS)

    fetch("g", s.in_g, s.g, 0)
    fetch("mods", s.in_mods, s.mods, 1)
    fetch_block(0)
    fetch_block(1)
    fetch("gp", s.in_gp, s.gp, 2)
    fetch("h3", s.in_h3, s.h3, 3)
    fetch_block(2)
    fetch_block(3)
    fetch("n3", s.in_n3, s.n3, 4)
    fetch("r3", s.in_r3, s.r3, 5)

    def fetch_rest(k):
        for i, (name, dst) in enumerate((("a", s.a), ("c", s.c), ("h", s.h), ("n", s.n), ("r", s.r))):
            fetch(name, getattr(s, f"in_{name}{k}"), dst, 6 + i)

    fetch_rest(2)

    homes = {"down": (s.b0, 0), "up": (s.b1, 0), "pt": (s.b2, 0), "qt": (s.b2, D), "ps": (s.b3, 0), "qs": (s.b3, D)}
    parts, store = [], []
    for t, start, width in ENTRIES:
        ref, base = homes[t]
        parts.append(ref.at[:, :, :, :, :, pl.ds(base + start, width)])
        store.append((getattr(s, "grad_" + t), start // 128, WIDTHS[t] // 128))
    buffers = [[getattr(s, f"r{k}_{i}") for i in range(len(ENTRIES))] for k in range(6)]
    scatter = Scatter(here, parts, store, buffers, [getattr(s, f"ss{k}") for k in range(12)])
    sender = Sender()
    little = Gather(here, sender, [s.small], [s.small_all], [getattr(s, f"ls{i}") for i in range(8)], s.ls8)

    barrier = pltpu.get_barrier_semaphore()
    partners = [device_at(y, x, 1 - c, z), device_at(y, 1 - x, c, z), device_at(1 - y, x, c, z)]
    partners += [device_at(y, x, c, (z + step) % 4) for step in (1, 2, 3)]
    for partner in partners:
        pl.semaphore_signal(barrier, inc=1, device_id=partner, device_id_type=MESH)
    pl.semaphore_wait(barrier, 6)

    s.rows[...] = jnp.zeros_like(s.rows)
    valid_rows(s)
    ones = jnp.ones((8, 2 * TOKENS), BF16)
    have("mods")
    for item in range(2):
        gate = s.mods[8, item : item + 1, :]

        def first(t, _):
            rows = rows_of(item, t, CHUNK)
            d3 = s.cotangent[rows, :].astype(F32) * s.valid[rows, :]
            s.d[rows, :] = d3
            s.dm[rows, :] = (gate * d3).astype(BF16)
            return 0

        lax.fori_loop(0, TOKENS // CHUNK, first, 0)
        s.rows[9 * item + 8 : 9 * item + 9, :] = s.dga3[item : item + 1, :]
    s.rows[22:23, :] = dot(ones, s.dm[...])[:1]

    have("g")
    for k in range(2):
        cols = slice(k * D // 2, (k + 1) * D // 2)
        for j in range(2):
            grad = t_dot(s.g[:, 2 * j * D : 2 * (j + 1) * D], s.dm[:, cols]).astype(BF16)
            s.b0[j, :, :, :, :, cols] = grad.reshape(2, 2, 4, 4 * D // DEVICES, D // 2)
        scatter.start(DOWN + k)
        scatter.point()
    fetch("p", s.in_p2, s.g, 0)

    have("gp", "h3")
    for j in range(4):
        cols = slice(j * D, (j + 1) * D)
        s.acc[...] = dot_t(s.dm[...], block(j))
        used(j)

        def slope(t, _):
            rows = rows_of(0, t, CHUNK)
            s.gp[rows, cols] = (s.acc[rows, :] * s.gp[rows, cols].astype(F32)).astype(BF16)
            return 0

        lax.fori_loop(0, 2 * TOKENS // CHUNK, slope, 0)
        s.rows[18 + j : 19 + j, :] = dot(ones, s.gp[:, cols])[:1]
        scatter.point()
        grad = t_dot(s.h3[...], s.gp[:, cols]).astype(BF16)
        s.b1[:, :, :, :, :, cols] = grad.reshape(2, 2, 2, 4, D // DEVICES, D)
        if j % 2:
            scatter.start(UP + j // 2)
        scatter.point()

    def back_through(first_block, source, count, every):
        for j in range(count):
            part = dot_t(source[:, j * D : (j + 1) * D], block(first_block + j))
            used(first_block + j)
            s.acc[...] = part if j == 0 else s.acc[...] + part
            if j % every == every - 1:
                scatter.point()

    back_through(4, s.gp, 4, 2)
    fetch("q", s.in_q2, s.gp.at[:, pl.ds(0, 3 * D)], 2)

    def norm_back(n_ref, r_ref, base, a_ref, gate_row, between=False):
        for item in range(2):
            scale = 1.0 + s.mods[base + 1, item : item + 1, :]
            gate = None if gate_row is None else s.mods[gate_row, item : item + 1, :]

            def body(t, totals):
                rows = rows_of(item, t, CHUNK)
                dh, n = s.acc[rows, :], n_ref[rows, :].astype(F32)
                g = dh * scale
                dhn = dh * n
                mean_g = jnp.mean(g, axis=-1, keepdims=True)
                mean_gn = jnp.mean(g * n, axis=-1, keepdims=True)
                d = s.d[rows, :] + r_ref[rows, :] * (g - mean_g - n * mean_gn)
                s.d[rows, :] = d
                fold = lambda v: jnp.sum(v.reshape(CHUNK // 8, 8, D), axis=0)
                new = [totals[0] + fold(dh), totals[1] + fold(dhn)]
                if gate is not None:
                    s.dm[rows, :] = (gate * d).astype(BF16)
                    new.append(totals[2] + fold(d * a_ref[rows, :].astype(F32)))
                return tuple(new)

            count = 2 if gate is None else 3
            totals = lax.fori_loop(0, TOKENS // CHUNK, body, (jnp.zeros((8, D), F32),) * count)
            for where, total in zip((base, base + 1, base - 1), totals):
                row = 9 * item + where
                s.rows[row : row + 1, :] = jnp.sum(total, axis=0, keepdims=True)
            if between or item:
                scatter.point()

    have("n3", "r3", "a")
    norm_back(s.n3, s.r3, 6, s.a, 5)
    have("c")
    s.b2[:, :, :, :, :, :D] = t_dot(s.c[...], s.dm[...]).astype(BF16).reshape(2, 2, 2, 4, D // DEVICES, D)
    scatter.start(PT)
    s.dc[...] = dot_t(s.dm[...], block(8)).astype(BF16)
    used(8)
    scatter.point()
    have("q", "p")
    for k in range(4):
        attend_back(s, s.gp, s.g, s.dc, 3 * k, 3 * k + 3)
        scatter.point()
    fetch("p", s.in_p1, s.g, 0)
    have("h")
    for j in range(3):
        cols = slice(D + j * D, 2 * D + j * D)
        grad = t_dot(s.h[...], s.gp[:, j * D : (j + 1) * D]).astype(BF16)
        s.b2[:, :, :, :, :, cols] = grad.reshape(2, 2, 2, 4, D // DEVICES, D)
        scatter.start(QT + j)
        scatter.point()
    back_through(9, s.gp, 3, 1)
    fetch("q", s.in_q1, s.gp.at[:, pl.ds(0, 3 * D)], 2)
    have("n", "r")
    fetch("c", s.in_c1, s.c, 7)
    fetch("h", s.in_h1, s.h, 8)
    fetch("a", s.in_a1, s.a, 6)
    have("a")
    norm_back(s.n, s.r, 3, s.a, 2)
    fetch("n", s.in_n1, s.n, 9)
    fetch("r", s.in_r1, s.r, 10)
    have("c")
    s.b3[:, :, :, :, :, :D] = t_dot(s.c[...], s.dm[...]).astype(BF16).reshape(2, 2, 2, 4, D // DEVICES, D)
    scatter.start(PS)
    s.dc[...] = dot_t(s.dm[...], block(12)).astype(BF16)
    used(12)
    scatter.point()
    have("q", "p")
    for k in range(4):
        attend_back(s, s.gp, s.g, s.dc, 3 * k, 3 * k + 3)
        scatter.point()
    have("h")
    for j in range(3):
        cols = slice(D + j * D, 2 * D + j * D)
        grad = t_dot(s.h[...], s.gp[:, j * D : (j + 1) * D]).astype(BF16)
        s.b3[:, :, :, :, :, cols] = grad.reshape(2, 2, 2, 4, D // DEVICES, D)
        scatter.start(QS + j)
        scatter.point()
    back_through(13, s.gp, 3, 1)
    have("n", "r")
    norm_back(s.n, s.r, 0, None, None, True)
    s.small[...] = s.rows[...].astype(BF16)
    little.start(0)
    scatter.point()
    little.stage1(0)
    scatter.point()
    little.stage2(0)
    scatter.point()
    little.stage3(0)
    scatter.point()
    little.finish(0)

    gathered = s.small_all[...].reshape(D, D)
    slot = lax.broadcasted_iota(jnp.int32, (D, 128), 0) % (D // DEVICES)
    for j in range(9):
        chosen = jnp.where((slot == j) | (slot == j + 9), s.chosen[...], jnp.zeros((D, 128), BF16))
        grad = t_dot(chosen, gathered)[: D // DEVICES]
        flatten_into(s.grad_ada, grad, j * (D // 128), 9 * D // 128)
        scatter.point()
    row = lax.broadcasted_iota(jnp.int32, (16, D), 0)
    slot = lax.broadcasted_iota(jnp.int32, (16, D), 1) % (D // DEVICES)
    take = ((row < 9) & ((slot == row) | (slot == row + 9))) | ((row >= 9) & (slot == row + 9))
    s.grad_bias[...] = dot(take.astype(F32).astype(BF16), gathered)
    scatter.rest()
    for i in range(len(ENTRIES)):
        scatter.drain(i)
    sender.drain()


def run_backward(cotangent, buckets, dga3, chosen, kept):
    vmem, any_space = pl.BlockSpec(memory_space=pltpu.VMEM), pl.BlockSpec(memory_space=pl.ANY)
    rows, part = 2 * TOKENS, D // DEVICES
    ins = {"cotangent": cotangent, "buckets": buckets, "dga3": dga3, "chosen": chosen}
    fetched = {"in_" + name: kept[name] for name in save_shapes(TOKENS)}
    for t in GRADS:
        shape = (4, DEVICES, part, D) if t == "down" else (DEVICES, part, WIDTHS[t])
        fetched["w_" + t] = kept["w_" + t].reshape(shape)
    ins |= fetched
    block_of = [(4 * part if t == "down" else part, width) for t, _, width in ENTRIES]
    outs = {"grad_" + t: (DEVICES * part * WIDTHS[t] * (4 if t == "down" else 1) // DEVICES // 128, 128) for t in GRADS}
    outs |= {"grad_ada": (part * 9 * D // 128, 128), "grad_bias": (16, D), "d": (rows, D)}
    dma = pltpu.SemaphoreType.DMA
    big = lambda *block: pltpu.VMEM((2, 2, 2, 4) + block, BF16)
    scratch = {
        "b0": big(4 * part, D), "b1": big(part, FF), "b2": big(part, FF), "b3": big(part, FF),
        "blocks": pltpu.VMEM((SLOTS, DEVICES, part, D), BF16),
        "g": pltpu.VMEM((rows, FF), BF16), "gp": pltpu.VMEM((rows, FF), BF16),
        "acc": pltpu.VMEM((rows, D), F32),
        "mods": pltpu.VMEM((9, 8, D), F32), "rows": pltpu.VMEM((24, D), F32),
        "small": pltpu.VMEM((24, D), BF16), "small_all": big(24, D),
        "r3": pltpu.VMEM((rows, 1), F32), "r": pltpu.VMEM((rows, 1), F32), "valid": pltpu.VMEM((rows, 1), F32),
        "load_sem": dma((16 + SLOTS,)),
    }
    scratch |= {name: pltpu.VMEM((rows, D), BF16) for name in ("dm", "dc", "h3", "n3", "a", "c", "h", "n")}
    for k, lead in enumerate(Scatter.LEADING):
        scratch |= {f"r{k}_{i}": pltpu.VMEM(lead + block, BF16) for i, block in enumerate(block_of)}
    scratch |= {f"ss{k}": dma((len(ENTRIES),) + extra) for k, extra in enumerate(Scatter.SEMAPHORES)}
    scratch |= {f"ls{i}": kind for i, kind in enumerate(Gather.scratch(1))}
    names = list(ins) + list(outs) + list(scratch)
    results = pl.pallas_call(
        lambda *refs: backward_kernel(names, *refs),
        out_shape=tuple(jax.ShapeDtypeStruct(shape, F32) for shape in outs.values()),
        in_specs=[vmem] * 4 + [any_space] * len(fetched),
        out_specs=(vmem,) * len(outs),
        scratch_shapes=list(scratch.values()),
        compiler_params=pltpu.CompilerParams(
            collective_id=2, has_side_effects=True, vmem_limit_bytes=VMEM_LIMIT
        ),
        name="backward",
    )(*ins.values())
    return dict(zip(outs, results))


def deliver_kernel(count, *refs):
    src, out, buf = refs[:count], refs[count : 2 * count], refs[2 * count : 3 * count]
    coming, going = refs[3 * count :]
    copies = []
    for i in sorted(range(count), key=lambda i: -math.prod(src[i].shape)):
        rows = src[i].shape[0]
        step = rows // 2 if rows >= 512 else rows
        for start in range(0, rows, step):
            at = pl.ds(start, min(step, rows - start))
            k = len(copies)
            copies.append((
                pltpu.make_async_copy(src[i].at[at], buf[i].at[at], coming.at[k]),
                pltpu.make_async_copy(buf[i].at[at], out[i].at[at], going.at[k]),
            ))
    for first, _ in copies:
        first.start()
    for first, second in copies:
        first.wait()
        second.start()
    for _, second in copies:
        second.wait()


def deliver(results):
    count = len(results)
    any_space = pl.BlockSpec(memory_space=pl.ANY)
    dma = pltpu.SemaphoreType.DMA((2 * count + 2,))
    return pl.pallas_call(
        lambda *refs: deliver_kernel(count, *refs),
        out_shape=tuple(jax.ShapeDtypeStruct(r.shape, r.dtype) for r in results),
        in_specs=[any_space] * count,
        out_specs=(any_space,) * count,
        scratch_shapes=[pltpu.VMEM(r.shape, r.dtype) for r in results] + [dma, dma],
        compiler_params=pltpu.CompilerParams(vmem_limit_bytes=VMEM_LIMIT),
        name="deliver",
    )(*results)


def norm_parts(rows):
    centre = rows - jnp.mean(rows, axis=-1, keepdims=True)
    inverse = lax.rsqrt(jnp.mean(centre * centre, axis=-1, keepdims=True) + EPS)
    return centre * inverse, inverse


def norm_back(grad, normed, inverse, scale):
    shift_grad = jnp.sum(grad, axis=1)
    scale_grad = jnp.sum(grad * normed, axis=1)
    pulled = grad * (1.0 + scale)
    back = inverse * (
        pulled
        - jnp.mean(pulled, axis=-1, keepdims=True)
        - normed * jnp.mean(pulled * normed, axis=-1, keepdims=True)
    )
    return back, shift_grad, scale_grad


def heads(x):
    return x.reshape(x.shape[0], x.shape[1], HEADS, HD)


def attention(low, qkv_w, proj_w, mask):
    packed = dot(low, qkv_w).astype(BF16)
    q, k, v = (heads(part) for part in jnp.split(packed, 3, axis=-1))
    scores = jnp.einsum("bqhd,bkhd->bhqk", q, k, preferred_element_type=F32) * HD ** (-0.5)
    scores = jnp.where(mask, scores, MASKED)
    soft = jax.nn.softmax(scores, axis=-1)
    context = jnp.einsum("bhqk,bkhd->bqhd", soft.astype(BF16), v, preferred_element_type=F32)
    context = context.astype(BF16).reshape(low.shape)
    return dot(context, proj_w), (q, k, v, soft, context)


def attention_back(grad_low, low, qkv_w, proj_w, kept):
    q, k, v, soft, context = kept
    proj_grad = jnp.einsum("bld,ble->de", context, grad_low, preferred_element_type=F32)
    ctx = heads(jnp.einsum("ble,de->bld", grad_low, proj_w, preferred_element_type=F32).astype(BF16))
    v_grad = jnp.einsum("bhqk,bqhd->bkhd", soft.astype(BF16), ctx, preferred_element_type=F32)
    soft_grad = jnp.einsum("bqhd,bkhd->bhqk", ctx, v, preferred_element_type=F32)
    row_dot = jnp.sum(soft_grad * soft, axis=-1, keepdims=True)
    score_grad = (soft * (soft_grad - row_dot)).astype(BF16)
    q_grad = jnp.einsum("bhqk,bkhd->bqhd", score_grad, k, preferred_element_type=F32) * HD ** (-0.5)
    k_grad = jnp.einsum("bhqk,bqhd->bkhd", score_grad, q, preferred_element_type=F32) * HD ** (-0.5)
    packed = jnp.concatenate(
        [part.astype(BF16).reshape(low.shape) for part in (q_grad, k_grad, v_grad)], axis=-1
    )
    qkv_grad = jnp.einsum("bld,ble->de", low, packed, preferred_element_type=F32)
    low_grad = jnp.einsum("ble,de->bld", packed, qkv_w, preferred_element_type=F32)
    return low_grad, qkv_grad, proj_grad


def gather_plain(shards):
    return tuple(lax.all_gather(s, AXES, axis=0) for s in shards)


def scatter_plain(parts, small):
    devices = lax.axis_size(AXES)
    sums = tuple(
        lax.psum_scatter(p.reshape((devices,) + p.shape[-2:]), AXES, scatter_dimension=0, tiled=True)[
            0
        ].astype(F32)
        for p in parts
    )
    return sums + (lax.all_gather(small, AXES, axis=0),)


def per_device_plain(latents, buckets, step_ids, qs, ps, qt, pt, up, down, ada, biases, cotangent):
    devices = lax.axis_size(AXES)
    micro = latents.shape[0]
    frames, spatial = latents.shape[2], latents.shape[3]
    tokens = frames * spatial
    rows = D // devices

    gather, scatter = gather_plain, scatter_plain

    ada_columns = lax.all_to_all(
        ada.reshape(rows, 9 * D), AXES, split_axis=1, concat_axis=0, tiled=True
    )
    own_bias = jnp.pad(biases, (0, D - biases.shape[0]))[None]
    small = jnp.concatenate([timestep_condition(step_ids[:, 0]), own_bias], axis=0)
    shards = [small] + [w.reshape(rows, -1) for w in (qs, ps, qt, pt, up)] + [down.reshape(-1, D)]
    small, *gathered = gather(shards)
    w_qs, w_ps, w_qt, w_pt, w_up = (w.reshape(D, -1) for w in gathered[:5])
    w_down = gathered[5].reshape(-1, D)
    small = small.reshape(devices, micro + 1, D)
    condition = small[:, :micro].reshape(devices * micro, D)
    bias = small[:, micro, : biases.shape[0]].reshape(-1).astype(F32)
    modulation = lax.all_to_all(
        dot(condition, ada_columns), AXES, split_axis=0, concat_axis=1, tiled=True
    )
    modulation = (modulation + bias[: 9 * D]).reshape(micro, 9, 1, D)
    b_up, b_down = bias[9 * D : 9 * D + FF], bias[9 * D + FF :]

    positions = jnp.arange(tokens)
    frame, place = positions // spatial, positions % spatial
    bucket = buckets[:, 0]
    length = jnp.where(bucket == 0, spatial, jnp.where(bucket == 1, spatial // 2, spatial // 8))
    valid = place[None, :] < length[:, None]
    space_mask = (frame[:, None] == frame[None, :])[None, None] & valid[:, None, None, :]
    time_mask = (place[:, None] == place[None, :])[None, None]
    valid_rows = valid.astype(F32)[:, :, None]

    sh1, sc1, ga1, sh2, sc2, ga2, sh3, sc3, ga3 = (modulation[:, i] for i in range(9))
    x = latents.reshape(micro, tokens, D).astype(F32)
    n1, r1 = norm_parts(x)
    h1 = (n1 * (1.0 + sc1) + sh1).astype(BF16)
    a1, kept1 = attention(h1, w_qs, w_ps, space_mask)
    x1 = x + ga1 * a1
    n2, r2 = norm_parts(x1)
    h2 = (n2 * (1.0 + sc2) + sh2).astype(BF16)
    a2, kept2 = attention(h2, w_qt, w_pt, time_mask)
    x2 = x1 + ga2 * a2
    n3, r3 = norm_parts(x2)
    h3 = (n3 * (1.0 + sc3) + sh3).astype(BF16)
    hidden = dot(h3, w_up) + b_up
    gelu, pull = jax.vjp(lambda u: jax.nn.gelu(u, approximate=True), hidden)
    g = gelu.astype(BF16)
    m = dot(g, w_down) + b_down
    x3 = x2 + ga3 * m
    output = (x3 * valid_rows).astype(BF16)

    d3 = cotangent.reshape(micro, tokens, D).astype(F32) * valid_rows
    dm = (ga3 * d3).astype(BF16)
    dga3 = jnp.sum(d3 * m, axis=1)
    db_down = jnp.sum(dm.astype(F32), axis=(0, 1))
    dw_down = jnp.einsum("bsk,bsd->kd", g, dm, preferred_element_type=F32)
    dg = jnp.einsum("bsd,kd->bsk", dm, w_down, preferred_element_type=F32)
    du = pull(dg)[0].astype(BF16)
    db_up = jnp.sum(du.astype(F32), axis=(0, 1))
    dw_up = jnp.einsum("bsd,bsk->dk", h3, du, preferred_element_type=F32)
    dh3 = jnp.einsum("bsk,dk->bsd", du, w_up, preferred_element_type=F32)
    dv, dsh3, dsc3 = norm_back(dh3, n3, r3, sc3)
    d2 = d3 + dv
    da2 = (ga2 * d2).astype(BF16)
    dga2 = jnp.sum(d2 * a2, axis=1)
    dh2, dw_qt, dw_pt = attention_back(da2, h2, w_qt, w_pt, kept2)
    dv, dsh2, dsc2 = norm_back(dh2, n2, r2, sc2)
    d1 = d2 + dv
    da1 = (ga1 * d1).astype(BF16)
    dga1 = jnp.sum(d1 * a1, axis=1)
    dh1, dw_qs, dw_ps = attention_back(da1, h1, w_qs, w_ps, kept1)
    dv, dsh1, dsc1 = norm_back(dh1, n1, r1, sc1)
    latents_grad = d1 + dv

    dmod = jnp.stack([dsh1, dsc1, dga1, dsh2, dsc2, dga2, dsh3, dsc3, dga3], axis=1)
    small = jnp.concatenate(
        [dmod.reshape(micro * 9, D), db_up.reshape(-1, D), db_down.reshape(-1, D)], axis=0
    ).astype(BF16)
    parts = [
        part.astype(BF16).reshape(tuple(gathered[i].shape))
        for i, part in ((5, dw_down), (4, dw_up), (3, dw_pt), (2, dw_qt), (1, dw_ps), (0, dw_qs))
    ]
    ddown, dup, dpt, dqt, dps, dqs, small = scatter(parts, small)
    flat = tuple(part.reshape(-1) for part in (dqs, dps, dqt, dpt, dup))
    small = small.reshape(devices, -1, D)
    dmod_all = small[:, : micro * 9].reshape(devices * micro, 9 * D)
    me = lax.axis_index(AXES)
    my_condition = lax.dynamic_slice_in_dim(condition, me * rows, rows, axis=1)
    dw_ada = lax.dot_general(
        my_condition, dmod_all, (((0,), (0,)), ((), ())), preferred_element_type=F32
    )
    db = jnp.concatenate(
        [
            jnp.sum(dmod_all.astype(F32), axis=0),
            jnp.sum(small[:, micro * 9 :].astype(F32), axis=0).reshape(-1),
        ]
    )
    db = lax.dynamic_slice_in_dim(db, me * biases.shape[0], biases.shape[0])

    shape = latents.shape
    return (
        output.reshape(shape),
        latents_grad.reshape(shape),
        *flat,
        ddown.reshape(-1),
        dw_ada.reshape(-1),
        db,
    )


def per_device(latents, buckets, step_ids, qs, ps, qt, pt, up, down, ada, biases, cotangent):
    rows = 2 * TOKENS
    conditions = timestep_condition(step_ids[:, 0])
    shards = [w.reshape(-1, 128) for w in (qs, ps, qt, pt, up, down)]
    tokens = latents.reshape(rows, D)
    grads_in = cotangent.reshape(rows, D)
    output, dga3, chosen, kept = run_forward(
        conditions, biases.reshape(1, -1), buckets, ada.reshape(-1, 128), shards, tokens, grads_in
    )
    grads = run_backward(grads_in, buckets, dga3, chosen, kept)
    me = lax.axis_index(AXES)
    bias_grad = grads["grad_bias"][:14].reshape(-1)
    names = ["d"] + ["grad_" + t for t in ("qs", "ps", "qt", "pt", "up", "down", "ada")]
    output, latents_grad, *flat = deliver([output] + [grads[name] for name in names])
    return (
        output.reshape(latents.shape),
        latents_grad.reshape(latents.shape),
        *(g.reshape(-1) for g in flat),
        lax.dynamic_slice_in_dim(bias_grad, me * SHARE, SHARE),
    )


def solution(mesh):
    items = P(None, AXES, None, None, None)
    flat = P(AXES)
    known = mesh.shape["wide"] == 8 and mesh.shape["narrow"] == 4
    return jax.shard_map(
        per_device if known else per_device_plain,
        mesh=mesh,
        in_specs=(items, P(None, AXES), P(None, AXES)) + (flat,) * 8 + (items,),
        out_specs=(items, items) + (flat,) * 8,
        check_vma=False,
    )
```

```python
import math

import jax
import jax.numpy as jnp
from jax import lax
from jax.experimental import pallas as pl
from jax.experimental.pallas import tpu as pltpu
from jax.sharding import PartitionSpec as P

D = 768
HEADS = 12
HD = 64
FF = 3072
AXES = ("wide", "narrow")
EPS = 1e-06
MASKED = -1e30
F32 = jnp.float32
BF16 = jnp.bfloat16
GELU = math.sqrt(2.0 / math.pi)
MESH = pl.DeviceIdType.MESH
DEVICES = 32
OWNERS = 9 * D // 256
SHARE = (10 * D + FF) // DEVICES
SPATIAL = 16
TOKENS = 256
VMEM_LIMIT = 67_000_000


def dot(a, b):
    return jnp.dot(a, b, preferred_element_type=F32)


def place():
    w, z = lax.axis_index("wide"), lax.axis_index("narrow")
    return w // 4, (w // 2) % 2, w % 2, z


def device_at(y, x, c, z):
    return {"wide": (y * 2 + x) * 2 + c, "narrow": z}


def remote(src, dst, send, recv, target):
    return pltpu.make_async_remote_copy(
        src_ref=src, dst_ref=dst, send_sem=send, recv_sem=recv,
        device_id=target, device_id_type=MESH,
    )


class Sender:
    def __init__(self):
        self.copies = []

    def go(self, src, dst, send, recv, target):
        copy = remote(src, dst, send, recv, target)
        copy.start()
        self.copies.append(copy)

    def drain(self):
        for copy in self.copies:
            copy.wait_send()


def timestep_condition(step_values):
    half_width = D // 2
    frequency = jnp.exp(-math.log(10000.0) * jnp.arange(half_width, dtype=F32) / half_width)
    angles = step_values.astype(F32)[:, None] * frequency
    return jax.nn.silu(jnp.concatenate([jnp.cos(angles), jnp.sin(angles)], axis=-1)).astype(BF16)


class Gather:
    SEMAPHORES = (3, 3, 10, 10, 3, 3, 3, 3)

    def __init__(self, here, sender, own, out, semaphores, local):
        self.here, self.sender, self.own, self.out, self.local = here, sender, own, out, local
        self.zs, self.zr, self.cs, self.cr, self.xs, self.xr, self.ys, self.yr = semaphores
        y, x, c, z = here
        self.sib = device_at(y, x, 1 - c, z)
        self.xn = device_at(y, 1 - x, c, z)
        self.yn = device_at(1 - y, x, c, z)

    @staticmethod
    def scratch(count):
        kinds = [pltpu.SemaphoreType.DMA((count, k)) for k in Gather.SEMAPHORES]
        return kinds + [pltpu.SemaphoreType.DMA((count,))]

    def start(self, i):
        y, x, c, z = self.here
        mine = self.out[i].at[y, x, c, z]
        for step in (2, 1, 3):
            self.sender.go(
                self.own[i], mine, self.zs.at[i, step - 1],
                self.zr.at[i, step - 1], device_at(y, x, c, (z + step) % 4),
            )
        pltpu.make_async_copy(self.own[i], mine, self.local.at[i]).start()
        self.sender.go(self.own[i], mine, self.cs.at[i, 0], self.cr.at[i, 0], self.sib)

    def along(self, ref, send, recv, target):
        self.sender.go(ref, ref, send, recv, target)

    def arrived(self, ref, send, recv):
        remote(ref, ref, send, recv, self.sib).wait_recv()

    def across(self, i, k, ref):
        self.sender.go(ref, ref, self.cs.at[i, k], self.cr.at[i, k], self.sib)

    def stage1(self, i):
        y, x, c, z = self.here
        out = self.out[i]
        pltpu.make_async_copy(self.own[i], out.at[y, x, c, z], self.local.at[i]).wait()
        for step in (1, 2, 3):
            self.arrived(out.at[y, x, c, (z + 4 - step) % 4], self.zs.at[i, step - 1], self.zr.at[i, step - 1])
        low, high = out.at[y, x, c, pl.ds(0, 2)], out.at[y, x, c, pl.ds(2, 2)]
        self.along(low, self.xs.at[i, 0], self.xr.at[i, 0], self.xn)
        self.along(high, self.ys.at[i, 0], self.yr.at[i, 0], self.yn)
        self.along(high, self.xs.at[i, 1], self.xr.at[i, 1], self.xn)
        self.along(low, self.ys.at[i, 1], self.yr.at[i, 1], self.yn)
        for step in (1, 2, 3):
            self.across(i, step, out.at[y, x, c, (z + 4 - step) % 4])

    def stage2(self, i):
        y, x, c, z = self.here
        low_x = self.out[i].at[y, 1 - x, c, pl.ds(0, 2)]
        high_y = self.out[i].at[1 - y, x, c, pl.ds(2, 2)]
        self.arrived(low_x, self.xs.at[i, 0], self.xr.at[i, 0])
        self.along(low_x, self.ys.at[i, 2], self.yr.at[i, 2], self.yn)
        self.arrived(high_y, self.ys.at[i, 0], self.yr.at[i, 0])
        self.along(high_y, self.xs.at[i, 2], self.xr.at[i, 2], self.xn)
        self.across(i, 4, low_x)
        self.across(i, 5, high_y)

    def stage3(self, i):
        y, x, c, z = self.here
        out = self.out[i]
        arrivals = (
            (out.at[y, 1 - x, c, pl.ds(2, 2)], self.xs.at[i, 1], self.xr.at[i, 1]),
            (out.at[1 - y, x, c, pl.ds(0, 2)], self.ys.at[i, 1], self.yr.at[i, 1]),
            (out.at[1 - y, 1 - x, c, pl.ds(2, 2)], self.xs.at[i, 2], self.xr.at[i, 2]),
            (out.at[1 - y, 1 - x, c, pl.ds(0, 2)], self.ys.at[i, 2], self.yr.at[i, 2]),
        )
        for k, (ref, send, recv) in enumerate(arrivals):
            self.arrived(ref, send, recv)
            self.across(i, 6 + k, ref)

    def finish(self, i):
        y, x, c, z = self.here
        o = 1 - c
        out = self.out[i]
        arrivals = [out.at[y, x, o, (z + 4 - step) % 4] for step in (0, 1, 2, 3)]
        arrivals += [
            out.at[y, 1 - x, o, pl.ds(0, 2)],
            out.at[1 - y, x, o, pl.ds(2, 2)],
            out.at[y, 1 - x, o, pl.ds(2, 2)],
            out.at[1 - y, x, o, pl.ds(0, 2)],
            out.at[1 - y, 1 - x, o, pl.ds(2, 2)],
            out.at[1 - y, 1 - x, o, pl.ds(0, 2)],
        ]
        for k, ref in enumerate(arrivals):
            self.arrived(ref, self.cs.at[i, k], self.cr.at[i, k])


class Spread:
    SEMAPHORES = (3, 3, 6, 6, 6, 6, 2, 2, 16, 16)

    def __init__(self, here, own, out, semaphores, local, pairs):
        self.here, self.own, self.out, self.local = here, own, out, local
        self.pairs = pairs
        self.zs, self.zr, self.xs, self.xr, self.ys, self.yr, self.ps, self.pr, self.cs, self.cr = semaphores
        self.sent = []
        y, x, c, z = here
        self.sib = device_at(y, x, 1 - c, z)
        self.xn = device_at(y, 1 - x, c, z)
        self.yn = device_at(1 - y, x, c, z)
        self.partner = z + 1 - 2 * (z % 2)
        self.opposite = (z + 2) % 4
        self.zp = device_at(y, x, c, self.partner)

    @staticmethod
    def scratch(count):
        kinds = [pltpu.SemaphoreType.DMA((count, k)) for k in Spread.SEMAPHORES]
        return kinds + [pltpu.SemaphoreType.DMA((count,))]

    def go(self, i, k, src, dst, send, recv, target):
        remote(src, dst, send.at[i, k], recv.at[i, k], target).start()
        self.sent.append((i, k, send, recv))

    def drain(self):
        for i, k, send, recv in self.sent:
            remote(self.own[i], self.own[i], send.at[i, k], recv.at[i, k], self.sib).wait_send()

    def to_x(self, i, k, ref):
        self.go(i, k, ref, ref, self.xs, self.xr, self.xn)

    def to_y(self, i, k, ref):
        self.go(i, k, ref, ref, self.ys, self.yr, self.yn)

    def across(self, i, k, ref):
        self.go(i, k, ref, ref, self.cs, self.cr, self.sib)

    def arrived(self, ref, send, recv):
        remote(ref, ref, send, recv, self.sib).wait_recv()

    def from_z(self, step):
        return (self.here[3] + 4 - step) % 4

    def beside(self, i):
        y, x, c, z = self.here
        own, mine = self.own[i], self.out[i].at[y, x, c, z]
        pltpu.make_async_copy(own, mine, self.local.at[i]).start()
        self.go(i, 0, own, mine, self.xs, self.xr, self.xn)
        self.go(i, 0, own, mine, self.ys, self.yr, self.yn)
        self.go(i, 0, own, mine, self.cs, self.cr, self.sib)

    def along(self, i):
        y, x, c, z = self.here
        own, mine = self.own[i], self.out[i].at[y, x, c, z]
        for step in (2, 1, 3):
            there = device_at(y, x, c, (z + step) % 4)
            self.go(i, step - 1, own, mine, self.zs, self.zr, there)

    def column(self, i):
        y, x, c, z = self.here
        for step in (2, 1, 3):
            ref = self.out[i].at[y, x, c, self.from_z(step)]
            self.arrived(ref, self.zs.at[i, step - 1], self.zr.at[i, step - 1])
            self.to_x(i, step, ref)
            self.to_y(i, step, ref)
            self.across(i, step, ref)

    def sides(self, i):
        y, x, c, z = self.here
        for step in (0, 2, 1, 3):
            from_x = self.out[i].at[y, 1 - x, c, self.from_z(step)]
            self.arrived(from_x, self.xs.at[i, step], self.xr.at[i, step])
            if step == 0 or step == 2 and not self.pairs[i]:
                self.to_y(i, 4 + step // 2, from_x)
            self.across(i, 4 + step, from_x)
            from_y = self.out[i].at[1 - y, x, c, self.from_z(step)]
            self.arrived(from_y, self.ys.at[i, step], self.yr.at[i, step])
            if step == 2 and self.pairs[i]:
                self.to_x(i, 4, from_y)
            if step % 2 and not self.pairs[i]:
                self.to_x(i, 4 + step // 2, from_y)
            self.across(i, 8 + step, from_y)

    def diagonal(self, i):
        y, x, c, z = self.here
        where = self.out[i].at[1 - y, 1 - x, c]
        blocks = self.corner(i)
        if self.pairs[i]:
            lanes = ((self.ys, self.yr, 4), (self.xs, self.xr, 4))
        else:
            lanes = ((self.ys, self.yr, 4), (self.ys, self.yr, 5), (self.xs, self.xr, 4), (self.xs, self.xr, 5))
        for k, (send, recv, n) in enumerate(lanes):
            ref = where.at[blocks[k]]
            self.arrived(ref, send.at[i, n], recv.at[i, n])
            if self.pairs[i]:
                self.go(i, k, ref, ref, self.ps, self.pr, self.zp)
            self.across(i, 12 + k, ref)

    def corner(self, i):
        if self.pairs[i]:
            return self.here[3], self.opposite, self.partner, (self.partner + 2) % 4
        return self.from_z(0), self.from_z(2), self.from_z(1), self.from_z(3)

    def pair(self, i):
        y, x, c, z = self.here
        where = self.out[i].at[1 - y, 1 - x, c]
        for k, block in enumerate(self.corner(i)[2:] if self.pairs[i] else ()):
            ref = where.at[block]
            self.arrived(ref, self.ps.at[i, k], self.pr.at[i, k])
            self.across(i, 14 + k, ref)

    def finish(self, i):
        y, x, c, z = self.here
        out, o = self.out[i], 1 - c
        pltpu.make_async_copy(self.own[i], out.at[y, x, c, z], self.local.at[i]).wait()
        arrivals = [out.at[y, x, o, self.from_z(step)] for step in range(4)]
        arrivals += [out.at[y, 1 - x, o, self.from_z(step)] for step in range(4)]
        arrivals += [out.at[1 - y, x, o, self.from_z(step)] for step in range(4)]
        arrivals += [out.at[1 - y, 1 - x, o, block] for block in self.corner(i)]
        for k, ref in enumerate(arrivals):
            self.arrived(ref, self.cs.at[i, k], self.cr.at[i, k])


PAIRED = (True, True, False, True, True, True, False, False)
SPREAD_STEPS = (
    (("A", 0), ("B", 0), ("A", 6),), (), (), (), (("A", 2),), (), (("A", 4), ("A", 7),), (), (),
    (("A", 1), ("B", 1), ("A", 3),), (), (("C", 0),), (("B", 2),), (), (("B", 4),), (("B", 3), ("C", 1),), (), (),
    (("X", 0), ("X", 1), ("C", 2), ("D", 0), ("D", 1), ("C", 4), ("P", 0),),
    (("B", 5), ("B", 6), ("P", 1), ("X", 2), ("C", 3),), (), (), (("B", 7), ("X", 4),), (),
    (("D", 2), ("A", 5), ("C", 5),), (("X", 3),), (), (("D", 4),), (), (("C", 6),), (), (),
    (("X", 5), ("P", 4), ("D", 3),), (("C", 7),), (("P", 3),), (("D", 5), ("X", 6),), (), (), (),
    (("P", 5), ("X", 7),), (), (), (("D", 6),), (("D", 7),), (), (),
)


class Steps:
    def __init__(self, calls, table):
        self.calls, self.table = calls, list(table)

    def run(self, steps):
        for kind, i in steps:
            self.calls[kind](i)

    def __call__(self):
        self.run(self.table.pop(0))

    def rolled(self, count, *parts):
        due = [[self.table.pop(0) if k % every == every - 1 else () for _, _, every in parts] for k in range(count)]

        def turn(j, _):
            for n, (body, also, _) in enumerate(parts):
                body(j)
                for k in range(count):
                    if k in also or due[k][n]:
                        @pl.when(j == k)
                        def _(k=k, n=n, also=also):
                            if k in also:
                                also[k]()
                            self.run(due[k][n])

            return 0

        lax.fori_loop(0, count, turn, 0)


class Names:
    def __init__(self, names, refs):
        for name, ref in zip(names, refs, strict=True):
            setattr(self, name, ref)


def rows_of(item, step, size):
    return pl.ds(pl.multiple_of(item * TOKENS + step * size, size), size)


def lane_cols(start, size=128):
    return pl.ds(start if isinstance(start, int) else pl.multiple_of(start, 128), size)


def dot_t(a, b):
    return lax.dot_general(a, b, (((1,), (1,)), ((), ())), preferred_element_type=F32)


def t_dot(a, b):
    return lax.dot_general(a, b, (((0,), (0,)), ((), ())), preferred_element_type=F32)


def weight_block(ref, start, size):
    cols = ref[:, :, :, :, :, lane_cols(start, size)]
    return cols.reshape(-1, size)


def two_heads(x, scale):
    lane = lax.broadcasted_iota(jnp.int32, x.shape, 1)
    x = x * jnp.asarray(scale, x.dtype)
    zero = jnp.zeros_like(x)
    return jnp.concatenate([jnp.where(lane < HD, x, zero), jnp.where(lane >= HD, x, zero)], axis=0)


def pick_heads(first, second):
    lane = lax.broadcasted_iota(jnp.int32, first.shape, 1)
    return jnp.where(lane < HD, first, second)


def norm_rows(v):
    centre = v - jnp.mean(v, axis=-1, keepdims=True)
    inverse = lax.rsqrt(jnp.mean(centre * centre, axis=-1, keepdims=True) + EPS)
    return centre * inverse, inverse


CHUNK = 32
PAIRS = HEADS // 2
TENSORS = ("qs", "ps", "qt", "pt", "up", "down")
PIECES = (("qs", 0, 3 * D), ("ps", 0, D), ("qt", 0, 3 * D), ("pt", 0, D))
PIECES += tuple((t, k * n, n) for t, n in (("up", FF // 2), ("down", D // 2)) for k in range(2))


def save_shapes(tokens):
    rows = 2 * tokens
    attention = {
        "n": ((rows, D), BF16), "r": ((rows, 1), F32), "h": ((rows, D), BF16),
        "q": ((rows, 3 * D), BF16), "p": ((rows, 2 * PAIRS * tokens), BF16),
        "c": ((rows, D), BF16), "a": ((rows, D), BF16),
    }
    out = {}
    for k in (1, 2):
        out.update({name + str(k): spec for name, spec in attention.items()})
    out.update({
        "n3": ((rows, D), BF16), "r3": ((rows, 1), F32), "h3": ((rows, D), BF16),
        "g": ((rows, FF), BF16), "gp": ((rows, FF), BF16), "mods": ((9, 8, D), F32),
    })
    return out


def unflatten(s, flat, own):
    rows, size = own.shape
    stride = size // 128
    s.stage[pl.ds(0, flat.shape[0]), :] = flat[...].astype(F32)
    for k in range(stride):
        own[:, k * 128 : (k + 1) * 128] = s.stage[pl.ds(k, rows, stride=stride), :].astype(BF16)


def lengths(buckets):
    return jnp.where(buckets == 0, SPATIAL, jnp.where(buckets == 1, SPATIAL // 2, SPATIAL // 8))


def valid_rows(s):
    length = lengths(s.buckets[...])
    spot = lax.broadcasted_iota(jnp.int32, (TOKENS, 1), 0) % SPATIAL
    for item in range(2):
        s.valid[item * TOKENS : (item + 1) * TOKENS, :] = (spot < length[item : item + 1, :]).astype(F32)


def norm_into(s, k, shift, scale, rows, item, v):
    n, r = norm_rows(v)
    getattr(s, "n" + k)[rows, :] = n.astype(BF16)
    getattr(s, "r" + k)[rows, :] = r
    h = n * (1.0 + s.mods[scale, item : item + 1, :]) + s.mods[shift, item : item + 1, :]
    getattr(s, "h" + k)[rows, :] = h.astype(BF16)


def project(s, k, weight, point):
    h, q = getattr(s, "h" + k), getattr(s, "q" + k)

    def column(j):
        q[:, lane_cols(j * D, D)] = dot(h[...], weight_block(weight, j * D, D)).astype(BF16)

    point.rolled(3, (column, {}, 1))


def attend(s, k, bias_of, first):
    q, p, c = getattr(s, "q" + k), getattr(s, "p" + k), getattr(s, "c" + k)

    def body(t, _):
        step = first + t
        item, pair = step // PAIRS, step % PAIRS
        rows = pl.ds(pl.multiple_of(item * TOKENS, TOKENS), TOKENS)
        at = [lane_cols(pair * 128 + j * D) for j in range(3)]
        scores = dot_t(two_heads(q[rows, at[0]], HD ** (-0.5)), q[rows, at[1]])
        scores = (scores.reshape(2, TOKENS, TOKENS) + bias_of(item)).reshape(2 * TOKENS, TOKENS)
        expanded = jnp.exp(scores - jnp.max(scores, axis=-1, keepdims=True))
        soft = (expanded * (1.0 / jnp.sum(expanded, axis=-1, keepdims=True))).astype(BF16)
        p[:, lane_cols(step * TOKENS, TOKENS)] = soft
        context = dot(soft, q[rows, at[2]])
        c[rows, at[0]] = pick_heads(context[:TOKENS], context[TOKENS:]).astype(BF16)
        return 0

    lax.fori_loop(0, PAIRS // 2, body, 0)


def after_attention(s, k, next_k, weight, gate, shift, scale):
    s.acc[...] = dot(getattr(s, "c" + k)[...], weight_block(weight, 0, D))
    for item in range(2):
        def body(t, _):
            rows = rows_of(item, t, CHUNK)
            a = s.acc[rows, :]
            v = s.x[rows, :] + s.mods[gate, item : item + 1, :] * a
            s.x[rows, :] = v
            getattr(s, "a" + k)[rows, :] = a.astype(BF16)
            norm_into(s, next_k, shift, scale, rows, item, v)
            return 0

        lax.fori_loop(0, TOKENS // CHUNK, body, 0)


def flat_bias(s):
    s.bias[...] = jnp.zeros_like(s.bias)
    for d in range(DEVICES):
        y, x, c, z = d // 16, (d // 8) % 2, (d // 4) % 2, d % 4
        piece = s.small_all[y, x, c, z].astype(F32)[2:3, :512]
        lane = lax.broadcasted_iota(jnp.int32, piece.shape, 1)
        piece = jnp.where(lane < SHARE, piece, 0.0)
        start = d * SHARE
        if start % 128:
            piece = pltpu.roll(piece, start % 128, 1)
        low = start // 128 * 128
        s.bias[:, low : low + 512] = s.bias[:, low : low + 512] + piece


def forward_kernel(names, *refs):
    s = Names(names, refs)
    here = place()
    y, x, c, z = here
    me = ((y * 2 + x) * 2 + c) * 4 + z
    sender = Sender()
    weights = [getattr(s, "w_" + t).at[:, :, :, :, :, pl.ds(at, size)] for t, at, size in PIECES]
    own = [getattr(s, "own_" + t).at[:, pl.ds(at, size)] for t, at, size in PIECES]
    gather = Spread(here, own, weights, [getattr(s, f"gs{i}") for i in range(10)], s.gs10, PAIRED)
    calls = {"A": gather.beside, "B": gather.along, "C": gather.column}
    calls |= {"X": gather.sides, "D": gather.diagonal, "P": gather.pair}
    point = Steps(calls, SPREAD_STEPS)
    little = Gather(here, sender, [s.small], [s.small_all], [getattr(s, f"ls{i}") for i in range(8)], s.ls8)
    saves = []

    def save(*names):
        for name in names:
            copy = pltpu.make_async_copy(getattr(s, name), getattr(s, "out_" + name), s.save_sem.at[len(saves)])
            copy.start()
            saves.append(copy)

    def target(k):
        d = (me + k) % DEVICES
        return d, {"wide": d // 4, "narrow": d % 4}

    barrier = pltpu.get_barrier_semaphore()

    def signal(k, _):
        pl.semaphore_signal(barrier, inc=1, device_id=target(k)[1], device_id_type=MESH)
        return 0

    lax.fori_loop(1, DEVICES, signal, 0)
    s.little[...] = jnp.zeros_like(s.little)
    s.little[0:2, :] = s.conditions[...].astype(F32)
    s.little[2:3, :SHARE] = s.biases[...].astype(F32)
    s.small[...] = s.little[...].astype(BF16)
    unflatten(s, s.flat_ada, s.ada)
    pl.semaphore_wait(barrier, DEVICES - 1)

    def columns_copy(k):
        d, there = target(k)
        src = s.ada.at[:, lane_cols(d * 256, 256)]
        return d, remote(src, s.ada_cols.at[me], s.a_send.at[k], s.a_recv.at[me], there)

    little.start(0)

    def send_columns(k, _):
        d, copy = columns_copy(k)

        @pl.when(d < OWNERS)
        def _():
            copy.start()

        return 0

    lax.fori_loop(1, DEVICES, send_columns, 0)
    owner = me < OWNERS
    mine = jnp.minimum(me, OWNERS - 1)
    own_columns = pltpu.make_async_copy(s.ada.at[:, lane_cols(mine * 256, 256)], s.ada_cols.at[me], s.own_sem.at[0])
    own_columns.start()
    for t in TENSORS:
        unflatten(s, getattr(s, "flat_" + t), getattr(s, "own_" + t))
    point()

    place_of = lambda n: lax.broadcasted_iota(jnp.int32, (TOKENS, TOKENS), n)
    same_frame = place_of(0) // SPATIAL == place_of(1) // SPATIAL
    same_place = place_of(0) % SPATIAL == place_of(1) % SPATIAL
    for item in range(2):
        seen = lax.broadcasted_iota(jnp.int32, (1, TOKENS), 1) % SPATIAL < lengths(s.buckets[...])[item : item + 1, :]
        s.space_bias[item] = jnp.where(same_frame, jnp.where(seen, 0.0, MASKED), MASKED)
    s.time_bias[...] = jnp.where(same_place, 0.0, MASKED)
    valid_rows(s)
    point()
    point()
    little.stage1(0)
    point()
    little.stage2(0)
    point()
    little.stage3(0)
    point()
    little.finish(0)
    point()
    own_columns.wait()

    def modulation_copy(k):
        d, there = target(k)
        src = s.mod_cols.at[pl.ds(pl.multiple_of(d * 8, 8), 8)]
        return remote(src, s.mod_all.at[me], s.m_send.at[k], s.m_recv.at[me], there)

    own_mod = pltpu.make_async_copy(
        s.mod_cols.at[pl.ds(pl.multiple_of(me * 8, 8), 8)], s.mod_all.at[mine], s.own_sem.at[1]
    )

    conditions = s.small_all[...].reshape(DEVICES * 8, D)
    point()

    @pl.when(owner)
    def _():
        def wait_columns(k, _):
            d, there = target(k)
            remote(s.ada_cols.at[d], s.ada_cols.at[d], s.a_send.at[k], s.a_recv.at[d], there).wait_recv()
            return 0

        lax.fori_loop(1, DEVICES, wait_columns, 0)
        s.mod_cols[...] = dot(conditions, s.ada_cols[...].reshape(D, 256))

        def send_modulation(k, _):
            modulation_copy(k).start()
            return 0

        lax.fori_loop(1, DEVICES, send_modulation, 0)
        own_mod.start()

    point()
    flat_bias(s)
    point()
    part = D // DEVICES
    spot = lambda shape, n: lax.broadcasted_iota(jnp.int32, shape, n)
    col = spot((D, 128), 1)
    wanted = (spot((D, 128), 0) == me * part + col) & (col < part)
    mine_only = dot(conditions, wanted.astype(F32).astype(BF16)).astype(BF16)
    row, item = spot((D, DEVICES * 8), 0), spot((D, DEVICES * 8), 1)
    slot = row % part
    copy_of = (row // part == item // 8) & (slot // 9 == item % 8) & (slot < 18)
    s.chosen[...] = dot(copy_of.astype(F32).astype(BF16), mine_only).astype(BF16)
    for _ in range(6):
        point()

    @pl.when(owner)
    def _():
        own_mod.wait()

    def wait_modulation(k, _):
        d, there = target(k)

        @pl.when(d < OWNERS)
        def _():
            remote(s.mod_all.at[d], s.mod_all.at[d], s.m_send.at[k], s.m_recv.at[d], there).wait_recv()

        return 0

    lax.fori_loop(1, DEVICES, wait_modulation, 0)
    for j in range(9):
        row = jnp.concatenate([s.mod_all[3 * j + i] for i in range(3)], axis=1)
        s.mods[j] = row + s.bias[:, j * D : (j + 1) * D]
    save("mods")

    for item in range(2):
        def first(t, _):
            rows = rows_of(item, t, CHUNK)
            v = s.latents[rows, :].astype(F32)
            s.x[rows, :] = v
            norm_into(s, "1", 0, 1, rows, item, v)
            return 0

        lax.fori_loop(0, TOKENS // CHUNK, first, 0)
        point()
    save("n1", "r1", "h1")

    def ready(i):
        point()
        gather.finish(i)
        t, at, size = PIECES[i]
        if at + size == getattr(s, "w_" + t).shape[-1]:
            save("w_" + t)

    ready(0)
    project(s, "1", s.w_qs, point)
    space = lambda item: s.space_bias[item]
    point.rolled(4, (lambda k: attend(s, "1", space, 3 * k), {}, 1))
    ready(1)
    after_attention(s, "1", "2", s.w_ps, 2, 3, 4)
    save("q1", "p1", "c1", "a1", "n2", "r2", "h2")
    point()
    ready(2)
    project(s, "2", s.w_qt, point)
    time = lambda item: s.time_bias[...]
    point.rolled(4, (lambda k: attend(s, "2", time, 3 * k), {}, 1))
    ready(3)
    after_attention(s, "2", "3", s.w_pt, 5, 6, 7)
    save("q2", "p2", "c2", "a2", "n3", "r3", "h3")
    point()
    ready(4)

    def up(j):
        cols = lane_cols(j * D, D)
        s.acc[...] = dot(s.h3[...], weight_block(s.w_up, j * D, D))
        b_up = s.bias[:, lane_cols((9 + j) * D, D)]

        def activate(t, _):
            rows = rows_of(0, t, CHUNK)
            u = s.acc[rows, :] + b_up
            square = u * u
            th = jnp.tanh(u * (GELU + (GELU * 0.044715) * square))
            half = 0.5 * u
            s.g[rows, cols] = (half + half * th).astype(BF16)
            slope = 0.5 + 0.5 * th + half * (1.0 - th * th) * (GELU + (3 * GELU * 0.044715) * square)
            s.gp[rows, cols] = slope.astype(BF16)
            return 0

        lax.fori_loop(0, 2 * TOKENS // CHUNK, activate, 0)

    point.rolled(2, (up, {}, 1))
    ready(5)
    point.rolled(2, (lambda j: up(2 + j), {}, 1))
    save("g", "gp")
    s.acc[...] = jnp.zeros_like(s.acc)
    for half in range(2):
        ready(6 + half)
        cols = slice(half * D // 2, (half + 1) * D // 2)

        def down(j, _):
            w = s.w_down[j // 2, j % 2, :, :, :, cols].reshape(D, D // 2)
            s.acc[:, cols] = s.acc[:, cols] + dot(s.g[:, lane_cols(j * D, D)], w)
            return 0

        lax.fori_loop(0, FF // D, down, 0)
    b_down = s.bias[:, (9 + FF // D) * D : (10 + FF // D) * D]
    for item in range(2):
        gate = s.mods[8, item : item + 1, :]

        def last(t, total):
            rows = rows_of(item, t, CHUNK)
            m = s.acc[rows, :] + b_down
            valid = s.valid[rows, :]
            s.output[rows, :] = ((s.x[rows, :] + gate * m) * valid).astype(BF16)
            d3 = s.cotangent[rows, :].astype(F32) * valid
            return total + jnp.sum((d3 * m).reshape(CHUNK // 8, 8, D), axis=0)

        total = lax.fori_loop(0, TOKENS // CHUNK, last, jnp.zeros((8, D), F32))
        s.dga3[item : item + 1, :] = jnp.sum(total, axis=0, keepdims=True)

    def drain(k, _):
        d, copy = columns_copy(k)

        @pl.when(d < OWNERS)
        def _():
            copy.wait_send()

        @pl.when(owner)
        def _():
            modulation_copy(k).wait_send()

        return 0

    lax.fori_loop(1, DEVICES, drain, 0)
    sender.drain()
    gather.drain()
    for copy in saves:
        copy.wait()


def run_forward(conditions, biases, buckets, ada, shards, latents, cotangent):
    vmem, any_space = pl.BlockSpec(memory_space=pltpu.VMEM), pl.BlockSpec(memory_space=pl.ANY)
    saved = save_shapes(TOKENS)
    part = D // DEVICES
    own = {t: (4 * part, D) if t == "down" else (part, WIDTHS[t]) for t in TENSORS}
    weights = {"w_" + t: ((2, 2, 2, 4) + own[t], BF16) for t in TENSORS}
    kept = {**saved, **weights}
    rows = 2 * TOKENS
    ins = ["conditions", "biases", "buckets", "flat_ada"] + ["flat_" + t for t in TENSORS] + ["latents", "cotangent"]
    outs = ["output", "dga3", "chosen"] + ["out_" + name for name in kept]
    dma = pltpu.SemaphoreType.DMA
    scratch = {name: pltpu.VMEM(*spec) for name, spec in kept.items()}
    scratch |= {"own_" + t: pltpu.VMEM(shape, BF16) for t, shape in own.items()}
    scratch |= {
        "small": pltpu.VMEM((8, D), BF16), "little": pltpu.VMEM((8, D), F32),
        "stage": pltpu.VMEM(ada.shape, F32), "ada": pltpu.VMEM((part, 9 * D), BF16),
        "valid": pltpu.VMEM((rows, 1), F32),
        "small_all": pltpu.VMEM((2, 2, 2, 4, 8, D), BF16),
        "ada_cols": pltpu.VMEM((DEVICES, part, 256), BF16),
        "mod_cols": pltpu.VMEM((DEVICES * 8, 256), F32),
        "mod_all": pltpu.VMEM((OWNERS, 8, 256), F32),
        "bias": pltpu.VMEM((1, DEVICES * SHARE + 512), F32),
        "x": pltpu.VMEM((rows, D), F32),
        "acc": pltpu.VMEM((rows, D), F32),
        "space_bias": pltpu.VMEM((2, TOKENS, TOKENS), F32),
        "time_bias": pltpu.VMEM((TOKENS, TOKENS), F32),
        "save_sem": dma((len(kept),)),
        "a_send": dma((DEVICES,)), "a_recv": dma((DEVICES,)),
        "m_send": dma((DEVICES,)), "m_recv": dma((DEVICES,)), "own_sem": dma((2,)),
    }
    scratch |= {f"gs{i}": kind for i, kind in enumerate(Spread.scratch(len(PIECES)))}
    scratch |= {f"ls{i}": kind for i, kind in enumerate(Gather.scratch(1))}
    names = ins + outs + list(scratch)
    results = pl.pallas_call(
        lambda *refs: forward_kernel(names, *refs),
        out_shape=(jax.ShapeDtypeStruct((rows, D), BF16), jax.ShapeDtypeStruct((2, D), F32), jax.ShapeDtypeStruct((D, 128), BF16))
        + tuple(jax.ShapeDtypeStruct(*spec) for spec in kept.values()),
        in_specs=[vmem] * len(ins),
        out_specs=(vmem,) * 3 + (any_space,) * len(kept),
        scratch_shapes=list(scratch.values()),
        compiler_params=pltpu.CompilerParams(
            collective_id=1, has_side_effects=True, vmem_limit_bytes=VMEM_LIMIT
        ),
        name="forward",
    )(conditions, biases, buckets, ada, *shards, latents, cotangent)
    return results[0], results[1], results[2], dict(zip(kept, results[3:]))


class Scatter:
    SEMAPHORES = ((), (), (2,), (2,), (4,), (4,), (4,), (4,), (4,), (4,), (3,), (3,))
    LEADING = ((2, 2, 4), (2,), (4,), (4,), (4,), (3,))

    def __init__(self, here, part, store, buffers, semaphores):
        self.here, self.part, self.store = here, part, store
        self.point = Steps({k: call for k, call in enumerate(self.stages())}, SCATTER_STEPS)
        self.r0, self.rp, self.rd, self.rx, self.ry, self.r3 = buffers
        self.cs, self.cr, self.ps, self.pr, self.ds, self.dr = semaphores[:6]
        self.xs, self.xr, self.ys, self.yr, self.zs, self.zr = semaphores[6:]
        y, x, c, z = here
        self.sib = device_at(y, x, 1 - c, z)
        self.xn = device_at(y, 1 - x, c, z)
        self.yn = device_at(1 - y, x, c, z)
        self.partner = z + 1 - 2 * (z % 2)
        self.opposite = (z + 2) % 4
        self.zp = device_at(y, x, c, self.partner)
        self.copies = [[] for _ in part]

    def stages(self):
        return self.chip, self.pair, self.diagonal, self.sides, self.last

    def by_y(self, i):
        return ((0,), (2,)) if SUMMED_IN_PAIRS[i] else ((0, 2), (1, 3))

    def hop(self, i, kind, k):
        y, x, c, z = self.here
        part = self.part[i]
        if kind == "c":
            return part.at[:, :, 1 - c], self.r0[i], self.cs.at[i], self.cr.at[i], self.sib
        if kind == "p":
            block = (self.partner + 2 * k) % 4
            return part.at[1 - y, 1 - x, c, block], self.rp[i].at[k], self.ps.at[i, k], self.pr.at[i, k], self.zp
        if kind == "d":
            block = (z + k) % 4
            there = self.yn if k in self.by_y(i)[0] else self.xn
            return part.at[1 - y, 1 - x, c, block], self.rd[i].at[k], self.ds.at[i, k], self.dr.at[i, k], there
        if kind == "x":
            block = (z + k) % 4
            return part.at[y, 1 - x, c, block], self.rx[i].at[block], self.xs.at[i, k], self.xr.at[i, k], self.xn
        if kind == "y":
            block = (z + k) % 4
            return part.at[1 - y, x, c, block], self.ry[i].at[block], self.ys.at[i, k], self.yr.at[i, k], self.yn
        there = (z + k + 1) % 4
        return part.at[y, x, c, there], self.r3[i].at[k], self.zs.at[i, k], self.zr.at[i, k], device_at(y, x, c, there)

    def send(self, i, kind, *which):
        for k in which:
            remote(*self.hop(i, kind, k)).start()
            self.copies[i].append((kind, k))

    def wait(self, i, kind, *which):
        for k in which:
            remote(*self.hop(i, kind, k)).wait_recv()

    def drain(self, i):
        for kind, k in self.copies[i]:
            remote(*self.hop(i, kind, k)).wait_send()
        self.copies[i] = []

    def start(self, i):
        self.send(i, "c", 0)

    def chip(self, i):
        c = self.here[2]
        part, r0 = self.part[i], self.r0[i]
        self.wait(i, "c", 0)

        def add(k, _):
            a, b, q = k // 8, (k // 4) % 2, k % 4
            part[a, b, c, q] = part[a, b, c, q] + r0[a, b, q]
            return 0

        lax.fori_loop(0, 16, add, 0)
        first, second = self.by_y(i)
        if SUMMED_IN_PAIRS[i]:
            self.send(i, "p", 0, 1)
        else:
            self.send(i, "d", *first, *second)
        self.send(i, "x", *[k for k in (1, 3, 0, 2) if k not in first])
        self.send(i, "y", *[k for k in (0, 2, 1, 3) if k not in second])

    def pair(self, i):
        if not SUMMED_IN_PAIRS[i]:
            return
        y, x, c, z = self.here
        part = self.part[i]
        for k, block in enumerate((z, self.opposite)):
            self.wait(i, "p", k)
            part[1 - y, 1 - x, c, block] = part[1 - y, 1 - x, c, block] + self.rp[i][k]
            self.send(i, "d", 2 * k)

    def diagonal(self, i):
        y, x, c, z = self.here
        part = self.part[i]
        first, second = self.by_y(i)
        for k in first:
            self.wait(i, "d", k)
            block = (z + k) % 4
            part[y, 1 - x, c, block] = part[y, 1 - x, c, block] + self.rd[i][k]
            self.send(i, "x", k)
        for k in second:
            self.wait(i, "d", k)
            block = (z + k) % 4
            part[1 - y, x, c, block] = part[1 - y, x, c, block] + self.rd[i][k]
            self.send(i, "y", k)

    def sides(self, i):
        y, x, c, z = self.here
        part, rx, ry = self.part[i], self.rx[i], self.ry[i]
        self.wait(i, "x", 1, 2, 3, 0)
        self.wait(i, "y", 1, 3, 0, 2)

        def add(q, _):
            both = rx[q].astype(F32) + ry[q].astype(F32)
            part[y, x, c, q] = (part[y, x, c, q].astype(F32) + both).astype(BF16)
            return 0

        lax.fori_loop(0, 4, add, 0)
        self.send(i, "z", 1, 0, 2)

    def last(self, i):
        y, x, c, z = self.here
        self.wait(i, "z", 0, 1, 2)
        part, r3 = self.part[i], self.r3[i]
        total = (part[y, x, c, z].astype(F32) + r3[0].astype(F32)) + (r3[1].astype(F32) + r3[2].astype(F32))
        out, start, stride = self.store[i]
        flatten_into(out, total, start, stride)

    def rest(self):
        while self.point.table:
            self.point()


def flatten_into(out, value, start, stride):
    rows, size = value.shape
    for k in range(size // 128):
        out[pl.ds(start + k, rows, stride=stride), :] = value[:, k * 128 : (k + 1) * 128]


GRADS = ("down", "up", "pt", "qt", "ps", "qs")
WIDTHS = {"down": D, "up": FF, "pt": D, "qt": 3 * D, "ps": D, "qs": 3 * D}
ENTRIES = [("down", k * D // 2, D // 2) for k in range(2)] + [("up", k * FF // 2, FF // 2) for k in range(2)]
ENTRIES += [("pt", 0, D)] + [("qt", k * D, D) for k in range(3)] + [("ps", 0, D)] + [("qs", k * D, D) for k in range(3)]
DOWN, UP, PT, QT, PS, QS = 0, 2, 4, 5, 8, 9
SUMMED_IN_PAIRS = (True, True, True, True, False, False, True, True, True, False, True, False)
SCATTER_STEPS = (
    (), (), (), (), ((0, 0),), (), ((0, 1),), (), ((1, 0), (0, 2),), ((1, 1),), (), (), ((2, 0), (1, 2), (0, 3),),
    (), ((0, 4), (2, 1), (1, 4),), ((3, 0), (2, 2), (1, 3),), (), (), (), (), ((2, 4),), ((0, 5), (4, 0), (1, 5),),
    ((3, 1), (0, 6),), ((3, 2), (0, 7),), ((2, 3), (3, 4),), ((2, 5),), ((4, 1), (1, 6), (0, 8),), (),
    ((3, 3), (1, 7), (4, 2), (3, 5),), ((2, 6), (1, 8), (4, 4),), ((2, 7),), ((3, 6),),
    ((2, 8), (3, 7), (0, 9), (1, 9),), ((0, 10), (4, 3), (3, 8),), ((2, 9), (0, 11), (1, 11),), ((4, 5),), (), (),
    ((4, 6), (3, 9), (1, 10),), ((4, 7), (2, 11),), ((2, 10),), ((4, 8), (3, 11),), ((3, 10),), (), ((4, 9),), (),
    (), (), (), (), ((4, 11),), ((4, 10),),
)
BLOCKS = [("down", j) for j in range(4)] + [("up", j) for j in range(4)]
BLOCKS += [("pt", 0)] + [("qt", j) for j in range(3)] + [("ps", 0)] + [("qs", j) for j in range(3)]
SLOTS = 4


def attend_back(s, q, p, c_grad, first):
    def body(t, _):
        step = first + t
        item, pair = step // PAIRS, step % PAIRS
        rows = pl.ds(pl.multiple_of(item * TOKENS, TOKENS), TOKENS)
        at = [lane_cols(pair * 128 + j * D) for j in range(3)]
        soft = p[:, lane_cols(step * TOKENS, TOKENS)]
        dc = c_grad[rows, at[0]]
        queries, keys, values = (q[rows, where] for where in at)
        v_grad = pick_heads(t_dot(soft[:TOKENS], dc), t_dot(soft[TOKENS:], dc))
        soft_grad = dot_t(two_heads(dc, 1.0), values)
        wide = soft.astype(F32)
        product = soft_grad * wide
        score = (product - wide * jnp.sum(product, axis=-1, keepdims=True)).astype(BF16)
        q_both = dot(score, keys)
        q_grad = pick_heads(q_both[:TOKENS], q_both[TOKENS:]) * HD ** (-0.5)
        k_grad = pick_heads(t_dot(score[:TOKENS], queries), t_dot(score[TOKENS:], queries)) * HD ** (-0.5)
        q[rows, at[0]] = q_grad.astype(BF16)
        q[rows, at[1]] = k_grad.astype(BF16)
        q[rows, at[2]] = v_grad.astype(BF16)
        return 0

    lax.fori_loop(0, PAIRS // 2, body, 0)


def backward_kernel(names, *refs):
    s = Names(names, refs)
    here = place()
    y, x, c, z = here
    me = ((y * 2 + x) * 2 + c) * 4 + z
    loads = {}

    def fetch(name, src, dst, k):
        loads[name] = pltpu.make_async_copy(src, dst, s.load_sem.at[k])
        loads[name].start()

    def have(*wanted):
        for name in wanted:
            loads.pop(name).wait()

    def fetch_block(k):
        tensor, j = BLOCKS[k]
        src = getattr(s, "w_" + tensor)
        src = src.at[j] if tensor == "down" else src.at[:, :, pl.ds(j * D, D)]
        pltpu.make_async_copy(src, s.blocks.at[k % SLOTS], s.load_sem.at[16 + k % SLOTS]).start()

    def block(k):
        slot = k % SLOTS
        pltpu.make_async_copy(s.w_ps, s.blocks.at[slot], s.load_sem.at[16 + slot]).wait()
        return s.blocks[slot].reshape(D, D)

    def used(k):
        if k + SLOTS < len(BLOCKS):
            fetch_block(k + SLOTS)

    def used_at(first, j, count):
        for k in range(count):
            if first + k + SLOTS < len(BLOCKS):
                @pl.when(j == k)
                def _(k=k):
                    fetch_block(first + k + SLOTS)

    fetch("g", s.in_g, s.g, 0)
    fetch("mods", s.in_mods, s.mods, 1)
    fetch_block(0)
    fetch_block(1)
    fetch("gp", s.in_gp, s.gp, 2)
    fetch("h3", s.in_h3, s.h3, 3)
    fetch_block(2)
    fetch_block(3)
    fetch("n3", s.in_n3, s.n3, 4)
    fetch("r3", s.in_r3, s.r3, 5)

    def fetch_rest(k):
        for i, (name, dst) in enumerate((("a", s.a), ("c", s.c), ("h", s.h), ("n", s.n), ("r", s.r))):
            fetch(name, getattr(s, f"in_{name}{k}"), dst, 6 + i)

    fetch_rest(2)

    homes = {"down": (s.b0, 0), "up": (s.b1, 0), "pt": (s.b2, 0), "qt": (s.b2, D), "ps": (s.b3, 0), "qs": (s.b3, D)}
    parts, store = [], []
    for t, start, width in ENTRIES:
        ref, base = homes[t]
        parts.append(ref.at[:, :, :, :, :, pl.ds(base + start, width)])
        store.append((getattr(s, "grad_" + t), start // 128, WIDTHS[t] // 128))
    buffers = [[getattr(s, f"r{k}_{i}") for i in range(len(ENTRIES))] for k in range(6)]
    scatter = Scatter(here, parts, store, buffers, [getattr(s, f"ss{k}") for k in range(12)])
    sender = Sender()
    little = Gather(here, sender, [s.small], [s.small_all], [getattr(s, f"ls{i}") for i in range(8)], s.ls8)

    barrier = pltpu.get_barrier_semaphore()
    partners = [device_at(y, x, 1 - c, z), device_at(y, 1 - x, c, z), device_at(1 - y, x, c, z)]
    partners += [device_at(y, x, c, (z + step) % 4) for step in (1, 2, 3)]
    for partner in partners:
        pl.semaphore_signal(barrier, inc=1, device_id=partner, device_id_type=MESH)
    pl.semaphore_wait(barrier, 6)

    s.rows[...] = jnp.zeros_like(s.rows)
    valid_rows(s)
    ones = jnp.ones((8, 2 * TOKENS), BF16)
    have("mods")
    for item in range(2):
        gate = s.mods[8, item : item + 1, :]

        def first(t, _):
            rows = rows_of(item, t, CHUNK)
            d3 = s.cotangent[rows, :].astype(F32) * s.valid[rows, :]
            s.d[rows, :] = d3
            s.dm[rows, :] = (gate * d3).astype(BF16)
            return 0

        lax.fori_loop(0, TOKENS // CHUNK, first, 0)
        s.rows[9 * item + 8 : 9 * item + 9, :] = s.dga3[item : item + 1, :]
    s.rows[22:23, :] = dot(ones, s.dm[...])[:1]

    have("g")

    def starts(first, indices):
        return {at: lambda i=first + n: scatter.start(i) for n, at in enumerate(indices)}

    def down(t):
        k, j = t // 2, t % 2
        cols = lane_cols(k * (D // 2), D // 2)
        grad = t_dot(s.g[:, lane_cols(2 * j * D, 2 * D)], s.dm[:, cols]).astype(BF16)
        s.b0[j, :, :, :, :, cols] = grad.reshape(2, 2, 4, 4 * D // DEVICES, D // 2)

    scatter.point.rolled(4, (down, starts(DOWN, (1, 3)), 2))
    fetch("p", s.in_p2, s.g, 0)

    have("gp", "h3")

    def up_back(j):
        cols = lane_cols(j * D, D)
        s.acc[...] = dot_t(s.dm[...], block(j))
        used_at(0, j, 4)

        def slope(t, _):
            rows = rows_of(0, t, CHUNK)
            s.gp[rows, cols] = (s.acc[rows, :] * s.gp[rows, cols].astype(F32)).astype(BF16)
            return 0

        lax.fori_loop(0, 2 * TOKENS // CHUNK, slope, 0)
        s.rows[pl.ds(18 + j, 1), :] = dot(ones, s.gp[:, cols])[:1]

    def up_grad(j):
        cols = lane_cols(j * D, D)
        grad = t_dot(s.h3[...], s.gp[:, cols]).astype(BF16)
        s.b1[:, :, :, :, :, cols] = grad.reshape(2, 2, 2, 4, D // DEVICES, D)

    scatter.point.rolled(4, (up_back, {}, 1), (up_grad, starts(UP, (1, 3)), 1))

    def back_through(first_block, source, count, every):
        s.acc[...] = jnp.zeros_like(s.acc)

        def body(j):
            s.acc[...] = s.acc[...] + dot_t(source[:, lane_cols(j * D, D)], block(first_block + j))
            used_at(first_block, j, count)

        scatter.point.rolled(count, (body, {}, every))

    def qkv_grad(out, j):
        grad = t_dot(s.h[...], s.gp[:, lane_cols(j * D, D)]).astype(BF16)
        out[:, :, :, :, :, lane_cols(D + j * D, D)] = grad.reshape(2, 2, 2, 4, D // DEVICES, D)

    back_through(4, s.gp, 4, 2)
    fetch("q", s.in_q2, s.gp.at[:, pl.ds(0, 3 * D)], 2)

    def norm_back(n_ref, r_ref, base, a_ref, gate_row, between=False):
        for item in range(2):
            scale = 1.0 + s.mods[base + 1, item : item + 1, :]
            gate = None if gate_row is None else s.mods[gate_row, item : item + 1, :]

            def body(t, totals):
                rows = rows_of(item, t, CHUNK)
                dh, n = s.acc[rows, :], n_ref[rows, :].astype(F32)
                g = dh * scale
                dhn = dh * n
                mean_g = jnp.mean(g, axis=-1, keepdims=True)
                mean_gn = jnp.mean(g * n, axis=-1, keepdims=True)
                d = s.d[rows, :] + r_ref[rows, :] * (g - mean_g - n * mean_gn)
                s.d[rows, :] = d
                fold = lambda v: jnp.sum(v.reshape(CHUNK // 8, 8, D), axis=0)
                new = [totals[0] + fold(dh), totals[1] + fold(dhn)]
                if gate is not None:
                    s.dm[rows, :] = (gate * d).astype(BF16)
                    new.append(totals[2] + fold(d * a_ref[rows, :].astype(F32)))
                return tuple(new)

            count = 2 if gate is None else 3
            totals = lax.fori_loop(0, TOKENS // CHUNK, body, (jnp.zeros((8, D), F32),) * count)
            for where, total in zip((base, base + 1, base - 1), totals):
                row = 9 * item + where
                s.rows[row : row + 1, :] = jnp.sum(total, axis=0, keepdims=True)
            if between or item:
                scatter.point()

    have("n3", "r3", "a")
    norm_back(s.n3, s.r3, 6, s.a, 5)
    have("c")
    s.b2[:, :, :, :, :, :D] = t_dot(s.c[...], s.dm[...]).astype(BF16).reshape(2, 2, 2, 4, D // DEVICES, D)
    scatter.start(PT)
    s.dc[...] = dot_t(s.dm[...], block(8)).astype(BF16)
    used(8)
    scatter.point()
    have("q", "p")
    scatter.point.rolled(4, (lambda k: attend_back(s, s.gp, s.g, s.dc, 3 * k), {}, 1))
    fetch("p", s.in_p1, s.g, 0)
    have("h")
    scatter.point.rolled(3, (lambda j: qkv_grad(s.b2, j), starts(QT, (0, 1, 2)), 1))
    back_through(9, s.gp, 3, 1)
    fetch("q", s.in_q1, s.gp.at[:, pl.ds(0, 3 * D)], 2)
    have("n", "r")
    fetch("c", s.in_c1, s.c, 7)
    fetch("h", s.in_h1, s.h, 8)
    fetch("a", s.in_a1, s.a, 6)
    have("a")
    norm_back(s.n, s.r, 3, s.a, 2)
    fetch("n", s.in_n1, s.n, 9)
    fetch("r", s.in_r1, s.r, 10)
    have("c")
    s.b3[:, :, :, :, :, :D] = t_dot(s.c[...], s.dm[...]).astype(BF16).reshape(2, 2, 2, 4, D // DEVICES, D)
    scatter.start(PS)
    s.dc[...] = dot_t(s.dm[...], block(12)).astype(BF16)
    used(12)
    scatter.point()
    have("q", "p")
    scatter.point.rolled(4, (lambda k: attend_back(s, s.gp, s.g, s.dc, 3 * k), {}, 1))
    have("h")
    scatter.point.rolled(3, (lambda j: qkv_grad(s.b3, j), starts(QS, (0, 1, 2)), 1))
    back_through(13, s.gp, 3, 1)
    have("n", "r")
    norm_back(s.n, s.r, 0, None, None, True)
    s.small[...] = s.rows[...].astype(BF16)
    little.start(0)
    scatter.point()
    little.stage1(0)
    scatter.point()
    little.stage2(0)
    scatter.point()
    little.stage3(0)
    scatter.point()
    little.finish(0)

    spot = lax.broadcasted_iota(jnp.int32, (D, 128), 0) % (D // DEVICES)

    def ada_grad(j):
        chosen = jnp.where((spot == j) | (spot == j + 9), s.chosen[...], jnp.zeros((D, 128), BF16))
        grad = t_dot(chosen, s.small_all[...].reshape(D, D))[: D // DEVICES]
        flatten_into(s.grad_ada, grad, j * (D // 128), 9 * D // 128)

    scatter.point.rolled(9, (ada_grad, {}, 1))
    gathered = s.small_all[...].reshape(D, D)
    row = lax.broadcasted_iota(jnp.int32, (16, D), 0)
    slot = lax.broadcasted_iota(jnp.int32, (16, D), 1) % (D // DEVICES)
    take = ((row < 9) & ((slot == row) | (slot == row + 9))) | ((row >= 9) & (slot == row + 9))
    s.grad_bias[...] = dot(take.astype(F32).astype(BF16), gathered)
    scatter.rest()
    for i in range(len(ENTRIES)):
        scatter.drain(i)
    sender.drain()


def run_backward(cotangent, buckets, dga3, chosen, kept):
    vmem, any_space = pl.BlockSpec(memory_space=pltpu.VMEM), pl.BlockSpec(memory_space=pl.ANY)
    rows, part = 2 * TOKENS, D // DEVICES
    ins = {"cotangent": cotangent, "buckets": buckets, "dga3": dga3, "chosen": chosen}
    fetched = {"in_" + name: kept[name] for name in save_shapes(TOKENS)}
    for t in GRADS:
        shape = (4, DEVICES, part, D) if t == "down" else (DEVICES, part, WIDTHS[t])
        fetched["w_" + t] = kept["w_" + t].reshape(shape)
    ins |= fetched
    block_of = [(4 * part if t == "down" else part, width) for t, _, width in ENTRIES]
    outs = {"grad_" + t: (DEVICES * part * WIDTHS[t] * (4 if t == "down" else 1) // DEVICES // 128, 128) for t in GRADS}
    outs |= {"grad_ada": (part * 9 * D // 128, 128), "grad_bias": (16, D), "d": (rows, D)}
    dma = pltpu.SemaphoreType.DMA
    big = lambda *block: pltpu.VMEM((2, 2, 2, 4) + block, BF16)
    scratch = {
        "b0": big(4 * part, D), "b1": big(part, FF), "b2": big(part, FF), "b3": big(part, FF),
        "blocks": pltpu.VMEM((SLOTS, DEVICES, part, D), BF16),
        "g": pltpu.VMEM((rows, FF), BF16), "gp": pltpu.VMEM((rows, FF), BF16),
        "acc": pltpu.VMEM((rows, D), F32),
        "mods": pltpu.VMEM((9, 8, D), F32), "rows": pltpu.VMEM((24, D), F32),
        "small": pltpu.VMEM((24, D), BF16), "small_all": big(24, D),
        "r3": pltpu.VMEM((rows, 1), F32), "r": pltpu.VMEM((rows, 1), F32), "valid": pltpu.VMEM((rows, 1), F32),
        "load_sem": dma((16 + SLOTS,)),
    }
    scratch |= {name: pltpu.VMEM((rows, D), BF16) for name in ("dm", "dc", "h3", "n3", "a", "c", "h", "n")}
    for k, lead in enumerate(Scatter.LEADING):
        scratch |= {f"r{k}_{i}": pltpu.VMEM(lead + block, BF16) for i, block in enumerate(block_of)}
    scratch |= {f"ss{k}": dma((len(ENTRIES),) + extra) for k, extra in enumerate(Scatter.SEMAPHORES)}
    scratch |= {f"ls{i}": kind for i, kind in enumerate(Gather.scratch(1))}
    names = list(ins) + list(outs) + list(scratch)
    results = pl.pallas_call(
        lambda *refs: backward_kernel(names, *refs),
        out_shape=tuple(jax.ShapeDtypeStruct(shape, F32) for shape in outs.values()),
        in_specs=[vmem] * 4 + [any_space] * len(fetched),
        out_specs=(vmem,) * len(outs),
        scratch_shapes=list(scratch.values()),
        compiler_params=pltpu.CompilerParams(
            collective_id=2, has_side_effects=True, vmem_limit_bytes=VMEM_LIMIT
        ),
        name="backward",
    )(*ins.values())
    return dict(zip(outs, results))


def deliver_kernel(count, *refs):
    src, out, buf = refs[:count], refs[count : 2 * count], refs[2 * count : 3 * count]
    coming, going = refs[3 * count :]
    copies = []
    for i in sorted(range(count), key=lambda i: -math.prod(src[i].shape)):
        rows = src[i].shape[0]
        step = rows // 2 if rows >= 512 else rows
        for start in range(0, rows, step):
            at = pl.ds(start, min(step, rows - start))
            k = len(copies)
            copies.append((
                pltpu.make_async_copy(src[i].at[at], buf[i].at[at], coming.at[k]),
                pltpu.make_async_copy(buf[i].at[at], out[i].at[at], going.at[k]),
            ))
    for first, _ in copies:
        first.start()
    for first, second in copies:
        first.wait()
        second.start()
    for _, second in copies:
        second.wait()


def deliver(results):
    count = len(results)
    any_space = pl.BlockSpec(memory_space=pl.ANY)
    dma = pltpu.SemaphoreType.DMA((2 * count + 2,))
    return pl.pallas_call(
        lambda *refs: deliver_kernel(count, *refs),
        out_shape=tuple(jax.ShapeDtypeStruct(r.shape, r.dtype) for r in results),
        in_specs=[any_space] * count,
        out_specs=(any_space,) * count,
        scratch_shapes=[pltpu.VMEM(r.shape, r.dtype) for r in results] + [dma, dma],
        compiler_params=pltpu.CompilerParams(vmem_limit_bytes=VMEM_LIMIT),
        name="deliver",
    )(*results)


def norm_parts(rows):
    centre = rows - jnp.mean(rows, axis=-1, keepdims=True)
    inverse = lax.rsqrt(jnp.mean(centre * centre, axis=-1, keepdims=True) + EPS)
    return centre * inverse, inverse


def norm_back(grad, normed, inverse, scale):
    shift_grad = jnp.sum(grad, axis=1)
    scale_grad = jnp.sum(grad * normed, axis=1)
    pulled = grad * (1.0 + scale)
    back = inverse * (
        pulled
        - jnp.mean(pulled, axis=-1, keepdims=True)
        - normed * jnp.mean(pulled * normed, axis=-1, keepdims=True)
    )
    return back, shift_grad, scale_grad


def heads(x):
    return x.reshape(x.shape[0], x.shape[1], HEADS, HD)


def attention(low, qkv_w, proj_w, mask):
    packed = dot(low, qkv_w).astype(BF16)
    q, k, v = (heads(part) for part in jnp.split(packed, 3, axis=-1))
    scores = jnp.einsum("bqhd,bkhd->bhqk", q, k, preferred_element_type=F32) * HD ** (-0.5)
    scores = jnp.where(mask, scores, MASKED)
    soft = jax.nn.softmax(scores, axis=-1)
    context = jnp.einsum("bhqk,bkhd->bqhd", soft.astype(BF16), v, preferred_element_type=F32)
    context = context.astype(BF16).reshape(low.shape)
    return dot(context, proj_w), (q, k, v, soft, context)


def attention_back(grad_low, low, qkv_w, proj_w, kept):
    q, k, v, soft, context = kept
    proj_grad = jnp.einsum("bld,ble->de", context, grad_low, preferred_element_type=F32)
    ctx = heads(jnp.einsum("ble,de->bld", grad_low, proj_w, preferred_element_type=F32).astype(BF16))
    v_grad = jnp.einsum("bhqk,bqhd->bkhd", soft.astype(BF16), ctx, preferred_element_type=F32)
    soft_grad = jnp.einsum("bqhd,bkhd->bhqk", ctx, v, preferred_element_type=F32)
    row_dot = jnp.sum(soft_grad * soft, axis=-1, keepdims=True)
    score_grad = (soft * (soft_grad - row_dot)).astype(BF16)
    q_grad = jnp.einsum("bhqk,bkhd->bqhd", score_grad, k, preferred_element_type=F32) * HD ** (-0.5)
    k_grad = jnp.einsum("bhqk,bqhd->bkhd", score_grad, q, preferred_element_type=F32) * HD ** (-0.5)
    packed = jnp.concatenate(
        [part.astype(BF16).reshape(low.shape) for part in (q_grad, k_grad, v_grad)], axis=-1
    )
    qkv_grad = jnp.einsum("bld,ble->de", low, packed, preferred_element_type=F32)
    low_grad = jnp.einsum("ble,de->bld", packed, qkv_w, preferred_element_type=F32)
    return low_grad, qkv_grad, proj_grad


def gather_plain(shards):
    return tuple(lax.all_gather(s, AXES, axis=0) for s in shards)


def scatter_plain(parts, small):
    devices = lax.axis_size(AXES)
    sums = tuple(
        lax.psum_scatter(p.reshape((devices,) + p.shape[-2:]), AXES, scatter_dimension=0, tiled=True)[
            0
        ].astype(F32)
        for p in parts
    )
    return sums + (lax.all_gather(small, AXES, axis=0),)


def per_device_plain(latents, buckets, step_ids, qs, ps, qt, pt, up, down, ada, biases, cotangent):
    devices = lax.axis_size(AXES)
    micro = latents.shape[0]
    frames, spatial = latents.shape[2], latents.shape[3]
    tokens = frames * spatial
    rows = D // devices

    gather, scatter = gather_plain, scatter_plain

    ada_columns = lax.all_to_all(
        ada.reshape(rows, 9 * D), AXES, split_axis=1, concat_axis=0, tiled=True
    )
    own_bias = jnp.pad(biases, (0, D - biases.shape[0]))[None]
    small = jnp.concatenate([timestep_condition(step_ids[:, 0]), own_bias], axis=0)
    shards = [small] + [w.reshape(rows, -1) for w in (qs, ps, qt, pt, up)] + [down.reshape(-1, D)]
    small, *gathered = gather(shards)
    w_qs, w_ps, w_qt, w_pt, w_up = (w.reshape(D, -1) for w in gathered[:5])
    w_down = gathered[5].reshape(-1, D)
    small = small.reshape(devices, micro + 1, D)
    condition = small[:, :micro].reshape(devices * micro, D)
    bias = small[:, micro, : biases.shape[0]].reshape(-1).astype(F32)
    modulation = lax.all_to_all(
        dot(condition, ada_columns), AXES, split_axis=0, concat_axis=1, tiled=True
    )
    modulation = (modulation + bias[: 9 * D]).reshape(micro, 9, 1, D)
    b_up, b_down = bias[9 * D : 9 * D + FF], bias[9 * D + FF :]

    positions = jnp.arange(tokens)
    frame, place = positions // spatial, positions % spatial
    bucket = buckets[:, 0]
    length = jnp.where(bucket == 0, spatial, jnp.where(bucket == 1, spatial // 2, spatial // 8))
    valid = place[None, :] < length[:, None]
    space_mask = (frame[:, None] == frame[None, :])[None, None] & valid[:, None, None, :]
    time_mask = (place[:, None] == place[None, :])[None, None]
    valid_rows = valid.astype(F32)[:, :, None]

    sh1, sc1, ga1, sh2, sc2, ga2, sh3, sc3, ga3 = (modulation[:, i] for i in range(9))
    x = latents.reshape(micro, tokens, D).astype(F32)
    n1, r1 = norm_parts(x)
    h1 = (n1 * (1.0 + sc1) + sh1).astype(BF16)
    a1, kept1 = attention(h1, w_qs, w_ps, space_mask)
    x1 = x + ga1 * a1
    n2, r2 = norm_parts(x1)
    h2 = (n2 * (1.0 + sc2) + sh2).astype(BF16)
    a2, kept2 = attention(h2, w_qt, w_pt, time_mask)
    x2 = x1 + ga2 * a2
    n3, r3 = norm_parts(x2)
    h3 = (n3 * (1.0 + sc3) + sh3).astype(BF16)
    hidden = dot(h3, w_up) + b_up
    gelu, pull = jax.vjp(lambda u: jax.nn.gelu(u, approximate=True), hidden)
    g = gelu.astype(BF16)
    m = dot(g, w_down) + b_down
    x3 = x2 + ga3 * m
    output = (x3 * valid_rows).astype(BF16)

    d3 = cotangent.reshape(micro, tokens, D).astype(F32) * valid_rows
    dm = (ga3 * d3).astype(BF16)
    dga3 = jnp.sum(d3 * m, axis=1)
    db_down = jnp.sum(dm.astype(F32), axis=(0, 1))
    dw_down = jnp.einsum("bsk,bsd->kd", g, dm, preferred_element_type=F32)
    dg = jnp.einsum("bsd,kd->bsk", dm, w_down, preferred_element_type=F32)
    du = pull(dg)[0].astype(BF16)
    db_up = jnp.sum(du.astype(F32), axis=(0, 1))
    dw_up = jnp.einsum("bsd,bsk->dk", h3, du, preferred_element_type=F32)
    dh3 = jnp.einsum("bsk,dk->bsd", du, w_up, preferred_element_type=F32)
    dv, dsh3, dsc3 = norm_back(dh3, n3, r3, sc3)
    d2 = d3 + dv
    da2 = (ga2 * d2).astype(BF16)
    dga2 = jnp.sum(d2 * a2, axis=1)
    dh2, dw_qt, dw_pt = attention_back(da2, h2, w_qt, w_pt, kept2)
    dv, dsh2, dsc2 = norm_back(dh2, n2, r2, sc2)
    d1 = d2 + dv
    da1 = (ga1 * d1).astype(BF16)
    dga1 = jnp.sum(d1 * a1, axis=1)
    dh1, dw_qs, dw_ps = attention_back(da1, h1, w_qs, w_ps, kept1)
    dv, dsh1, dsc1 = norm_back(dh1, n1, r1, sc1)
    latents_grad = d1 + dv

    dmod = jnp.stack([dsh1, dsc1, dga1, dsh2, dsc2, dga2, dsh3, dsc3, dga3], axis=1)
    small = jnp.concatenate(
        [dmod.reshape(micro * 9, D), db_up.reshape(-1, D), db_down.reshape(-1, D)], axis=0
    ).astype(BF16)
    parts = [
        part.astype(BF16).reshape(tuple(gathered[i].shape))
        for i, part in ((5, dw_down), (4, dw_up), (3, dw_pt), (2, dw_qt), (1, dw_ps), (0, dw_qs))
    ]
    ddown, dup, dpt, dqt, dps, dqs, small = scatter(parts, small)
    flat = tuple(part.reshape(-1) for part in (dqs, dps, dqt, dpt, dup))
    small = small.reshape(devices, -1, D)
    dmod_all = small[:, : micro * 9].reshape(devices * micro, 9 * D)
    me = lax.axis_index(AXES)
    my_condition = lax.dynamic_slice_in_dim(condition, me * rows, rows, axis=1)
    dw_ada = lax.dot_general(
        my_condition, dmod_all, (((0,), (0,)), ((), ())), preferred_element_type=F32
    )
    db = jnp.concatenate(
        [
            jnp.sum(dmod_all.astype(F32), axis=0),
            jnp.sum(small[:, micro * 9 :].astype(F32), axis=0).reshape(-1),
        ]
    )
    db = lax.dynamic_slice_in_dim(db, me * biases.shape[0], biases.shape[0])

    shape = latents.shape
    return (
        output.reshape(shape),
        latents_grad.reshape(shape),
        *flat,
        ddown.reshape(-1),
        dw_ada.reshape(-1),
        db,
    )


def per_device(latents, buckets, step_ids, qs, ps, qt, pt, up, down, ada, biases, cotangent):
    rows = 2 * TOKENS
    conditions = timestep_condition(step_ids[:, 0])
    shards = [w.reshape(-1, 128) for w in (qs, ps, qt, pt, up, down)]
    tokens = latents.reshape(rows, D)
    grads_in = cotangent.reshape(rows, D)
    output, dga3, chosen, kept = run_forward(
        conditions, biases.reshape(1, -1), buckets, ada.reshape(-1, 128), shards, tokens, grads_in
    )
    grads = run_backward(grads_in, buckets, dga3, chosen, kept)
    me = lax.axis_index(AXES)
    bias_grad = grads["grad_bias"][:14].reshape(-1)
    names = ["d"] + ["grad_" + t for t in ("qs", "ps", "qt", "pt", "up", "down", "ada")]
    output, latents_grad, *flat = deliver([output] + [grads[name] for name in names])
    return (
        output.reshape(latents.shape),
        latents_grad.reshape(latents.shape),
        *(g.reshape(-1) for g in flat),
        lax.dynamic_slice_in_dim(bias_grad, me * SHARE, SHARE),
    )


def solution(mesh):
    items = P(None, AXES, None, None, None)
    flat = P(AXES)
    known = mesh.shape["wide"] == 8 and mesh.shape["narrow"] == 4
    return jax.shard_map(
        per_device if known else per_device_plain,
        mesh=mesh,
        in_specs=(items, P(None, AXES), P(None, AXES)) + (flat,) * 8 + (items,),
        out_specs=(items, items) + (flat,) * 8,
        check_vma=False,
    )
```

```python
import math

import jax
import jax.numpy as jnp
from jax import lax
from jax.experimental import pallas as pl
from jax.experimental.pallas import tpu as pltpu
from jax.sharding import PartitionSpec as P

D = 768
HEADS = 12
HD = 64
FF = 3072
AXES = ("wide", "narrow")
EPS = 1e-06
MASKED = -1e30
F32 = jnp.float32
BF16 = jnp.bfloat16
GELU = math.sqrt(2.0 / math.pi)
MESH = pl.DeviceIdType.MESH
DEVICES = 32
OWNERS = 9 * D // 256
SHARE = (10 * D + FF) // DEVICES
SPATIAL = 16
TOKENS = 256
VMEM_LIMIT = 67_000_000


def dot(a, b):
    return jnp.dot(a, b, preferred_element_type=F32)


def place():
    w, z = lax.axis_index("wide"), lax.axis_index("narrow")
    return w // 4, (w // 2) % 2, w % 2, z


def device_at(y, x, c, z):
    return {"wide": (y * 2 + x) * 2 + c, "narrow": z}


def remote(src, dst, send, recv, target):
    return pltpu.make_async_remote_copy(
        src_ref=src, dst_ref=dst, send_sem=send, recv_sem=recv,
        device_id=target, device_id_type=MESH,
    )


class Sender:
    def __init__(self):
        self.copies = []

    def go(self, src, dst, send, recv, target):
        copy = remote(src, dst, send, recv, target)
        copy.start()
        self.copies.append(copy)

    def drain(self):
        for copy in self.copies:
            copy.wait_send()


def timestep_condition(step_values):
    half_width = D // 2
    frequency = jnp.exp(-math.log(10000.0) * jnp.arange(half_width, dtype=F32) / half_width)
    angles = step_values.astype(F32)[:, None] * frequency
    return jax.nn.silu(jnp.concatenate([jnp.cos(angles), jnp.sin(angles)], axis=-1)).astype(BF16)


class Gather:
    SEMAPHORES = (3, 3, 10, 10, 3, 3, 3, 3)

    def __init__(self, here, sender, own, out, semaphores, local):
        self.here, self.sender, self.own, self.out, self.local = here, sender, own, out, local
        self.zs, self.zr, self.cs, self.cr, self.xs, self.xr, self.ys, self.yr = semaphores
        y, x, c, z = here
        self.sib = device_at(y, x, 1 - c, z)
        self.xn = device_at(y, 1 - x, c, z)
        self.yn = device_at(1 - y, x, c, z)

    @staticmethod
    def scratch(count):
        kinds = [pltpu.SemaphoreType.DMA((count, k)) for k in Gather.SEMAPHORES]
        return kinds + [pltpu.SemaphoreType.DMA((count,))]

    def start(self, i):
        y, x, c, z = self.here
        mine = self.out[i].at[y, x, c, z]
        for step in (2, 1, 3):
            self.sender.go(
                self.own[i], mine, self.zs.at[i, step - 1],
                self.zr.at[i, step - 1], device_at(y, x, c, (z + step) % 4),
            )
        pltpu.make_async_copy(self.own[i], mine, self.local.at[i]).start()
        self.sender.go(self.own[i], mine, self.cs.at[i, 0], self.cr.at[i, 0], self.sib)

    def along(self, ref, send, recv, target):
        self.sender.go(ref, ref, send, recv, target)

    def arrived(self, ref, send, recv):
        remote(ref, ref, send, recv, self.sib).wait_recv()

    def across(self, i, k, ref):
        self.sender.go(ref, ref, self.cs.at[i, k], self.cr.at[i, k], self.sib)

    def stage1(self, i):
        y, x, c, z = self.here
        out = self.out[i]
        pltpu.make_async_copy(self.own[i], out.at[y, x, c, z], self.local.at[i]).wait()
        for step in (1, 2, 3):
            self.arrived(out.at[y, x, c, (z + 4 - step) % 4], self.zs.at[i, step - 1], self.zr.at[i, step - 1])
        low, high = out.at[y, x, c, pl.ds(0, 2)], out.at[y, x, c, pl.ds(2, 2)]
        self.along(low, self.xs.at[i, 0], self.xr.at[i, 0], self.xn)
        self.along(high, self.ys.at[i, 0], self.yr.at[i, 0], self.yn)
        self.along(high, self.xs.at[i, 1], self.xr.at[i, 1], self.xn)
        self.along(low, self.ys.at[i, 1], self.yr.at[i, 1], self.yn)
        for step in (1, 2, 3):
            self.across(i, step, out.at[y, x, c, (z + 4 - step) % 4])

    def stage2(self, i):
        y, x, c, z = self.here
        low_x = self.out[i].at[y, 1 - x, c, pl.ds(0, 2)]
        high_y = self.out[i].at[1 - y, x, c, pl.ds(2, 2)]
        self.arrived(low_x, self.xs.at[i, 0], self.xr.at[i, 0])
        self.along(low_x, self.ys.at[i, 2], self.yr.at[i, 2], self.yn)
        self.arrived(high_y, self.ys.at[i, 0], self.yr.at[i, 0])
        self.along(high_y, self.xs.at[i, 2], self.xr.at[i, 2], self.xn)
        self.across(i, 4, low_x)
        self.across(i, 5, high_y)

    def stage3(self, i):
        y, x, c, z = self.here
        out = self.out[i]
        arrivals = (
            (out.at[y, 1 - x, c, pl.ds(2, 2)], self.xs.at[i, 1], self.xr.at[i, 1]),
            (out.at[1 - y, x, c, pl.ds(0, 2)], self.ys.at[i, 1], self.yr.at[i, 1]),
            (out.at[1 - y, 1 - x, c, pl.ds(2, 2)], self.xs.at[i, 2], self.xr.at[i, 2]),
            (out.at[1 - y, 1 - x, c, pl.ds(0, 2)], self.ys.at[i, 2], self.yr.at[i, 2]),
        )
        for k, (ref, send, recv) in enumerate(arrivals):
            self.arrived(ref, send, recv)
            self.across(i, 6 + k, ref)

    def finish(self, i):
        y, x, c, z = self.here
        o = 1 - c
        out = self.out[i]
        arrivals = [out.at[y, x, o, (z + 4 - step) % 4] for step in (0, 1, 2, 3)]
        arrivals += [
            out.at[y, 1 - x, o, pl.ds(0, 2)],
            out.at[1 - y, x, o, pl.ds(2, 2)],
            out.at[y, 1 - x, o, pl.ds(2, 2)],
            out.at[1 - y, x, o, pl.ds(0, 2)],
            out.at[1 - y, 1 - x, o, pl.ds(2, 2)],
            out.at[1 - y, 1 - x, o, pl.ds(0, 2)],
        ]
        for k, ref in enumerate(arrivals):
            self.arrived(ref, self.cs.at[i, k], self.cr.at[i, k])


class Spread:
    SEMAPHORES = (3, 3, 6, 6, 6, 6, 2, 2, 16, 16)

    def __init__(self, here, own, out, semaphores, local, pairs):
        self.here, self.own, self.out, self.local = here, own, out, local
        self.pairs = pairs
        self.zs, self.zr, self.xs, self.xr, self.ys, self.yr, self.ps, self.pr, self.cs, self.cr = semaphores
        self.sent = []
        y, x, c, z = here
        self.sib = device_at(y, x, 1 - c, z)
        self.xn = device_at(y, 1 - x, c, z)
        self.yn = device_at(1 - y, x, c, z)
        self.partner = z + 1 - 2 * (z % 2)
        self.opposite = (z + 2) % 4
        self.zp = device_at(y, x, c, self.partner)

    @staticmethod
    def scratch(count):
        kinds = [pltpu.SemaphoreType.DMA((count, k)) for k in Spread.SEMAPHORES]
        return kinds + [pltpu.SemaphoreType.DMA((count,))]

    def go(self, i, k, src, dst, send, recv, target):
        remote(src, dst, send.at[i, k], recv.at[i, k], target).start()
        self.sent.append((i, k, send, recv))

    def drain(self):
        for i, k, send, recv in self.sent:
            remote(self.own[i], self.own[i], send.at[i, k], recv.at[i, k], self.sib).wait_send()

    def to_x(self, i, k, ref):
        self.go(i, k, ref, ref, self.xs, self.xr, self.xn)

    def to_y(self, i, k, ref):
        self.go(i, k, ref, ref, self.ys, self.yr, self.yn)

    def across(self, i, k, ref):
        self.go(i, k, ref, ref, self.cs, self.cr, self.sib)

    def arrived(self, ref, send, recv):
        remote(ref, ref, send, recv, self.sib).wait_recv()

    def from_z(self, step):
        return (self.here[3] + 4 - step) % 4

    def beside(self, i):
        y, x, c, z = self.here
        own, mine = self.own[i], self.out[i].at[y, x, c, z]
        pltpu.make_async_copy(own, mine, self.local.at[i]).start()
        self.go(i, 0, own, mine, self.xs, self.xr, self.xn)
        self.go(i, 0, own, mine, self.ys, self.yr, self.yn)
        self.go(i, 0, own, mine, self.cs, self.cr, self.sib)

    def along(self, i):
        y, x, c, z = self.here
        own, mine = self.own[i], self.out[i].at[y, x, c, z]
        for step in (2, 1, 3):
            there = device_at(y, x, c, (z + step) % 4)
            self.go(i, step - 1, own, mine, self.zs, self.zr, there)

    def column(self, i):
        y, x, c, z = self.here
        for step in (2, 1, 3):
            ref = self.out[i].at[y, x, c, self.from_z(step)]
            self.arrived(ref, self.zs.at[i, step - 1], self.zr.at[i, step - 1])
            self.to_x(i, step, ref)
            self.to_y(i, step, ref)
            self.across(i, step, ref)

    def sides(self, i):
        y, x, c, z = self.here
        for step in (0, 2, 1, 3):
            from_x = self.out[i].at[y, 1 - x, c, self.from_z(step)]
            self.arrived(from_x, self.xs.at[i, step], self.xr.at[i, step])
            if step == 0 or step == 2 and not self.pairs[i]:
                self.to_y(i, 4 + step // 2, from_x)
            self.across(i, 4 + step, from_x)
            from_y = self.out[i].at[1 - y, x, c, self.from_z(step)]
            self.arrived(from_y, self.ys.at[i, step], self.yr.at[i, step])
            if step == 2 and self.pairs[i]:
                self.to_x(i, 4, from_y)
            if step % 2 and not self.pairs[i]:
                self.to_x(i, 4 + step // 2, from_y)
            self.across(i, 8 + step, from_y)

    def diagonal(self, i):
        y, x, c, z = self.here
        where = self.out[i].at[1 - y, 1 - x, c]
        blocks = self.corner(i)
        if self.pairs[i]:
            lanes = ((self.ys, self.yr, 4), (self.xs, self.xr, 4))
        else:
            lanes = ((self.ys, self.yr, 4), (self.ys, self.yr, 5), (self.xs, self.xr, 4), (self.xs, self.xr, 5))
        for k, (send, recv, n) in enumerate(lanes):
            ref = where.at[blocks[k]]
            self.arrived(ref, send.at[i, n], recv.at[i, n])
            if self.pairs[i]:
                self.go(i, k, ref, ref, self.ps, self.pr, self.zp)
            self.across(i, 12 + k, ref)

    def corner(self, i):
        if self.pairs[i]:
            return self.here[3], self.opposite, self.partner, (self.partner + 2) % 4
        return self.from_z(0), self.from_z(2), self.from_z(1), self.from_z(3)

    def pair(self, i):
        y, x, c, z = self.here
        where = self.out[i].at[1 - y, 1 - x, c]
        for k, block in enumerate(self.corner(i)[2:] if self.pairs[i] else ()):
            ref = where.at[block]
            self.arrived(ref, self.ps.at[i, k], self.pr.at[i, k])
            self.across(i, 14 + k, ref)

    def finish(self, i):
        y, x, c, z = self.here
        out, o = self.out[i], 1 - c
        pltpu.make_async_copy(self.own[i], out.at[y, x, c, z], self.local.at[i]).wait()
        arrivals = [out.at[y, x, o, self.from_z(step)] for step in range(4)]
        arrivals += [out.at[y, 1 - x, o, self.from_z(step)] for step in range(4)]
        arrivals += [out.at[1 - y, x, o, self.from_z(step)] for step in range(4)]
        arrivals += [out.at[1 - y, 1 - x, o, block] for block in self.corner(i)]
        for k, ref in enumerate(arrivals):
            self.arrived(ref, self.cs.at[i, k], self.cr.at[i, k])


PAIRED = (True, True, False, True, True, True, False, False)
SPREAD_STEPS = (
    (("A", 0), ("B", 0),), (), (), (("A", 1), ("A", 2), ("A", 3),), (("A", 6),), (("A", 4),), (), (("A", 5),), (),
    (("B", 1),), (("B", 2),), (("C", 0),), (), (("B", 4),), (("B", 3),), (("C", 1),), (), (),
    (("X", 0), ("X", 1), ("C", 2), ("D", 0), ("D", 1), ("C", 4), ("P", 0),),
    (("B", 5), ("P", 1), ("X", 2), ("C", 3),), (), (), (("B", 6), ("X", 4),), (), (), (("D", 2), ("C", 5),), (),
    (("B", 7), ("X", 3), ("D", 4),), (), (), (("C", 6),), (), (("D", 3), ("X", 5),), (),
    (("A", 7), ("C", 7), ("P", 4), ("X", 6),), (("P", 3), ("D", 5),), (), (), (), (("P", 5), ("X", 7),), (), (),
    (("D", 6),), (("D", 7),), (), (),
)


class Steps:
    def __init__(self, calls, table):
        self.calls, self.table = calls, list(table)

    def run(self, steps):
        for kind, i in steps:
            self.calls[kind](i)

    def __call__(self):
        self.run(self.table.pop(0))

    def rolled(self, count, *parts):
        due = [[self.table.pop(0) if k % every == every - 1 else () for _, _, every in parts] for k in range(count)]

        def turn(j, _):
            for n, (body, also, _) in enumerate(parts):
                body(j)
                for k in range(count):
                    if k in also or due[k][n]:
                        @pl.when(j == k)
                        def _(k=k, n=n, also=also):
                            if k in also:
                                also[k]()
                            self.run(due[k][n])

            return 0

        lax.fori_loop(0, count, turn, 0)


class Names:
    def __init__(self, names, refs):
        for name, ref in zip(names, refs, strict=True):
            setattr(self, name, ref)


def rows_of(item, step, size):
    return pl.ds(pl.multiple_of(item * TOKENS + step * size, size), size)


def lane_cols(start, size=128):
    return pl.ds(start if isinstance(start, int) else pl.multiple_of(start, 128), size)


def dot_t(a, b):
    return lax.dot_general(a, b, (((1,), (1,)), ((), ())), preferred_element_type=F32)


def t_dot(a, b):
    return lax.dot_general(a, b, (((0,), (0,)), ((), ())), preferred_element_type=F32)


def weight_block(ref, start, size):
    cols = ref[:, :, :, :, :, lane_cols(start, size)]
    return cols.reshape(-1, size)


def two_heads(x, scale):
    lane = lax.broadcasted_iota(jnp.int32, x.shape, 1)
    x = x * jnp.asarray(scale, x.dtype)
    zero = jnp.zeros_like(x)
    return jnp.concatenate([jnp.where(lane < HD, x, zero), jnp.where(lane >= HD, x, zero)], axis=0)


def pick_heads(first, second):
    lane = lax.broadcasted_iota(jnp.int32, first.shape, 1)
    return jnp.where(lane < HD, first, second)


def norm_rows(v):
    centre = v - jnp.mean(v, axis=-1, keepdims=True)
    inverse = lax.rsqrt(jnp.mean(centre * centre, axis=-1, keepdims=True) + EPS)
    return centre * inverse, inverse


CHUNK = 32
PAIRS = HEADS // 2
TENSORS = ("qs", "ps", "qt", "pt", "up", "down")
PIECES = (("qs", 0, 3 * D), ("ps", 0, D), ("qt", 0, 3 * D), ("pt", 0, D))
PIECES += tuple((t, k * n, n) for t, n in (("up", FF // 2), ("down", D // 2)) for k in range(2))


def save_shapes(tokens):
    rows = 2 * tokens
    attention = {
        "n": ((rows, D), BF16), "r": ((rows, 1), F32), "h": ((rows, D), BF16),
        "q": ((rows, 3 * D), BF16), "p": ((rows, 2 * PAIRS * tokens), BF16),
        "c": ((rows, D), BF16), "a": ((rows, D), BF16),
    }
    out = {}
    for k in (1, 2):
        out.update({name + str(k): spec for name, spec in attention.items()})
    out.update({
        "n3": ((rows, D), BF16), "r3": ((rows, 1), F32), "h3": ((rows, D), BF16),
        "g": ((rows, FF), BF16), "gp": ((rows, FF), BF16), "mods": ((9, 8, D), F32),
    })
    return out


def unflatten(s, flat, own):
    rows, size = own.shape
    stride = size // 128
    s.stage[pl.ds(0, flat.shape[0]), :] = flat[...].astype(F32)
    for k in range(stride):
        own[:, k * 128 : (k + 1) * 128] = s.stage[pl.ds(k, rows, stride=stride), :].astype(BF16)


def lengths(buckets):
    return jnp.where(buckets == 0, SPATIAL, jnp.where(buckets == 1, SPATIAL // 2, SPATIAL // 8))


def valid_rows(s):
    length = lengths(s.buckets[...])
    spot = lax.broadcasted_iota(jnp.int32, (TOKENS, 1), 0) % SPATIAL
    for item in range(2):
        s.valid[item * TOKENS : (item + 1) * TOKENS, :] = (spot < length[item : item + 1, :]).astype(F32)


def norm_into(s, k, shift, scale, rows, item, v):
    n, r = norm_rows(v)
    getattr(s, "n" + k)[rows, :] = n.astype(BF16)
    getattr(s, "r" + k)[rows, :] = r
    h = n * (1.0 + s.mods[scale, item : item + 1, :]) + s.mods[shift, item : item + 1, :]
    getattr(s, "h" + k)[rows, :] = h.astype(BF16)


def project(s, k, weight, point):
    h, q = getattr(s, "h" + k), getattr(s, "q" + k)

    def column(j):
        q[:, lane_cols(j * D, D)] = dot(h[...], weight_block(weight, j * D, D)).astype(BF16)

    point.rolled(3, (column, {}, 1))


def attend(s, k, bias_of, first):
    q, p, c = getattr(s, "q" + k), getattr(s, "p" + k), getattr(s, "c" + k)

    def body(t, _):
        step = first + t
        item, pair = step // PAIRS, step % PAIRS
        rows = pl.ds(pl.multiple_of(item * TOKENS, TOKENS), TOKENS)
        at = [lane_cols(pair * 128 + j * D) for j in range(3)]
        scores = dot_t(two_heads(q[rows, at[0]], HD ** (-0.5)), q[rows, at[1]])
        scores = (scores.reshape(2, TOKENS, TOKENS) + bias_of(item)).reshape(2 * TOKENS, TOKENS)
        expanded = jnp.exp(scores - jnp.max(scores, axis=-1, keepdims=True))
        soft = (expanded * (1.0 / jnp.sum(expanded, axis=-1, keepdims=True))).astype(BF16)
        p[:, lane_cols(step * TOKENS, TOKENS)] = soft
        context = dot(soft, q[rows, at[2]])
        c[rows, at[0]] = pick_heads(context[:TOKENS], context[TOKENS:]).astype(BF16)
        return 0

    lax.fori_loop(0, PAIRS // 2, body, 0)


def after_attention(s, k, next_k, weight, gate, shift, scale):
    s.acc[...] = dot(getattr(s, "c" + k)[...], weight_block(weight, 0, D))
    for item in range(2):
        def body(t, _):
            rows = rows_of(item, t, CHUNK)
            a = s.acc[rows, :]
            v = s.x[rows, :] + s.mods[gate, item : item + 1, :] * a
            s.x[rows, :] = v
            getattr(s, "a" + k)[rows, :] = a.astype(BF16)
            norm_into(s, next_k, shift, scale, rows, item, v)
            return 0

        lax.fori_loop(0, TOKENS // CHUNK, body, 0)


def flat_bias(s):
    s.bias[...] = jnp.zeros_like(s.bias)
    for d in range(DEVICES):
        y, x, c, z = d // 16, (d // 8) % 2, (d // 4) % 2, d % 4
        piece = s.small_all[y, x, c, z].astype(F32)[2:3, :512]
        lane = lax.broadcasted_iota(jnp.int32, piece.shape, 1)
        piece = jnp.where(lane < SHARE, piece, 0.0)
        start = d * SHARE
        if start % 128:
            piece = pltpu.roll(piece, start % 128, 1)
        low = start // 128 * 128
        s.bias[:, low : low + 512] = s.bias[:, low : low + 512] + piece


def forward_kernel(names, *refs):
    s = Names(names, refs)
    here = place()
    y, x, c, z = here
    me = ((y * 2 + x) * 2 + c) * 4 + z
    sender = Sender()
    weights = [getattr(s, "w_" + t).at[:, :, :, :, :, pl.ds(at, size)] for t, at, size in PIECES]
    own = [getattr(s, "own_" + t).at[:, pl.ds(at, size)] for t, at, size in PIECES]
    gather = Spread(here, own, weights, [getattr(s, f"gs{i}") for i in range(10)], s.gs10, PAIRED)
    calls = {"A": gather.beside, "B": gather.along, "C": gather.column}
    calls |= {"X": gather.sides, "D": gather.diagonal, "P": gather.pair}
    point = Steps(calls, SPREAD_STEPS)
    little = Gather(here, sender, [s.small], [s.small_all], [getattr(s, f"ls{i}") for i in range(8)], s.ls8)
    saves = []

    def save(*names):
        for name in names:
            copy = pltpu.make_async_copy(getattr(s, name), getattr(s, "out_" + name), s.save_sem.at[len(saves)])
            copy.start()
            saves.append(copy)

    def target(k):
        d = (me + k) % DEVICES
        return d, {"wide": d // 4, "narrow": d % 4}

    barrier = pltpu.get_barrier_semaphore()

    def signal(k, _):
        pl.semaphore_signal(barrier, inc=1, device_id=target(k)[1], device_id_type=MESH)
        return 0

    lax.fori_loop(1, DEVICES, signal, 0)
    s.little[...] = jnp.zeros_like(s.little)
    s.little[0:2, :] = s.conditions[...].astype(F32)
    s.little[2:3, :SHARE] = s.biases[...].astype(F32)
    s.small[...] = s.little[...].astype(BF16)
    unflatten(s, s.flat_ada, s.ada)
    pl.semaphore_wait(barrier, DEVICES - 1)

    def columns_copy(k):
        d, there = target(k)
        src = s.ada.at[:, lane_cols(d * 256, 256)]
        return d, remote(src, s.ada_cols.at[me], s.a_send.at[k], s.a_recv.at[me], there)

    little.start(0)

    def send_columns(k, _):
        d, copy = columns_copy(k)

        @pl.when(d < OWNERS)
        def _():
            copy.start()

        return 0

    lax.fori_loop(1, DEVICES, send_columns, 0)
    owner = me < OWNERS
    mine = jnp.minimum(me, OWNERS - 1)
    own_columns = pltpu.make_async_copy(s.ada.at[:, lane_cols(mine * 256, 256)], s.ada_cols.at[me], s.own_sem.at[0])
    own_columns.start()
    for t in TENSORS:
        unflatten(s, getattr(s, "flat_" + t), getattr(s, "own_" + t))
    point()

    place_of = lambda n: lax.broadcasted_iota(jnp.int32, (TOKENS, TOKENS), n)
    same_frame = place_of(0) // SPATIAL == place_of(1) // SPATIAL
    same_place = place_of(0) % SPATIAL == place_of(1) % SPATIAL
    for item in range(2):
        seen = lax.broadcasted_iota(jnp.int32, (1, TOKENS), 1) % SPATIAL < lengths(s.buckets[...])[item : item + 1, :]
        s.space_bias[item] = jnp.where(same_frame, jnp.where(seen, 0.0, MASKED), MASKED)
    s.time_bias[...] = jnp.where(same_place, 0.0, MASKED)
    valid_rows(s)
    point()
    point()
    little.stage1(0)
    point()
    little.stage2(0)
    point()
    little.stage3(0)
    point()
    little.finish(0)
    point()
    own_columns.wait()

    def modulation_copy(k):
        d, there = target(k)
        src = s.mod_cols.at[pl.ds(pl.multiple_of(d * 8, 8), 8)]
        return remote(src, s.mod_all.at[me], s.m_send.at[k], s.m_recv.at[me], there)

    own_mod = pltpu.make_async_copy(
        s.mod_cols.at[pl.ds(pl.multiple_of(me * 8, 8), 8)], s.mod_all.at[mine], s.own_sem.at[1]
    )

    conditions = s.small_all[...].reshape(DEVICES * 8, D)
    point()

    @pl.when(owner)
    def _():
        def wait_columns(k, _):
            d, there = target(k)
            remote(s.ada_cols.at[d], s.ada_cols.at[d], s.a_send.at[k], s.a_recv.at[d], there).wait_recv()
            return 0

        lax.fori_loop(1, DEVICES, wait_columns, 0)
        s.mod_cols[...] = dot(conditions, s.ada_cols[...].reshape(D, 256))

        def send_modulation(k, _):
            modulation_copy(k).start()
            return 0

        lax.fori_loop(1, DEVICES, send_modulation, 0)
        own_mod.start()

    point()
    flat_bias(s)
    point()
    part = D // DEVICES
    spot = lambda shape, n: lax.broadcasted_iota(jnp.int32, shape, n)
    col = spot((D, 128), 1)
    wanted = (spot((D, 128), 0) == me * part + col) & (col < part)
    mine_only = dot(conditions, wanted.astype(F32).astype(BF16)).astype(BF16)
    row, item = spot((D, DEVICES * 8), 0), spot((D, DEVICES * 8), 1)
    slot = row % part
    copy_of = (row // part == item // 8) & (slot // 9 == item % 8) & (slot < 18)
    s.chosen[...] = dot(copy_of.astype(F32).astype(BF16), mine_only).astype(BF16)
    for _ in range(6):
        point()

    @pl.when(owner)
    def _():
        own_mod.wait()

    def wait_modulation(k, _):
        d, there = target(k)

        @pl.when(d < OWNERS)
        def _():
            remote(s.mod_all.at[d], s.mod_all.at[d], s.m_send.at[k], s.m_recv.at[d], there).wait_recv()

        return 0

    lax.fori_loop(1, DEVICES, wait_modulation, 0)
    for j in range(9):
        row = jnp.concatenate([s.mod_all[3 * j + i] for i in range(3)], axis=1)
        s.mods[j] = row + s.bias[:, j * D : (j + 1) * D]
    save("mods")

    for item in range(2):
        def first(t, _):
            rows = rows_of(item, t, CHUNK)
            v = s.latents[rows, :].astype(F32)
            s.x[rows, :] = v
            norm_into(s, "1", 0, 1, rows, item, v)
            return 0

        lax.fori_loop(0, TOKENS // CHUNK, first, 0)
        point()
    save("n1", "r1", "h1")

    def ready(i):
        point()
        gather.finish(i)
        t, at, size = PIECES[i]
        if at + size == getattr(s, "w_" + t).shape[-1]:
            save("w_" + t)

    ready(0)
    project(s, "1", s.w_qs, point)
    space = lambda item: s.space_bias[item]
    point.rolled(4, (lambda k: attend(s, "1", space, 3 * k), {}, 1))
    ready(1)
    after_attention(s, "1", "2", s.w_ps, 2, 3, 4)
    save("q1", "p1", "c1", "a1", "n2", "r2", "h2")
    point()
    ready(2)
    project(s, "2", s.w_qt, point)
    time = lambda item: s.time_bias[...]
    point.rolled(4, (lambda k: attend(s, "2", time, 3 * k), {}, 1))
    ready(3)
    after_attention(s, "2", "3", s.w_pt, 5, 6, 7)
    save("q2", "p2", "c2", "a2", "n3", "r3", "h3")
    point()
    ready(4)

    def up(j):
        cols = lane_cols(j * D, D)
        s.acc[...] = dot(s.h3[...], weight_block(s.w_up, j * D, D))
        b_up = s.bias[:, lane_cols((9 + j) * D, D)]

        def activate(t, _):
            rows = rows_of(0, t, CHUNK)
            u = s.acc[rows, :] + b_up
            square = u * u
            th = jnp.tanh(u * (GELU + (GELU * 0.044715) * square))
            half = 0.5 * u
            s.g[rows, cols] = (half + half * th).astype(BF16)
            slope = 0.5 + 0.5 * th + half * (1.0 - th * th) * (GELU + (3 * GELU * 0.044715) * square)
            s.gp[rows, cols] = slope.astype(BF16)
            return 0

        lax.fori_loop(0, 2 * TOKENS // CHUNK, activate, 0)

    point.rolled(2, (up, {}, 1))
    ready(5)
    point.rolled(2, (lambda j: up(2 + j), {}, 1))
    save("g", "gp")
    s.acc[...] = jnp.zeros_like(s.acc)
    for half in range(2):
        ready(6 + half)
        cols = slice(half * D // 2, (half + 1) * D // 2)

        def down(j, _):
            w = s.w_down[j // 2, j % 2, :, :, :, cols].reshape(D, D // 2)
            s.acc[:, cols] = s.acc[:, cols] + dot(s.g[:, lane_cols(j * D, D)], w)
            return 0

        lax.fori_loop(0, FF // D, down, 0)
    b_down = s.bias[:, (9 + FF // D) * D : (10 + FF // D) * D]
    for item in range(2):
        gate = s.mods[8, item : item + 1, :]

        def last(t, total):
            rows = rows_of(item, t, CHUNK)
            m = s.acc[rows, :] + b_down
            valid = s.valid[rows, :]
            s.output[rows, :] = ((s.x[rows, :] + gate * m) * valid).astype(BF16)
            d3 = s.cotangent[rows, :].astype(F32) * valid
            return total + jnp.sum((d3 * m).reshape(CHUNK // 8, 8, D), axis=0)

        total = lax.fori_loop(0, TOKENS // CHUNK, last, jnp.zeros((8, D), F32))
        s.dga3[item : item + 1, :] = jnp.sum(total, axis=0, keepdims=True)

    def drain(k, _):
        d, copy = columns_copy(k)

        @pl.when(d < OWNERS)
        def _():
            copy.wait_send()

        @pl.when(owner)
        def _():
            modulation_copy(k).wait_send()

        return 0

    lax.fori_loop(1, DEVICES, drain, 0)
    sender.drain()
    gather.drain()
    for copy in saves:
        copy.wait()


def run_forward(conditions, biases, buckets, ada, shards, latents, cotangent):
    vmem, any_space = pl.BlockSpec(memory_space=pltpu.VMEM), pl.BlockSpec(memory_space=pl.ANY)
    saved = save_shapes(TOKENS)
    part = D // DEVICES
    own = {t: (4 * part, D) if t == "down" else (part, WIDTHS[t]) for t in TENSORS}
    weights = {"w_" + t: ((2, 2, 2, 4) + own[t], BF16) for t in TENSORS}
    kept = {**saved, **weights}
    rows = 2 * TOKENS
    ins = ["conditions", "biases", "buckets", "flat_ada"] + ["flat_" + t for t in TENSORS] + ["latents", "cotangent"]
    outs = ["output", "dga3", "chosen"] + ["out_" + name for name in kept]
    dma = pltpu.SemaphoreType.DMA
    scratch = {name: pltpu.VMEM(*spec) for name, spec in kept.items()}
    scratch |= {"own_" + t: pltpu.VMEM(shape, BF16) for t, shape in own.items()}
    scratch |= {
        "small": pltpu.VMEM((8, D), BF16), "little": pltpu.VMEM((8, D), F32),
        "stage": pltpu.VMEM((ada.shape[0] + 64, 128), F32), "ada": pltpu.VMEM((part, 9 * D), BF16),
        "valid": pltpu.VMEM((rows, 1), F32),
        "small_all": pltpu.VMEM((2, 2, 2, 4, 8, D), BF16),
        "ada_cols": pltpu.VMEM((DEVICES, part, 256), BF16),
        "mod_cols": pltpu.VMEM((DEVICES * 8, 256), F32),
        "mod_all": pltpu.VMEM((OWNERS, 8, 256), F32),
        "bias": pltpu.VMEM((1, DEVICES * SHARE + 512), F32),
        "x": pltpu.VMEM((rows, D), F32),
        "acc": pltpu.VMEM((rows, D), F32),
        "space_bias": pltpu.VMEM((2, TOKENS, TOKENS), F32),
        "time_bias": pltpu.VMEM((TOKENS, TOKENS), F32),
        "save_sem": dma((len(kept),)),
        "a_send": dma((DEVICES,)), "a_recv": dma((DEVICES,)),
        "m_send": dma((DEVICES,)), "m_recv": dma((DEVICES,)), "own_sem": dma((2,)),
    }
    scratch |= {f"gs{i}": kind for i, kind in enumerate(Spread.scratch(len(PIECES)))}
    scratch |= {f"ls{i}": kind for i, kind in enumerate(Gather.scratch(1))}
    names = ins + outs + list(scratch)
    results = pl.pallas_call(
        lambda *refs: forward_kernel(names, *refs),
        out_shape=(jax.ShapeDtypeStruct((rows, D), BF16), jax.ShapeDtypeStruct((2, D), F32), jax.ShapeDtypeStruct((D, 128), BF16))
        + tuple(jax.ShapeDtypeStruct(*spec) for spec in kept.values()),
        in_specs=[vmem] * len(ins),
        out_specs=(vmem,) * 3 + (any_space,) * len(kept),
        scratch_shapes=list(scratch.values()),
        compiler_params=pltpu.CompilerParams(
            collective_id=1, has_side_effects=True, vmem_limit_bytes=VMEM_LIMIT
        ),
        name="forward",
    )(conditions, biases, buckets, ada, *shards, latents, cotangent)
    return results[0], results[1], results[2], dict(zip(kept, results[3:]))


class Scatter:
    SEMAPHORES = ((), (), (2,), (2,), (4,), (4,), (4,), (4,), (4,), (4,), (3,), (3,))
    LEADING = ((2, 2, 4), (2,), (4,), (4,), (4,), (3,))

    def __init__(self, here, part, store, buffers, semaphores):
        self.here, self.part, self.store = here, part, store
        self.point = Steps({k: call for k, call in enumerate(self.stages())}, SCATTER_STEPS)
        self.r0, self.rp, self.rd, self.rx, self.ry, self.r3 = buffers
        self.cs, self.cr, self.ps, self.pr, self.ds, self.dr = semaphores[:6]
        self.xs, self.xr, self.ys, self.yr, self.zs, self.zr = semaphores[6:]
        y, x, c, z = here
        self.sib = device_at(y, x, 1 - c, z)
        self.xn = device_at(y, 1 - x, c, z)
        self.yn = device_at(1 - y, x, c, z)
        self.partner = z + 1 - 2 * (z % 2)
        self.opposite = (z + 2) % 4
        self.zp = device_at(y, x, c, self.partner)
        self.copies = [[] for _ in part]

    def stages(self):
        return self.chip, self.pair, self.diagonal, self.sides, self.last

    def by_y(self, i):
        return ((0,), (2,)) if SUMMED_IN_PAIRS[i] else ((0, 2), (1, 3))

    def hop(self, i, kind, k):
        y, x, c, z = self.here
        part = self.part[i]
        if kind == "c":
            return part.at[:, :, 1 - c], self.r0[i], self.cs.at[i], self.cr.at[i], self.sib
        if kind == "p":
            block = (self.partner + 2 * k) % 4
            return part.at[1 - y, 1 - x, c, block], self.rp[i].at[k], self.ps.at[i, k], self.pr.at[i, k], self.zp
        if kind == "d":
            block = (z + k) % 4
            there = self.yn if k in self.by_y(i)[0] else self.xn
            return part.at[1 - y, 1 - x, c, block], self.rd[i].at[k], self.ds.at[i, k], self.dr.at[i, k], there
        if kind == "x":
            block = (z + k) % 4
            return part.at[y, 1 - x, c, block], self.rx[i].at[block], self.xs.at[i, k], self.xr.at[i, k], self.xn
        if kind == "y":
            block = (z + k) % 4
            return part.at[1 - y, x, c, block], self.ry[i].at[block], self.ys.at[i, k], self.yr.at[i, k], self.yn
        there = (z + k + 1) % 4
        return part.at[y, x, c, there], self.r3[i].at[k], self.zs.at[i, k], self.zr.at[i, k], device_at(y, x, c, there)

    def send(self, i, kind, *which):
        for k in which:
            remote(*self.hop(i, kind, k)).start()
            self.copies[i].append((kind, k))

    def wait(self, i, kind, *which):
        for k in which:
            remote(*self.hop(i, kind, k)).wait_recv()

    def drain(self, i):
        for kind, k in self.copies[i]:
            remote(*self.hop(i, kind, k)).wait_send()
        self.copies[i] = []

    def start(self, i):
        self.send(i, "c", 0)

    def chip(self, i):
        c = self.here[2]
        part, r0 = self.part[i], self.r0[i]
        self.wait(i, "c", 0)

        def add(k, _):
            a, b, q = k // 8, (k // 4) % 2, k % 4
            part[a, b, c, q] = part[a, b, c, q] + r0[a, b, q]
            return 0

        lax.fori_loop(0, 16, add, 0)
        first, second = self.by_y(i)
        if SUMMED_IN_PAIRS[i]:
            self.send(i, "p", 0, 1)
        else:
            self.send(i, "d", *first, *second)
        self.send(i, "x", *[k for k in (1, 3, 0, 2) if k not in first])
        self.send(i, "y", *[k for k in (0, 2, 1, 3) if k not in second])

    def pair(self, i):
        if not SUMMED_IN_PAIRS[i]:
            return
        y, x, c, z = self.here
        part = self.part[i]
        for k, block in enumerate((z, self.opposite)):
            self.wait(i, "p", k)
            part[1 - y, 1 - x, c, block] = part[1 - y, 1 - x, c, block] + self.rp[i][k]
            self.send(i, "d", 2 * k)

    def diagonal(self, i):
        y, x, c, z = self.here
        part = self.part[i]
        first, second = self.by_y(i)
        for k in first:
            self.wait(i, "d", k)
            block = (z + k) % 4
            part[y, 1 - x, c, block] = part[y, 1 - x, c, block] + self.rd[i][k]
            self.send(i, "x", k)
        for k in second:
            self.wait(i, "d", k)
            block = (z + k) % 4
            part[1 - y, x, c, block] = part[1 - y, x, c, block] + self.rd[i][k]
            self.send(i, "y", k)

    def sides(self, i):
        y, x, c, z = self.here
        part, rx, ry = self.part[i], self.rx[i], self.ry[i]
        self.wait(i, "x", 1, 2, 3, 0)
        self.wait(i, "y", 1, 3, 0, 2)

        def add(q, _):
            both = rx[q].astype(F32) + ry[q].astype(F32)
            part[y, x, c, q] = (part[y, x, c, q].astype(F32) + both).astype(BF16)
            return 0

        lax.fori_loop(0, 4, add, 0)
        self.send(i, "z", 1, 0, 2)

    def last(self, i):
        y, x, c, z = self.here
        self.wait(i, "z", 0, 1, 2)
        part, r3 = self.part[i], self.r3[i]
        total = (part[y, x, c, z].astype(F32) + r3[0].astype(F32)) + (r3[1].astype(F32) + r3[2].astype(F32))
        out, start, stride = self.store[i]
        flatten_into(out, total, start, stride)

    def rest(self):
        while self.point.table:
            self.point()


def flatten_into(out, value, start, stride):
    rows, size = value.shape
    for k in range(size // 128):
        out[pl.ds(start + k, rows, stride=stride), :] = value[:, k * 128 : (k + 1) * 128]


GRADS = ("down", "up", "pt", "qt", "ps", "qs")
WIDTHS = {"down": D, "up": FF, "pt": D, "qt": 3 * D, "ps": D, "qs": 3 * D}
ENTRIES = [("down", k * D // 2, D // 2) for k in range(2)] + [("up", k * FF // 2, FF // 2) for k in range(2)]
ENTRIES += [("pt", 0, D)] + [("qt", k * D, D) for k in range(3)] + [("ps", 0, D)] + [("qs", k * D, D) for k in range(3)]
DOWN, UP, PT, QT, PS, QS = 0, 2, 4, 5, 8, 9
SUMMED_IN_PAIRS = (False, False, False, True, True, True, True, False, False, False, False, False)
SCATTER_STEPS = (
    (), (), (), ((0, 0), (1, 0),), (), ((0, 1), (1, 1),), ((2, 0),), (), ((0, 2), (1, 2),), (), ((2, 1),), (),
    ((0, 3), (3, 0),), (), ((0, 4), (1, 3), (2, 2),), (), ((3, 1), (4, 0),), ((1, 4),), (), (), (), ((0, 5),), (),
    ((0, 6), (2, 3), (4, 1), (0, 7), (1, 5), (1, 7),), ((1, 6), (2, 4), (3, 2),), (), ((0, 8), (3, 3), (1, 8),),
    ((2, 7),), ((2, 6), (2, 5), (3, 4), (4, 2),), ((2, 8),), (), ((3, 7), (3, 6), (4, 3), (3, 5), (0, 9), (1, 9),),
    ((3, 8), (4, 4), (0, 10), (1, 10),), ((2, 9),), ((0, 11), (4, 7), (1, 11),), (), ((2, 10), (4, 6),), (),
    ((3, 9), (4, 5), (2, 11),), (), ((3, 10), (4, 8),), ((3, 11), (4, 9),), (), (), (), (), ((4, 10),), (), (), (),
    (), ((4, 11),),
)
BLOCKS = [("down", j) for j in range(4)] + [("up", j) for j in range(4)]
BLOCKS += [("pt", 0)] + [("qt", j) for j in range(3)] + [("ps", 0)] + [("qs", j) for j in range(3)]
SLOTS = 4


def attend_back(s, q, p, c_grad, first):
    def body(t, _):
        step = first + t
        item, pair = step // PAIRS, step % PAIRS
        rows = pl.ds(pl.multiple_of(item * TOKENS, TOKENS), TOKENS)
        at = [lane_cols(pair * 128 + j * D) for j in range(3)]
        soft = p[:, lane_cols(step * TOKENS, TOKENS)]
        dc = c_grad[rows, at[0]]
        queries, keys, values = (q[rows, where] for where in at)
        v_grad = pick_heads(t_dot(soft[:TOKENS], dc), t_dot(soft[TOKENS:], dc))
        soft_grad = dot_t(two_heads(dc, 1.0), values)
        wide = soft.astype(F32)
        product = soft_grad * wide
        score = (product - wide * jnp.sum(product, axis=-1, keepdims=True)).astype(BF16)
        q_both = dot(score, keys)
        q_grad = pick_heads(q_both[:TOKENS], q_both[TOKENS:]) * HD ** (-0.5)
        k_grad = pick_heads(t_dot(score[:TOKENS], queries), t_dot(score[TOKENS:], queries)) * HD ** (-0.5)
        q[rows, at[0]] = q_grad.astype(BF16)
        q[rows, at[1]] = k_grad.astype(BF16)
        q[rows, at[2]] = v_grad.astype(BF16)
        return 0

    lax.fori_loop(0, PAIRS // 2, body, 0)


def backward_kernel(names, *refs):
    s = Names(names, refs)
    here = place()
    y, x, c, z = here
    me = ((y * 2 + x) * 2 + c) * 4 + z
    loads = {}

    def fetch(name, src, dst, k):
        loads[name] = pltpu.make_async_copy(src, dst, s.load_sem.at[k])
        loads[name].start()

    def have(*wanted):
        for name in wanted:
            loads.pop(name).wait()

    def fetch_block(k):
        tensor, j = BLOCKS[k]
        src = getattr(s, "w_" + tensor)
        src = src.at[j] if tensor == "down" else src.at[:, :, pl.ds(j * D, D)]
        pltpu.make_async_copy(src, s.blocks.at[k % SLOTS], s.load_sem.at[16 + k % SLOTS]).start()

    def block(k):
        slot = k % SLOTS
        pltpu.make_async_copy(s.w_ps, s.blocks.at[slot], s.load_sem.at[16 + slot]).wait()
        return s.blocks[slot].reshape(D, D)

    def used(k):
        if k + SLOTS < len(BLOCKS):
            fetch_block(k + SLOTS)

    def used_at(first, j, count):
        for k in range(count):
            if first + k + SLOTS < len(BLOCKS):
                @pl.when(j == k)
                def _(k=k):
                    fetch_block(first + k + SLOTS)

    fetch("g", s.in_g, s.g, 0)
    fetch("mods", s.in_mods, s.mods, 1)
    fetch_block(0)
    fetch_block(1)
    fetch("gp", s.in_gp, s.gp, 2)
    fetch("h3", s.in_h3, s.h3, 3)
    fetch_block(2)
    fetch_block(3)
    fetch("n3", s.in_n3, s.n3, 4)
    fetch("r3", s.in_r3, s.r3, 5)

    def fetch_rest(k):
        for i, (name, dst) in enumerate((("a", s.a), ("c", s.c), ("h", s.h), ("n", s.n), ("r", s.r))):
            fetch(name, getattr(s, f"in_{name}{k}"), dst, 6 + i)

    fetch_rest(2)

    homes = {"down": (s.b0, 0), "up": (s.b1, 0), "pt": (s.b2, 0), "qt": (s.b2, D), "ps": (s.b3, 0), "qs": (s.b3, D)}
    parts, store = [], []
    for t, start, width in ENTRIES:
        ref, base = homes[t]
        parts.append(ref.at[:, :, :, :, :, pl.ds(base + start, width)])
        store.append((getattr(s, "grad_" + t), start // 128, WIDTHS[t] // 128))
    buffers = [[getattr(s, f"r{k}_{i}") for i in range(len(ENTRIES))] for k in range(6)]
    scatter = Scatter(here, parts, store, buffers, [getattr(s, f"ss{k}") for k in range(12)])
    sender = Sender()
    little = Gather(here, sender, [s.small], [s.small_all], [getattr(s, f"ls{i}") for i in range(8)], s.ls8)

    barrier = pltpu.get_barrier_semaphore()
    partners = [device_at(y, x, 1 - c, z), device_at(y, 1 - x, c, z), device_at(1 - y, x, c, z)]
    partners += [device_at(y, x, c, (z + step) % 4) for step in (1, 2, 3)]
    for partner in partners:
        pl.semaphore_signal(barrier, inc=1, device_id=partner, device_id_type=MESH)
    pl.semaphore_wait(barrier, 6)

    s.rows[...] = jnp.zeros_like(s.rows)
    valid_rows(s)
    ones = jnp.ones((8, 2 * TOKENS), BF16)
    have("mods")
    for item in range(2):
        gate = s.mods[8, item : item + 1, :]

        def first(t, _):
            rows = rows_of(item, t, CHUNK)
            d3 = s.cotangent[rows, :].astype(F32) * s.valid[rows, :]
            s.d[rows, :] = d3
            s.dm[rows, :] = (gate * d3).astype(BF16)
            return 0

        lax.fori_loop(0, TOKENS // CHUNK, first, 0)
        s.rows[9 * item + 8 : 9 * item + 9, :] = s.dga3[item : item + 1, :]
    s.rows[22:23, :] = dot(ones, s.dm[...])[:1]

    have("g")

    def starts(first, indices):
        return {at: lambda i=first + n: scatter.start(i) for n, at in enumerate(indices)}

    def down(t):
        k, j = t // 2, t % 2
        cols = lane_cols(k * (D // 2), D // 2)
        grad = t_dot(s.g[:, lane_cols(2 * j * D, 2 * D)], s.dm[:, cols]).astype(BF16)
        s.b0[j, :, :, :, :, cols] = grad.reshape(2, 2, 4, 4 * D // DEVICES, D // 2)

    scatter.point.rolled(4, (down, starts(DOWN, (1, 3)), 2))
    fetch("p", s.in_p2, s.g, 0)

    have("gp", "h3")

    def up_back(j):
        cols = lane_cols(j * D, D)
        s.acc[...] = dot_t(s.dm[...], block(j))
        used_at(0, j, 4)

        def slope(t, _):
            rows = rows_of(0, t, CHUNK)
            s.gp[rows, cols] = (s.acc[rows, :] * s.gp[rows, cols].astype(F32)).astype(BF16)
            return 0

        lax.fori_loop(0, 2 * TOKENS // CHUNK, slope, 0)
        s.rows[pl.ds(18 + j, 1), :] = dot(ones, s.gp[:, cols])[:1]

    def up_grad(j):
        cols = lane_cols(j * D, D)
        grad = t_dot(s.h3[...], s.gp[:, cols]).astype(BF16)
        s.b1[:, :, :, :, :, cols] = grad.reshape(2, 2, 2, 4, D // DEVICES, D)

    scatter.point.rolled(4, (up_back, {}, 1), (up_grad, starts(UP, (1, 3)), 1))

    def back_through(first_block, source, count, every):
        s.acc[...] = jnp.zeros_like(s.acc)

        def body(j):
            s.acc[...] = s.acc[...] + dot_t(source[:, lane_cols(j * D, D)], block(first_block + j))
            used_at(first_block, j, count)

        scatter.point.rolled(count, (body, {}, every))

    def qkv_grad(out, j):
        grad = t_dot(s.h[...], s.gp[:, lane_cols(j * D, D)]).astype(BF16)
        out[:, :, :, :, :, lane_cols(D + j * D, D)] = grad.reshape(2, 2, 2, 4, D // DEVICES, D)

    back_through(4, s.gp, 4, 2)
    fetch("q", s.in_q2, s.gp.at[:, pl.ds(0, 3 * D)], 2)

    def norm_back(n_ref, r_ref, base, a_ref, gate_row, between=False):
        for item in range(2):
            scale = 1.0 + s.mods[base + 1, item : item + 1, :]
            gate = None if gate_row is None else s.mods[gate_row, item : item + 1, :]

            def body(t, totals):
                rows = rows_of(item, t, CHUNK)
                dh, n = s.acc[rows, :], n_ref[rows, :].astype(F32)
                g = dh * scale
                dhn = dh * n
                mean_g = jnp.mean(g, axis=-1, keepdims=True)
                mean_gn = jnp.mean(g * n, axis=-1, keepdims=True)
                d = s.d[rows, :] + r_ref[rows, :] * (g - mean_g - n * mean_gn)
                s.d[rows, :] = d
                fold = lambda v: jnp.sum(v.reshape(CHUNK // 8, 8, D), axis=0)
                new = [totals[0] + fold(dh), totals[1] + fold(dhn)]
                if gate is not None:
                    s.dm[rows, :] = (gate * d).astype(BF16)
                    new.append(totals[2] + fold(d * a_ref[rows, :].astype(F32)))
                return tuple(new)

            count = 2 if gate is None else 3
            totals = lax.fori_loop(0, TOKENS // CHUNK, body, (jnp.zeros((8, D), F32),) * count)
            for where, total in zip((base, base + 1, base - 1), totals):
                row = 9 * item + where
                s.rows[row : row + 1, :] = jnp.sum(total, axis=0, keepdims=True)
            if between or item:
                scatter.point()

    have("n3", "r3", "a")
    norm_back(s.n3, s.r3, 6, s.a, 5)
    have("c")
    s.b2[:, :, :, :, :, :D] = t_dot(s.c[...], s.dm[...]).astype(BF16).reshape(2, 2, 2, 4, D // DEVICES, D)
    scatter.start(PT)
    s.dc[...] = dot_t(s.dm[...], block(8)).astype(BF16)
    used(8)
    scatter.point()
    have("q", "p")
    scatter.point.rolled(4, (lambda k: attend_back(s, s.gp, s.g, s.dc, 3 * k), {}, 1))
    fetch("p", s.in_p1, s.g, 0)
    have("h")
    scatter.point.rolled(3, (lambda j: qkv_grad(s.b2, j), starts(QT, (0, 1, 2)), 1))
    back_through(9, s.gp, 3, 1)
    fetch("q", s.in_q1, s.gp.at[:, pl.ds(0, 3 * D)], 2)
    have("n", "r")
    fetch("c", s.in_c1, s.c, 7)
    fetch("h", s.in_h1, s.h, 8)
    fetch("a", s.in_a1, s.a, 6)
    have("a")
    norm_back(s.n, s.r, 3, s.a, 2)
    fetch("n", s.in_n1, s.n, 9)
    fetch("r", s.in_r1, s.r, 10)
    have("c")
    s.b3[:, :, :, :, :, :D] = t_dot(s.c[...], s.dm[...]).astype(BF16).reshape(2, 2, 2, 4, D // DEVICES, D)
    scatter.start(PS)
    s.dc[...] = dot_t(s.dm[...], block(12)).astype(BF16)
    used(12)
    scatter.point()
    have("q", "p")
    scatter.point.rolled(4, (lambda k: attend_back(s, s.gp, s.g, s.dc, 3 * k), {}, 1))
    have("h")
    scatter.point.rolled(3, (lambda j: qkv_grad(s.b3, j), starts(QS, (0, 1, 2)), 1))
    back_through(13, s.gp, 3, 1)
    have("n", "r")
    norm_back(s.n, s.r, 0, None, None, True)
    s.small[...] = s.rows[...].astype(BF16)
    little.start(0)
    scatter.point()
    little.stage1(0)
    scatter.point()
    little.stage2(0)
    scatter.point()
    little.stage3(0)
    scatter.point()
    little.finish(0)

    spot = lax.broadcasted_iota(jnp.int32, (D, 128), 0) % (D // DEVICES)

    def ada_grad(j):
        chosen = jnp.where((spot == j) | (spot == j + 9), s.chosen[...], jnp.zeros((D, 128), BF16))
        grad = t_dot(chosen, s.small_all[...].reshape(D, D))[: D // DEVICES]
        flatten_into(s.grad_ada, grad, j * (D // 128), 9 * D // 128)

    scatter.point.rolled(9, (ada_grad, {}, 1))
    gathered = s.small_all[...].reshape(D, D)
    row = lax.broadcasted_iota(jnp.int32, (16, D), 0)
    slot = lax.broadcasted_iota(jnp.int32, (16, D), 1) % (D // DEVICES)
    take = ((row < 9) & ((slot == row) | (slot == row + 9))) | ((row >= 9) & (slot == row + 9))
    s.grad_bias[...] = dot(take.astype(F32).astype(BF16), gathered)
    scatter.rest()
    for i in range(len(ENTRIES)):
        scatter.drain(i)
    sender.drain()


def run_backward(cotangent, buckets, dga3, chosen, kept):
    vmem, any_space = pl.BlockSpec(memory_space=pltpu.VMEM), pl.BlockSpec(memory_space=pl.ANY)
    rows, part = 2 * TOKENS, D // DEVICES
    ins = {"cotangent": cotangent, "buckets": buckets, "dga3": dga3, "chosen": chosen}
    fetched = {"in_" + name: kept[name] for name in save_shapes(TOKENS)}
    for t in GRADS:
        shape = (4, DEVICES, part, D) if t == "down" else (DEVICES, part, WIDTHS[t])
        fetched["w_" + t] = kept["w_" + t].reshape(shape)
    ins |= fetched
    block_of = [(4 * part if t == "down" else part, width) for t, _, width in ENTRIES]
    outs = {"grad_" + t: (DEVICES * part * WIDTHS[t] * (4 if t == "down" else 1) // DEVICES // 128, 128) for t in GRADS}
    outs |= {"grad_ada": (part * 9 * D // 128, 128), "grad_bias": (16, D), "d": (rows, D)}
    dma = pltpu.SemaphoreType.DMA
    big = lambda *block: pltpu.VMEM((2, 2, 2, 4) + block, BF16)
    scratch = {
        "b0": big(4 * part, D), "b1": big(part, FF), "b2": big(part, FF), "b3": big(part, FF),
        "blocks": pltpu.VMEM((SLOTS, DEVICES, part, D), BF16),
        "g": pltpu.VMEM((rows, FF), BF16), "gp": pltpu.VMEM((rows, FF), BF16),
        "acc": pltpu.VMEM((rows, D), F32),
        "mods": pltpu.VMEM((9, 8, D), F32), "rows": pltpu.VMEM((24, D), F32),
        "small": pltpu.VMEM((24, D), BF16), "small_all": big(24, D),
        "r3": pltpu.VMEM((rows, 1), F32), "r": pltpu.VMEM((rows, 1), F32), "valid": pltpu.VMEM((rows, 1), F32),
        "load_sem": dma((16 + SLOTS,)),
    }
    scratch |= {name: pltpu.VMEM((rows, D), BF16) for name in ("dm", "dc", "h3", "n3", "a", "c", "h", "n")}
    for k, lead in enumerate(Scatter.LEADING):
        scratch |= {f"r{k}_{i}": pltpu.VMEM(lead + block, BF16) for i, block in enumerate(block_of)}
    scratch |= {f"ss{k}": dma((len(ENTRIES),) + extra) for k, extra in enumerate(Scatter.SEMAPHORES)}
    scratch |= {f"ls{i}": kind for i, kind in enumerate(Gather.scratch(1))}
    names = list(ins) + list(outs) + list(scratch)
    results = pl.pallas_call(
        lambda *refs: backward_kernel(names, *refs),
        out_shape=tuple(jax.ShapeDtypeStruct(shape, F32) for shape in outs.values()),
        in_specs=[vmem] * 4 + [any_space] * len(fetched),
        out_specs=(vmem,) * len(outs),
        scratch_shapes=list(scratch.values()),
        compiler_params=pltpu.CompilerParams(
            collective_id=2, has_side_effects=True, vmem_limit_bytes=VMEM_LIMIT
        ),
        name="backward",
    )(*ins.values())
    return dict(zip(outs, results))


def deliver_kernel(count, *refs):
    src, out, buf = refs[:count], refs[count : 2 * count], refs[2 * count : 3 * count]
    coming, going = refs[3 * count :]
    copies = []
    for i in sorted(range(count), key=lambda i: -math.prod(src[i].shape)):
        rows = src[i].shape[0]
        step = rows // 2 if rows >= 512 else rows
        for start in range(0, rows, step):
            at = pl.ds(start, min(step, rows - start))
            k = len(copies)
            copies.append((
                pltpu.make_async_copy(src[i].at[at], buf[i].at[at], coming.at[k]),
                pltpu.make_async_copy(buf[i].at[at], out[i].at[at], going.at[k]),
            ))
    for first, _ in copies:
        first.start()
    for first, second in copies:
        first.wait()
        second.start()
    for _, second in copies:
        second.wait()


def deliver(results):
    count = len(results)
    any_space = pl.BlockSpec(memory_space=pl.ANY)
    dma = pltpu.SemaphoreType.DMA((2 * count + 2,))
    return pl.pallas_call(
        lambda *refs: deliver_kernel(count, *refs),
        out_shape=tuple(jax.ShapeDtypeStruct(r.shape, r.dtype) for r in results),
        in_specs=[any_space] * count,
        out_specs=(any_space,) * count,
        scratch_shapes=[pltpu.VMEM(r.shape, r.dtype) for r in results] + [dma, dma],
        compiler_params=pltpu.CompilerParams(vmem_limit_bytes=VMEM_LIMIT),
        name="deliver",
    )(*results)


def norm_parts(rows):
    centre = rows - jnp.mean(rows, axis=-1, keepdims=True)
    inverse = lax.rsqrt(jnp.mean(centre * centre, axis=-1, keepdims=True) + EPS)
    return centre * inverse, inverse


def norm_back(grad, normed, inverse, scale):
    shift_grad = jnp.sum(grad, axis=1)
    scale_grad = jnp.sum(grad * normed, axis=1)
    pulled = grad * (1.0 + scale)
    back = inverse * (
        pulled
        - jnp.mean(pulled, axis=-1, keepdims=True)
        - normed * jnp.mean(pulled * normed, axis=-1, keepdims=True)
    )
    return back, shift_grad, scale_grad


def heads(x):
    return x.reshape(x.shape[0], x.shape[1], HEADS, HD)


def attention(low, qkv_w, proj_w, mask):
    packed = dot(low, qkv_w).astype(BF16)
    q, k, v = (heads(part) for part in jnp.split(packed, 3, axis=-1))
    scores = jnp.einsum("bqhd,bkhd->bhqk", q, k, preferred_element_type=F32) * HD ** (-0.5)
    scores = jnp.where(mask, scores, MASKED)
    soft = jax.nn.softmax(scores, axis=-1)
    context = jnp.einsum("bhqk,bkhd->bqhd", soft.astype(BF16), v, preferred_element_type=F32)
    context = context.astype(BF16).reshape(low.shape)
    return dot(context, proj_w), (q, k, v, soft, context)


def attention_back(grad_low, low, qkv_w, proj_w, kept):
    q, k, v, soft, context = kept
    proj_grad = jnp.einsum("bld,ble->de", context, grad_low, preferred_element_type=F32)
    ctx = heads(jnp.einsum("ble,de->bld", grad_low, proj_w, preferred_element_type=F32).astype(BF16))
    v_grad = jnp.einsum("bhqk,bqhd->bkhd", soft.astype(BF16), ctx, preferred_element_type=F32)
    soft_grad = jnp.einsum("bqhd,bkhd->bhqk", ctx, v, preferred_element_type=F32)
    row_dot = jnp.sum(soft_grad * soft, axis=-1, keepdims=True)
    score_grad = (soft * (soft_grad - row_dot)).astype(BF16)
    q_grad = jnp.einsum("bhqk,bkhd->bqhd", score_grad, k, preferred_element_type=F32) * HD ** (-0.5)
    k_grad = jnp.einsum("bhqk,bqhd->bkhd", score_grad, q, preferred_element_type=F32) * HD ** (-0.5)
    packed = jnp.concatenate(
        [part.astype(BF16).reshape(low.shape) for part in (q_grad, k_grad, v_grad)], axis=-1
    )
    qkv_grad = jnp.einsum("bld,ble->de", low, packed, preferred_element_type=F32)
    low_grad = jnp.einsum("ble,de->bld", packed, qkv_w, preferred_element_type=F32)
    return low_grad, qkv_grad, proj_grad


def gather_plain(shards):
    return tuple(lax.all_gather(s, AXES, axis=0) for s in shards)


def scatter_plain(parts, small):
    devices = lax.axis_size(AXES)
    sums = tuple(
        lax.psum_scatter(p.reshape((devices,) + p.shape[-2:]), AXES, scatter_dimension=0, tiled=True)[
            0
        ].astype(F32)
        for p in parts
    )
    return sums + (lax.all_gather(small, AXES, axis=0),)


def per_device_plain(latents, buckets, step_ids, qs, ps, qt, pt, up, down, ada, biases, cotangent):
    devices = lax.axis_size(AXES)
    micro = latents.shape[0]
    frames, spatial = latents.shape[2], latents.shape[3]
    tokens = frames * spatial
    rows = D // devices

    gather, scatter = gather_plain, scatter_plain

    ada_columns = lax.all_to_all(
        ada.reshape(rows, 9 * D), AXES, split_axis=1, concat_axis=0, tiled=True
    )
    own_bias = jnp.pad(biases, (0, D - biases.shape[0]))[None]
    small = jnp.concatenate([timestep_condition(step_ids[:, 0]), own_bias], axis=0)
    shards = [small] + [w.reshape(rows, -1) for w in (qs, ps, qt, pt, up)] + [down.reshape(-1, D)]
    small, *gathered = gather(shards)
    w_qs, w_ps, w_qt, w_pt, w_up = (w.reshape(D, -1) for w in gathered[:5])
    w_down = gathered[5].reshape(-1, D)
    small = small.reshape(devices, micro + 1, D)
    condition = small[:, :micro].reshape(devices * micro, D)
    bias = small[:, micro, : biases.shape[0]].reshape(-1).astype(F32)
    modulation = lax.all_to_all(
        dot(condition, ada_columns), AXES, split_axis=0, concat_axis=1, tiled=True
    )
    modulation = (modulation + bias[: 9 * D]).reshape(micro, 9, 1, D)
    b_up, b_down = bias[9 * D : 9 * D + FF], bias[9 * D + FF :]

    positions = jnp.arange(tokens)
    frame, place = positions // spatial, positions % spatial
    bucket = buckets[:, 0]
    length = jnp.where(bucket == 0, spatial, jnp.where(bucket == 1, spatial // 2, spatial // 8))
    valid = place[None, :] < length[:, None]
    space_mask = (frame[:, None] == frame[None, :])[None, None] & valid[:, None, None, :]
    time_mask = (place[:, None] == place[None, :])[None, None]
    valid_rows = valid.astype(F32)[:, :, None]

    sh1, sc1, ga1, sh2, sc2, ga2, sh3, sc3, ga3 = (modulation[:, i] for i in range(9))
    x = latents.reshape(micro, tokens, D).astype(F32)
    n1, r1 = norm_parts(x)
    h1 = (n1 * (1.0 + sc1) + sh1).astype(BF16)
    a1, kept1 = attention(h1, w_qs, w_ps, space_mask)
    x1 = x + ga1 * a1
    n2, r2 = norm_parts(x1)
    h2 = (n2 * (1.0 + sc2) + sh2).astype(BF16)
    a2, kept2 = attention(h2, w_qt, w_pt, time_mask)
    x2 = x1 + ga2 * a2
    n3, r3 = norm_parts(x2)
    h3 = (n3 * (1.0 + sc3) + sh3).astype(BF16)
    hidden = dot(h3, w_up) + b_up
    gelu, pull = jax.vjp(lambda u: jax.nn.gelu(u, approximate=True), hidden)
    g = gelu.astype(BF16)
    m = dot(g, w_down) + b_down
    x3 = x2 + ga3 * m
    output = (x3 * valid_rows).astype(BF16)

    d3 = cotangent.reshape(micro, tokens, D).astype(F32) * valid_rows
    dm = (ga3 * d3).astype(BF16)
    dga3 = jnp.sum(d3 * m, axis=1)
    db_down = jnp.sum(dm.astype(F32), axis=(0, 1))
    dw_down = jnp.einsum("bsk,bsd->kd", g, dm, preferred_element_type=F32)
    dg = jnp.einsum("bsd,kd->bsk", dm, w_down, preferred_element_type=F32)
    du = pull(dg)[0].astype(BF16)
    db_up = jnp.sum(du.astype(F32), axis=(0, 1))
    dw_up = jnp.einsum("bsd,bsk->dk", h3, du, preferred_element_type=F32)
    dh3 = jnp.einsum("bsk,dk->bsd", du, w_up, preferred_element_type=F32)
    dv, dsh3, dsc3 = norm_back(dh3, n3, r3, sc3)
    d2 = d3 + dv
    da2 = (ga2 * d2).astype(BF16)
    dga2 = jnp.sum(d2 * a2, axis=1)
    dh2, dw_qt, dw_pt = attention_back(da2, h2, w_qt, w_pt, kept2)
    dv, dsh2, dsc2 = norm_back(dh2, n2, r2, sc2)
    d1 = d2 + dv
    da1 = (ga1 * d1).astype(BF16)
    dga1 = jnp.sum(d1 * a1, axis=1)
    dh1, dw_qs, dw_ps = attention_back(da1, h1, w_qs, w_ps, kept1)
    dv, dsh1, dsc1 = norm_back(dh1, n1, r1, sc1)
    latents_grad = d1 + dv

    dmod = jnp.stack([dsh1, dsc1, dga1, dsh2, dsc2, dga2, dsh3, dsc3, dga3], axis=1)
    small = jnp.concatenate(
        [dmod.reshape(micro * 9, D), db_up.reshape(-1, D), db_down.reshape(-1, D)], axis=0
    ).astype(BF16)
    parts = [
        part.astype(BF16).reshape(tuple(gathered[i].shape))
        for i, part in ((5, dw_down), (4, dw_up), (3, dw_pt), (2, dw_qt), (1, dw_ps), (0, dw_qs))
    ]
    ddown, dup, dpt, dqt, dps, dqs, small = scatter(parts, small)
    flat = tuple(part.reshape(-1) for part in (dqs, dps, dqt, dpt, dup))
    small = small.reshape(devices, -1, D)
    dmod_all = small[:, : micro * 9].reshape(devices * micro, 9 * D)
    me = lax.axis_index(AXES)
    my_condition = lax.dynamic_slice_in_dim(condition, me * rows, rows, axis=1)
    dw_ada = lax.dot_general(
        my_condition, dmod_all, (((0,), (0,)), ((), ())), preferred_element_type=F32
    )
    db = jnp.concatenate(
        [
            jnp.sum(dmod_all.astype(F32), axis=0),
            jnp.sum(small[:, micro * 9 :].astype(F32), axis=0).reshape(-1),
        ]
    )
    db = lax.dynamic_slice_in_dim(db, me * biases.shape[0], biases.shape[0])

    shape = latents.shape
    return (
        output.reshape(shape),
        latents_grad.reshape(shape),
        *flat,
        ddown.reshape(-1),
        dw_ada.reshape(-1),
        db,
    )


def per_device(latents, buckets, step_ids, qs, ps, qt, pt, up, down, ada, biases, cotangent):
    rows = 2 * TOKENS
    conditions = timestep_condition(step_ids[:, 0])
    shards = [w.reshape(-1, 128) for w in (qs, ps, qt, pt, up, down)]
    tokens = latents.reshape(rows, D)
    grads_in = cotangent.reshape(rows, D)
    output, dga3, chosen, kept = run_forward(
        conditions, biases.reshape(1, -1), buckets, ada.reshape(-1, 128), shards, tokens, grads_in
    )
    grads = run_backward(grads_in, buckets, dga3, chosen, kept)
    me = lax.axis_index(AXES)
    bias_grad = grads["grad_bias"][:14].reshape(-1)
    names = ["d"] + ["grad_" + t for t in ("qs", "ps", "qt", "pt", "up", "down", "ada")]
    output, latents_grad, *flat = deliver([output] + [grads[name] for name in names])
    return (
        output.reshape(latents.shape),
        latents_grad.reshape(latents.shape),
        *(g.reshape(-1) for g in flat),
        lax.dynamic_slice_in_dim(bias_grad, me * SHARE, SHARE),
    )


def solution(mesh):
    items = P(None, AXES, None, None, None)
    flat = P(AXES)
    known = mesh.shape["wide"] == 8 and mesh.shape["narrow"] == 4
    return jax.shard_map(
        per_device if known else per_device_plain,
        mesh=mesh,
        in_specs=(items, P(None, AXES), P(None, AXES)) + (flat,) * 8 + (items,),
        out_specs=(items, items) + (flat,) * 8,
        check_vma=False,
    )
```
